32 devices in a mesh: head: 4 (over z), frame: 8 (over y, x, core).
Axes of the slice: x: 2, y: 2, z: 4, core: 2. Of those that a mesh axis runs over, the one named last changes fastest.
Arguments:
- queries: bfloat16 [4096, 2048], P(('frame', 'head')), may hold values from -6 to 6
- key_states: bfloat16 [4096, 2048], P(('frame', 'head')), may hold values from -6 to 6
- value_states: bfloat16 [4096, 2048], P(('frame', 'head')), may hold values from -6 to 6
- attn_out: bfloat16 [4096, 2048], P(('frame', 'head')), may hold values from -6 to 6
- grad_out: bfloat16 [4096, 2048], P(('frame', 'head')), may hold values from -192 to 192
- frame_order: int32 [8], replicated, may hold values from 0 to 7, each once
- block_live: int32 [8, 4, 4], replicated, may hold values from 0 to 1, as said below
Outputs:
- grad_queries: bfloat16 [4096, 2048], P('frame', 'head')
- grad_keys: bfloat16 [4096, 2048], P('frame', 'head')
- grad_values: bfloat16 [4096, 2048], P('frame', 'head')
The draws below stay inside these ranges and needn't reach their ends.
Inputs may be any that keep to these rules, and one draw needn't show every extreme that they name: `block_live`: every entry at distance 0 is 1; every entry at distances of 4 or more is 0.
All inputs are finite; a program needn't handle non-finite values.
Results may differ from the reference program's by a relative error of at most 0.0049.
Values may be sent and summed in bfloat16 or wider, within the bound.
No kernel may reach another device: no remote copies, remote signals or barrier semaphores. Data moves between devices by JAX's collectives and lax.ppermute only.
A program may use at most 128 MiB of HBM per device.

```python
import jax
import jax.numpy as jnp
from jax import lax

HEADS = 16
HEAD_DIM = 128
REACH = 4
FRAMES = 8
FRAME_TOK = 512
NBLK = 4
TOKENS = 4096


def draw_pair(key):
    width = HEADS * HEAD_DIM
    query_base = jnp.clip(jax.random.normal(jax.random.fold_in(key, 11), (TOKENS, width), jnp.float32), -6.0, 6.0)
    key_base = jnp.clip(jax.random.normal(jax.random.fold_in(key, 12), (TOKENS, width), jnp.float32), -6.0, 6.0)
    return (query_base, key_base)


def draw_queries(key, part):
    return draw_pair(key)[0].astype(jnp.bfloat16)


def draw_key_states(key, part):
    return draw_pair(key)[1].astype(jnp.bfloat16)


def draw_block_live(key, part):
    distance = jnp.arange(FRAMES, dtype=jnp.int32)
    shifts = jax.random.randint(jax.random.fold_in(key, 21), (FRAMES,), -1, 2).astype(jnp.int32)
    powers = jnp.left_shift(jnp.int32(1), jnp.arange(20, dtype=jnp.int32))
    levels = jnp.sum((distance[:, None] >= powers[None, :]).astype(jnp.int32), axis=1)
    band = jnp.maximum(jnp.right_shift(jnp.int32(NBLK), levels + 1), 1)
    band = jnp.where(distance < REACH, band, 0)
    rows = jnp.arange(NBLK, dtype=jnp.int32)
    offset = rows[None, :, None] - rows[None, None, :] - shifts[:, None, None]
    inside = jnp.abs(offset) < band[:, None, None]
    whole = (distance == 0)[:, None, None]
    return jnp.where(whole | inside, 1, 0).astype(jnp.int32)


def block_levels(key, extent, pieces, least, top_value):
    loudness, own = 1.0, jax.random.fold_in(key, 6)
    for position, blocks in pieces:
        draws = jnp.exp(jax.random.uniform(jax.random.fold_in(own, position), (blocks,), jnp.float32, least / len(pieces), top_value / len(pieces)))
        loudness = loudness * jnp.repeat(draws, extent[position] // blocks).reshape([-1 if axis == position else 1 for axis in range(len(extent))])
    return loudness


def centred(rng, extent, scale, bound, cuts=(), kind=jnp.bfloat16):
    drawn = scale * jax.random.normal(rng, extent, jnp.float32)
    if cuts:
        drawn = drawn * block_levels(rng, extent, cuts, -0.22, 0.18)
    return jnp.clip(drawn, -bound, bound).astype(kind)


def setup_inputs(seed: int = 0) -> dict:
    streams_of = jax.random.split(jax.random.key(seed), 8)
    queries = draw_queries(jax.random.fold_in(streams_of[7], 71), 0)
    key_states = draw_key_states(jax.random.fold_in(streams_of[7], 71), 0)
    value_states = centred(streams_of[2], (TOKENS, HEADS * HEAD_DIM), 1.0, 6.0, ((0, 32),))
    attn_out = centred(streams_of[3], (TOKENS, HEADS * HEAD_DIM), 1.0, 6.0, ((0, 32),))
    grad_out = centred(streams_of[4], (TOKENS, HEADS * HEAD_DIM), 32.0, 192.0, ((0, 32),))
    frame_order = jax.random.permutation(streams_of[5], FRAMES).astype(jnp.int32)
    block_live = draw_block_live(jax.random.fold_in(streams_of[7], 71), 0)
    return {"queries": queries, "key_states": key_states, "value_states": value_states, "attn_out": attn_out, "grad_out": grad_out, "frame_order": frame_order, "block_live": block_live}


def block_mask(block_live, frame_order, slot_query, slot_key):
    distance = jnp.abs(frame_order[slot_query] - frame_order[slot_key]).astype(jnp.int32)
    blocks = lax.dynamic_index_in_dim(block_live, distance, 0, keepdims=False)
    count = blocks.shape[0]
    width = FRAME_TOK // count
    spread = jnp.broadcast_to(blocks[:, None, :, None], (count, width, count, width))
    return jnp.any(blocks > 0), spread.reshape(FRAME_TOK, FRAME_TOK) > 0


def reference(queries, key_states, value_states, attn_out, grad_out, frame_order, block_live):
    scale = HEAD_DIM ** -0.5
    shape3 = (TOKENS, HEADS, HEAD_DIM)
    query_all = queries.reshape(shape3).astype(jnp.float32)
    key_all = key_states.reshape(shape3).astype(jnp.float32)
    value_all = value_states.reshape(shape3).astype(jnp.float32)
    grad_all = grad_out.reshape(shape3).astype(jnp.float32)
    delta_all = jnp.sum(grad_all * attn_out.reshape(shape3).astype(jnp.float32), axis=2)
    slots = jnp.arange(FRAMES, dtype=jnp.int32)

    def rows_of(array, slot):
        return lax.dynamic_slice_in_dim(array, (slot * FRAME_TOK).astype(jnp.int32), FRAME_TOK, 0)

    def totals_for(slot_query):
        query_blk = rows_of(query_all, slot_query)

        def over_keys(state, slot_key):
            live, mask = block_mask(block_live, frame_order, slot_query, slot_key)

            def update(current):
                peak, total = current
                scores = scale * jnp.einsum("qhd,khd->hqk", query_blk, rows_of(key_all, slot_key))
                new_peak = jnp.maximum(peak, jnp.max(jnp.where(mask, scores, -1e30), axis=2))
                fresh = jnp.sum(jnp.where(mask, jnp.exp(scores - new_peak[:, :, None]), 0.0), axis=2)
                return (new_peak, total * jnp.exp(peak - new_peak) + fresh)

            return lax.cond(live, update, lambda current: current, state), None

        start = (jnp.full((HEADS, FRAME_TOK), -1e30, jnp.float32), jnp.zeros((HEADS, FRAME_TOK), jnp.float32))
        peak, total = lax.scan(over_keys, start, slots)[0]
        return peak + jnp.log(total)

    log_all = lax.map(totals_for, slots)

    def frame_step(carry, slot_query):
        query_blk = rows_of(query_all, slot_query)
        grad_blk = rows_of(grad_all, slot_query)
        delta_blk = rows_of(delta_all, slot_query).T
        log_blk = lax.dynamic_index_in_dim(log_all, slot_query, 0, keepdims=False)

        def over_keys(state, slot_key):
            live, mask = block_mask(block_live, frame_order, slot_query, slot_key)

            def update(current):
                grad_query, grad_key_acc, grad_value_acc = current
                key_blk = rows_of(key_all, slot_key)
                value_blk = rows_of(value_all, slot_key)
                scores = scale * jnp.einsum("qhd,khd->hqk", query_blk, key_blk)
                probs = jnp.where(mask, jnp.exp(scores - log_blk[:, :, None]), 0.0)
                probs_low = probs.astype(jnp.bfloat16).astype(jnp.float32)
                grad_probs = jnp.einsum("qhd,khd->hqk", grad_blk, value_blk)
                grad_scores = (probs * (grad_probs - delta_blk[:, :, None])).astype(jnp.bfloat16).astype(jnp.float32)
                grad_query = grad_query + scale * jnp.einsum("hqk,khd->qhd", grad_scores, key_blk)
                begin = (slot_key * FRAME_TOK).astype(jnp.int32)
                key_term = scale * jnp.einsum("hqk,qhd->khd", grad_scores, query_blk)
                value_term = jnp.einsum("hqk,qhd->khd", probs_low, grad_blk)
                old_key = lax.dynamic_slice_in_dim(grad_key_acc, begin, FRAME_TOK, 0)
                old_value = lax.dynamic_slice_in_dim(grad_value_acc, begin, FRAME_TOK, 0)
                grad_key_acc = lax.dynamic_update_slice_in_dim(grad_key_acc, old_key + key_term, begin, 0)
                grad_value_acc = lax.dynamic_update_slice_in_dim(grad_value_acc, old_value + value_term, begin, 0)
                return (grad_query, grad_key_acc, grad_value_acc)

            return lax.cond(live, update, lambda current: current, state), None

        start = (jnp.zeros((FRAME_TOK, HEADS, HEAD_DIM), jnp.float32), carry[0], carry[1])
        grad_query, grad_key_acc, grad_value_acc = lax.scan(over_keys, start, slots)[0]
        return (grad_key_acc, grad_value_acc), grad_query

    start = (jnp.zeros(shape3, jnp.float32), jnp.zeros(shape3, jnp.float32))
    (grad_key_acc, grad_value_acc), grad_frames = lax.scan(frame_step, start, slots)
    width = HEADS * HEAD_DIM
    grad_queries = grad_frames.reshape(TOKENS, width).astype(jnp.bfloat16)
    grad_keys = grad_key_acc.reshape(TOKENS, width).astype(jnp.bfloat16)
    grad_values = grad_value_acc.reshape(TOKENS, width).astype(jnp.bfloat16)
    return (grad_queries, grad_keys, grad_values)
```

```python
import functools

import jax
import jax.numpy as jnp
from jax import lax
from jax.experimental import pallas as pl
from jax.experimental.pallas import tpu as pltpu
from jax.sharding import PartitionSpec as P

HEADS = 16
HEAD_DIM = 128
NEG = -1e30
GROUP = 4
EXTRA = 8


VMEM = pl.BlockSpec(memory_space=pltpu.VMEM)
SMEM = pl.BlockSpec(memory_space=pltpu.SMEM)
F32 = jnp.float32
BF16 = jnp.bfloat16
NT = (((1,), (1,)), ((), ()))
TN = (((0,), (0,)), ((), ()))
NN = (((1,), (0,)), ((), ()))


def dot(a, b, dims):
    return lax.dot_general(a, b, dims, preferred_element_type=F32)


def sds(shape, dtype):
    return jax.ShapeDtypeStruct(shape, dtype)


def cost(flops, nbytes):
    return pl.CostEstimate(flops=int(flops), bytes_accessed=int(nbytes), transcendentals=0)


class Plan:
    def __init__(self, rows):
        self.nz = lax.axis_size("head")
        self.nf = lax.axis_size("frame")
        self.hh = HEADS // self.nz
        self.na = min(self.hh, self.nf)
        self.nb = self.nf // self.na
        self.rows = rows
        self.own = self.na * self.nz
        self.total = self.own * self.nb
        assert self.hh == self.na and rows == HEAD_DIM


def over_head(value, step):
    count = lax.axis_size("head")
    return lax.ppermute(value, "head", [(i, i ^ step) for i in range(count)])


def over_frame(value, step):
    count = lax.axis_size("frame")
    return lax.ppermute(value, "frame", [(i, i ^ step) for i in range(count)])


def prep_kernel(plan, head_first, ids, x_ref, *outs):
    hd = HEAD_DIM
    z, a = ids[0], ids[1]
    for p, out in enumerate(outs):
        for c in range(out.shape[0]):
            r, s = (p, c) if head_first else (c, p)
            head = (z ^ r) * plan.hh + (a ^ s)
            out[c] = x_ref[:, pl.ds(pl.multiple_of(head * hd, hd), hd)]


def prep(plan, ids, x, head_first):
    pieces, chunk = (plan.nz, plan.na) if head_first else (plan.na, plan.nz)
    return pl.pallas_call(
        functools.partial(prep_kernel, plan, head_first),
        out_shape=[sds((chunk, plan.rows, HEAD_DIM), BF16)] * pieces,
        in_specs=[SMEM, VMEM],
        out_specs=[VMEM] * pieces,
        cost_estimate=cost(0, 4 * x.size),
        name="prep",
    )(ids, x)


def prep_grad_kernel(plan, ids, g_ref, o_ref, *outs):
    hd, rows = HEAD_DIM, plan.rows
    z, a = ids[0], ids[1]
    ones = jnp.ones((EXTRA, hd), BF16)
    row = lax.broadcasted_iota(jnp.int32, (EXTRA, rows), 0)
    for s, out in enumerate(outs):
        for r in range(plan.nz):
            head = (z ^ r) * plan.hh + (a ^ s)
            cols = pl.ds(pl.multiple_of(head * hd, hd), hd)
            grad = g_ref[:, cols]
            out[r, :rows] = grad
            product = grad.astype(F32) * o_ref[:, cols].astype(F32)
            high = product.astype(BF16)
            low = (product - high.astype(F32)).astype(BF16)
            delta = dot(ones, high, NT) + dot(ones, low, NT)
            first = delta.astype(BF16)
            rest = delta - first.astype(F32)
            second = rest.astype(BF16)
            third = (rest - second.astype(F32)).astype(BF16)
            parts = jnp.where(
                row == 0,
                first.astype(F32),
                jnp.where(row == 1, second.astype(F32), jnp.where(row == 2, third.astype(F32), 0.0)),
            )
            out[r, rows:] = parts.astype(BF16)


def prep_grad(plan, ids, g, o):
    return pl.pallas_call(
        functools.partial(prep_grad_kernel, plan),
        out_shape=[sds((plan.nz, plan.rows + EXTRA, HEAD_DIM), BF16)] * plan.na,
        in_specs=[SMEM, VMEM, VMEM],
        out_specs=[VMEM] * plan.na,
        cost_estimate=cost(0, 6 * g.size),
        name="prep_grad",
    )(ids, g, o)


def lists_kernel(plan, ids, order, live_ref, by_key, n_key, by_query, n_query):
    nz, na, nb, own = plan.nz, plan.na, plan.nb, plan.own
    z, a, b = ids[0], ids[1], ids[2]

    def clear(i, carry):
        n_query[i] = 0
        return carry

    lax.fori_loop(0, plan.total, clear, 0)

    def key_block(j, carry):
        s_key, r_key = j // nz, j % nz
        place_key = order[(a ^ s_key) * nb + b]
        block_key = z ^ r_key

        def query_block(i, count):
            t, m = i // own, i % own
            s, r = m // nz, m % nz
            place = order[(a ^ s) * nb + (b ^ t)]
            distance = jnp.abs(place - place_key)
            live = (live_ref[distance, z ^ r, block_key] > 0).astype(jnp.int32)
            by_key[j, count] = i
            seen = n_query[i]
            by_query[i, seen] = j
            n_query[i] = seen + live
            return count + live

        n_key[j] = lax.fori_loop(0, plan.total, query_block, 0)
        return carry

    lax.fori_loop(0, own, key_block, 0)


def lists(plan, ids, order, live):
    own, total = plan.own, plan.total
    return pl.pallas_call(
        functools.partial(lists_kernel, plan),
        out_shape=[
            sds((own, total + 1), jnp.int32),
            sds((own,), jnp.int32),
            sds((total, own + 1), jnp.int32),
            sds((total,), jnp.int32),
        ],
        in_specs=[SMEM] * 3,
        out_specs=[SMEM] * 4,
        cost_estimate=cost(0, 8 * own * total),
        name="lists",
    )(ids, order, live)


def picks(table, row, count, first):
    out = []
    for u in range(GROUP):
        valid = first + u < count
        out.append((jnp.where(valid, table[row, first + u], 0), valid))
    return out


def totals_kernel(plan, by_query, n_query, k_ref, *refs):
    nb, own, rows = plan.nb, plan.own, plan.rows
    q_refs, out = refs[:nb], refs[nb]
    scale = HEAD_DIM**-0.5
    for t, q_ref in enumerate(q_refs):

        def query_block(m, carry, q_ref=q_ref, t=t):
            i = t * own + m
            count = n_query[i]
            q = q_ref[m]

            def group(step, state):
                peak, total = state
                parts = []
                for j, valid in picks(by_query, i, count, step * GROUP):
                    part = scale * dot(k_ref[j], q, NT)
                    parts.append(jnp.where(valid, part, NEG))
                best = functools.reduce(jnp.maximum, parts)
                new_peak = jnp.maximum(peak, jnp.max(best, axis=0, keepdims=True))
                sums = functools.reduce(jnp.add, [jnp.exp(part - new_peak) for part in parts])
                fresh = jnp.sum(sums, axis=0, keepdims=True)
                return new_peak, total * jnp.exp(peak - new_peak) + fresh

            start = (jnp.full((1, rows), NEG, F32), jnp.zeros((1, rows), F32))
            steps = (count + GROUP - 1) // GROUP
            peak, total = lax.fori_loop(0, steps, group, start)
            safe = jnp.where(total > 0.0, total, 1.0)
            out[pl.ds(i, 1), :] = jnp.where(total > 0.0, peak + jnp.log(safe), NEG)
            return carry

        lax.fori_loop(0, own, query_block, 0)


def totals(plan, by_query, n_query, keys, queries):
    pairs = plan.own * plan.total
    return pl.pallas_call(
        functools.partial(totals_kernel, plan),
        out_shape=sds((plan.total, plan.rows), F32),
        in_specs=[SMEM, SMEM] + [VMEM] * (1 + plan.nb),
        out_specs=VMEM,
        cost_estimate=cost(pairs * 2 * 128**3, 0),
        name="totals",
    )(by_query, n_query, keys, *queries)


def grads_kernel(plan, by_key, n_key, ids, *refs):
    nz, na, nb, own, rows = plan.nz, plan.na, plan.nb, plan.own, plan.rows
    hd = HEAD_DIM
    scale = hd**-0.5
    refs = list(refs)
    take = lambda n: [refs.pop(0) for _ in range(n)]
    q_refs, g_refs, lse_refs = take(nb), take(nb), take(nb)
    k_ref, v_ref = take(2)
    kv_outs, dq_outs = take(na), take(nb)
    q_all, g_all, lse_all, delta_all, dq_all, dk_acc, dv_acc = refs

    for t in range(nb):
        span = pl.ds(t * own, own)
        rivals = [lse_refs[u][pl.ds((t ^ u) * own, own), :] for u in range(nb)]
        peak = functools.reduce(jnp.maximum, rivals)
        lse_all[span, :] = peak + jnp.log(sum(jnp.exp(x - peak) for x in rivals))

        def fill(m, carry, t=t):
            i = t * own + m
            q_all[i] = q_refs[t][m]
            g_all[i] = g_refs[t][m, :rows]
            extra = g_refs[t][m, rows:].astype(F32)
            delta_all[pl.ds(i, 1), :] = jnp.sum(extra, axis=0, keepdims=True)
            dq_all[i] = jnp.zeros((rows, hd), F32)
            return carry

        lax.fori_loop(0, own, fill, 0)

    def key_block(j, carry):
        count = n_key[j]
        k, v = k_ref[j], v_ref[j]
        dk_acc[...] = jnp.zeros_like(dk_acc)
        dv_acc[...] = jnp.zeros_like(dv_acc)

        def group(step, carry):
            chosen = picks(by_key, j, count, step * GROUP)
            q = jnp.concatenate([q_all[i] for i, _ in chosen], axis=0)
            g = jnp.concatenate([g_all[i] for i, _ in chosen], axis=0)
            lse = jnp.concatenate(
                [jnp.where(ok, lse_all[pl.ds(i, 1), :], -NEG) for i, ok in chosen], axis=1
            )
            delta = jnp.concatenate([delta_all[pl.ds(i, 1), :] for i, _ in chosen], axis=1)
            probs = jnp.exp(scale * dot(k, q, NT) - lse)
            dv_acc[...] += dot(probs.astype(BF16), g, NN)
            grad_scores = (probs * (dot(v, g, NT) - delta)).astype(BF16)
            dk_acc[...] += dot(grad_scores, q, NN)
            dq = dot(grad_scores, k, TN)
            for u, (i, _) in enumerate(chosen):
                dq_all[i] += dq[u * rows : (u + 1) * rows]
            return carry

        lax.fori_loop(0, (count + GROUP - 1) // GROUP, group, 0)
        s, place = j // nz, ids[0] ^ (j % nz)
        for slot, out in enumerate(kv_outs):

            @pl.when(s == slot)
            def _():
                out[0, place] = (scale * dk_acc[...]).astype(BF16)
                out[1, place] = dv_acc[...].astype(BF16)

        return carry

    lax.fori_loop(0, own, key_block, 0)
    for t in range(nb):

        def drain(m, carry, t=t):
            dq_outs[t][m] = scale * dq_all[t * own + m]
            return carry

        lax.fori_loop(0, own, drain, 0)


def grads(plan, by_key, n_key, ids, queries, out_grads, lses, keys, values):
    nb, na, own, rows, total = plan.nb, plan.na, plan.own, plan.rows, plan.total
    hd = HEAD_DIM
    outs = pl.pallas_call(
        functools.partial(grads_kernel, plan),
        out_shape=[sds((2, plan.nz, rows, hd), BF16)] * na + [sds((own, rows, hd), F32)] * nb,
        in_specs=[SMEM] * 3 + [VMEM] * (3 * nb + 2),
        out_specs=[VMEM] * (na + nb),
        scratch_shapes=[
            pltpu.VMEM((total, rows, hd), BF16),
            pltpu.VMEM((total, rows, hd), BF16),
            pltpu.VMEM((total, rows), F32),
            pltpu.VMEM((total, rows), F32),
            pltpu.VMEM((total, rows, hd), F32),
            pltpu.VMEM((rows, hd), F32),
            pltpu.VMEM((rows, hd), F32),
        ],
        cost_estimate=cost(own * total * 10 * 128**3, 0),
        name="grads",
    )(by_key, n_key, ids, *queries, *out_grads, *lses, keys, values)
    return outs[:na], outs[na:]


def pack_kernel(plan, ids, *refs):
    nb, nz = plan.nb, plan.nz
    for s, out in enumerate(refs[nb:]):
        for r in range(nz):
            total = sum(ref[s * nz + r] for ref in refs[:nb])
            out[ids[0] ^ r] = total.astype(BF16)


def pack(plan, ids, partials):
    return pl.pallas_call(
        functools.partial(pack_kernel, plan),
        out_shape=[sds((plan.nz, plan.rows, HEAD_DIM), BF16)] * plan.na,
        in_specs=[SMEM] + [VMEM] * plan.nb,
        out_specs=[VMEM] * plan.na,
        cost_estimate=cost(0, 1 << 20),
        name="pack",
    )(ids, *partials)


def assemble_kernel(plan, n, ids, *refs):
    na, nz, rows, hd = plan.na, plan.nz, plan.rows, HEAD_DIM
    for s in range(na):
        cols = pl.ds(pl.multiple_of((ids[1] ^ s) * hd, hd), hd)
        for w in range(n):
            for r in range(nz):
                refs[na + w][r * rows : (r + 1) * rows, cols] = refs[s][w, r]


def assemble(plan, ids, pieces):
    n = pieces[0].shape[0]
    return pl.pallas_call(
        functools.partial(assemble_kernel, plan, n),
        out_shape=[sds((plan.nz * plan.rows, plan.na * HEAD_DIM), BF16)] * n,
        in_specs=[SMEM] + [VMEM] * plan.na,
        out_specs=[VMEM] * n,
        cost_estimate=cost(0, 1 << 20),
        name="assemble",
    )(ids, *pieces)


def local(queries, key_states, value_states, attn_out, grad_out, frame_order, block_live):
    plan = Plan(queries.shape[0])
    nz, na, nb = plan.nz, plan.na, plan.nb
    slot = lax.axis_index("frame")
    ids = jnp.stack([lax.axis_index("head"), slot // nb, slot % nb]).astype(jnp.int32)

    def head_stage(pieces):
        moved = {r: over_head(pieces[r], r) for r in [*range(2, nz), 1]}
        return [pieces[0]] + [moved[r] for r in range(1, nz)]

    def frame_stage(pieces):
        moved = {s: over_frame(pieces[s], s * nb) for s in range(na - 1, 0, -1)}
        return [pieces[0]] + [moved[s] for s in range(1, na)]

    def regroup(pieces):
        return [jnp.concatenate([p[i : i + 1] for p in pieces]) for i in range(pieces[0].shape[0])]

    def flat_frames_first(by_frame):
        return jnp.concatenate(by_frame)

    def flat_heads_first(by_head):
        return jnp.concatenate([p[s : s + 1] for s in range(na) for p in by_head])

    q_sent = head_stage(prep(plan, ids, queries, True))
    k_near = frame_stage(prep(plan, ids, key_states, False))
    g_near = frame_stage(prep_grad(plan, ids, grad_out, attn_out))
    v_near = frame_stage(prep(plan, ids, value_states, False))
    by_key, n_key, by_query, n_query = lists(plan, ids, frame_order, block_live)
    keys = flat_heads_first(head_stage(regroup(k_near)))
    q_own = flat_frames_first(frame_stage(regroup(q_sent)))
    q_all = [q_own] + [over_frame(q_own, t) for t in range(1, nb)]
    g_own = flat_heads_first(head_stage(regroup(g_near)))
    g_all = [g_own] + [over_frame(g_own, t) for t in range(1, nb)]
    values = flat_heads_first(head_stage(regroup(v_near)))

    lse_own = totals(plan, by_query, n_query, keys, q_all)
    lses = [lse_own] + [over_frame(lse_own, t) for t in range(1, nb)]
    kv_sent, dq_parts = grads(plan, by_key, n_key, ids, q_all, g_all, lses, keys, values)
    dq_parts = [dq_parts[0]] + [over_frame(dq_parts[t], t) for t in range(1, nb)]
    kv_home = frame_stage(kv_sent)
    dq_home = frame_stage(pack(plan, ids, dq_parts))
    grad_key, grad_value = assemble(plan, ids, kv_home)
    (grad_query,) = assemble(plan, ids, [p[None] for p in dq_home])
    return grad_query, grad_key, grad_value


def solution(mesh):
    rows = P(("frame", "head"), None)
    in_specs = (rows,) * 5 + (P(), P())
    out_specs = (P("frame", "head"),) * 3
    return jax.shard_map(local, mesh=mesh, in_specs=in_specs, out_specs=out_specs, check_vma=False)
```

```python
import functools

import jax
import jax.numpy as jnp
from jax import lax
from jax.experimental import pallas as pl
from jax.experimental.pallas import tpu as pltpu
from jax.sharding import PartitionSpec as P

HEADS = 16
HEAD_DIM = 128
NEG = -1e30
KEY_GROUP = 6
QUERY_GROUP = 4
PAIR = 2
EXTRA = 8


VMEM = pl.BlockSpec(memory_space=pltpu.VMEM)
SMEM = pl.BlockSpec(memory_space=pltpu.SMEM)
F32 = jnp.float32
BF16 = jnp.bfloat16
NT = (((1,), (1,)), ((), ()))
TN = (((0,), (0,)), ((), ()))
NN = (((1,), (0,)), ((), ()))


def dot(a, b, dims):
    return lax.dot_general(a, b, dims, preferred_element_type=F32)


def sds(shape, dtype):
    return jax.ShapeDtypeStruct(shape, dtype)


def lasts(microseconds):
    return pl.CostEstimate(flops=0, bytes_accessed=int(microseconds * 3.5e6), transcendentals=0)


class Plan:
    def __init__(self, rows):
        self.nz = lax.axis_size("head")
        self.nf = lax.axis_size("frame")
        self.hh = HEADS // self.nz
        self.na = min(self.hh, self.nf)
        self.nb = self.nf // self.na
        self.rows = rows
        self.own = self.na * self.nz
        self.total = self.own * self.nb
        assert self.hh == self.na and rows == HEAD_DIM


def over_head(value, step):
    count = lax.axis_size("head")
    return lax.ppermute(value, "head", [(i, i ^ step) for i in range(count)])


def over_frame(value, step):
    count = lax.axis_size("frame")
    return lax.ppermute(value, "frame", [(i, i ^ step) for i in range(count)])


def prep_kernel(plan, head_first, ids, x_ref, *outs):
    hd = HEAD_DIM
    z, a = ids[0], ids[1]
    for p, out in enumerate(outs):
        for c in range(out.shape[0]):
            r, s = (p, c) if head_first else (c, p)
            head = (z ^ r) * plan.hh + (a ^ s)
            out[c] = x_ref[:, pl.ds(pl.multiple_of(head * hd, hd), hd)]


def prep(plan, ids, x, head_first):
    pieces, chunk = (plan.nz, plan.na) if head_first else (plan.na, plan.nz)
    return pl.pallas_call(
        functools.partial(prep_kernel, plan, head_first),
        out_shape=[sds((chunk, plan.rows, HEAD_DIM), BF16)] * pieces,
        in_specs=[SMEM, VMEM],
        out_specs=[VMEM] * pieces,
        cost_estimate=lasts(2),
        name="prep",
    )(ids, x)


def prep_grad_kernel(plan, ids, g_ref, o_ref, *outs):
    hd, rows = HEAD_DIM, plan.rows
    z, a = ids[0], ids[1]
    ones = jnp.ones((EXTRA, hd), BF16)
    row = lax.broadcasted_iota(jnp.int32, (EXTRA, rows), 0)
    for s, out in enumerate(outs):
        for r in range(plan.nz):
            head = (z ^ r) * plan.hh + (a ^ s)
            cols = pl.ds(pl.multiple_of(head * hd, hd), hd)
            grad = g_ref[:, cols]
            out[r, :rows] = grad
            product = grad.astype(F32) * o_ref[:, cols].astype(F32)
            high = product.astype(BF16)
            low = (product - high.astype(F32)).astype(BF16)
            delta = dot(ones, high, NT) + dot(ones, low, NT)
            first = delta.astype(BF16)
            rest = delta - first.astype(F32)
            second = rest.astype(BF16)
            third = (rest - second.astype(F32)).astype(BF16)
            parts = jnp.where(
                row == 0,
                first.astype(F32),
                jnp.where(row == 1, second.astype(F32), jnp.where(row == 2, third.astype(F32), 0.0)),
            )
            out[r, rows:] = parts.astype(BF16)


def prep_grad(plan, ids, g, o):
    return pl.pallas_call(
        functools.partial(prep_grad_kernel, plan),
        out_shape=[sds((plan.nz, plan.rows + EXTRA, HEAD_DIM), BF16)] * plan.na,
        in_specs=[SMEM, VMEM, VMEM],
        out_specs=[VMEM] * plan.na,
        cost_estimate=lasts(2.5),
        name="prep_grad",
    )(ids, g, o)


def lists_kernel(plan, ids, order, live_ref, by_key, n_key, by_query, n_query):
    nz, na, nb = plan.nz, plan.na, plan.nb
    z, a, b = ids[0], ids[1], ids[2]
    true = [z ^ r for r in range(nz)]

    def key_frame(s_key, carry):
        place_key = order[(a ^ s_key) * nb + b]

        def query_frame(ts, counts):
            t = ts // na
            place = order[(a ^ (ts - t * na)) * nb + (b ^ t)]
            distance = jnp.abs(place - place_key)
            away = (ts != s_key).astype(jnp.int32)
            counts = list(counts)
            for r in range(nz):
                i = ts * nz + r
                seen = jnp.where(s_key == 0, 0, n_query[i])
                for rk in range(nz):
                    live = jnp.where(live_ref[distance, true[r], true[rk]] > 0, away, 0)
                    by_key[s_key * nz + rk, counts[rk]] = i
                    by_query[i, seen] = s_key * nz + rk
                    counts[rk] = counts[rk] + live
                    seen = seen + live
                n_query[i] = seen
            return tuple(counts)

        counts = lax.fori_loop(0, na * nb, query_frame, (jnp.int32(0),) * nz)
        for rk in range(nz):
            n_key[s_key * nz + rk] = counts[rk]
        return carry

    lax.fori_loop(0, na, key_frame, 0)


def lists(plan, ids, order, live):
    own, total = plan.own, plan.total
    return pl.pallas_call(
        functools.partial(lists_kernel, plan),
        out_shape=[
            sds((own, total + KEY_GROUP), jnp.int32),
            sds((own,), jnp.int32),
            sds((total, own + QUERY_GROUP), jnp.int32),
            sds((total,), jnp.int32),
        ],
        in_specs=[SMEM] * 3,
        out_specs=[SMEM] * 4,
        cost_estimate=lasts(5),
        name="lists",
    )(ids, order, live)


def picks(table, row, count, first, size):
    out = []
    for u in range(size):
        valid = first + u < count
        out.append((jnp.where(valid, table[row, first + u], 0), valid))
    return out


def rounds(count, size):
    return lax.div(count + (size - 1), size)


def totals_kernel(plan, by_query, n_query, k_ref, *refs):
    nz, na, nb, own, rows = plan.nz, plan.na, plan.nb, plan.own, plan.rows
    q_refs, out, peaks, sums = refs[:nb], refs[nb], refs[nb + 1], refs[nb + 2]
    scale = HEAD_DIM**-0.5
    length = nz * rows

    def scores_of(i, q, first):
        parts = []
        for j, valid in picks(by_query, i, n_query[i], first, QUERY_GROUP):
            parts.append(jnp.where(valid, scale * dot(k_ref[j], q, NT), NEG))
        return parts

    for t, q_ref in enumerate(q_refs):

        def frame(s, carry, q_ref=q_ref, t=t):
            if t == 0:
                keys = k_ref[pl.ds(s * nz, nz)].reshape(length, HEAD_DIM)
                wide = scale * dot(keys, q_ref[pl.ds(s * nz, nz)].reshape(length, HEAD_DIM), NT)
            for r in range(nz):
                i = (t * na + s) * nz + r
                parts = scores_of(i, q_ref[s * nz + r], 0)
                if t == 0:
                    column = wide[:, r * rows : (r + 1) * rows]
                    parts += [column[c * rows : (c + 1) * rows] for c in range(nz)]
                peak = jnp.max(functools.reduce(jnp.maximum, parts), axis=0, keepdims=True)
                mass = functools.reduce(jnp.add, [jnp.exp(part - peak) for part in parts])
                peaks[pl.ds(i, 1), :] = peak
                sums[pl.ds(i, 1), :] = jnp.sum(mass, axis=0, keepdims=True)
            return carry

        lax.fori_loop(0, na, frame, 0)

        def block(m, carry, q_ref=q_ref, t=t):
            i = t * own + m

            def group(step, carry):
                parts = scores_of(i, q_ref[m], step * QUERY_GROUP)
                old = peaks[pl.ds(i, 1), :]
                best = functools.reduce(jnp.maximum, parts)
                peak = jnp.maximum(old, jnp.max(best, axis=0, keepdims=True))
                mass = functools.reduce(jnp.add, [jnp.exp(part - peak) for part in parts])
                fresh = jnp.sum(mass, axis=0, keepdims=True)
                peaks[pl.ds(i, 1), :] = peak
                sums[pl.ds(i, 1), :] = sums[pl.ds(i, 1), :] * jnp.exp(old - peak) + fresh
                return carry

            return lax.fori_loop(1, rounds(n_query[i], QUERY_GROUP), group, carry)

        lax.fori_loop(0, own, block, 0)
    peak = peaks[...]
    out[...] = jnp.where(peak > 0.5 * NEG, peak + jnp.log(sums[...]), NEG)


def totals(plan, by_query, n_query, keys, queries):
    return pl.pallas_call(
        functools.partial(totals_kernel, plan),
        out_shape=sds((plan.total, plan.rows), F32),
        in_specs=[SMEM, SMEM] + [VMEM] * (1 + plan.nb),
        out_specs=VMEM,
        scratch_shapes=[pltpu.VMEM((plan.total, plan.rows), F32)] * 2,
        cost_estimate=lasts(10),
        name="totals",
    )(by_query, n_query, keys, *queries)


def grads_kernel(plan, by_key, n_key, ids, *refs):
    nz, na, nb, own, rows = plan.nz, plan.na, plan.nb, plan.own, plan.rows
    hd = HEAD_DIM
    scale = hd**-0.5
    length = nz * rows
    refs = list(refs)
    take = lambda n: [refs.pop(0) for _ in range(n)]
    q_refs, g_refs, lse_refs = take(nb), take(nb), take(nb)
    k_ref, v_ref = take(2)
    kv_outs, dq_outs = take(na), take(nb)
    q_all, g_all, lse_all, delta_all, dq_all, dk_all, dv_all = refs

    for t in range(nb):
        span = pl.ds(t * own, own)
        rivals = [lse_refs[u][pl.ds((t ^ u) * own, own), :] for u in range(nb)]
        peak = functools.reduce(jnp.maximum, rivals)
        lse_all[span, :] = peak + jnp.log(sum(jnp.exp(x - peak) for x in rivals))

        def fill(m, carry, t=t):
            i = t * own + m
            q_all[i] = q_refs[t][m]
            g_all[i] = g_refs[t][m, :rows]
            extra = g_refs[t][m, rows:].astype(F32)
            delta_all[pl.ds(i, 1), :] = jnp.sum(extra, axis=0, keepdims=True)
            if t > 0:
                dq_all[i] = jnp.zeros((rows, hd), F32)
            return carry

        lax.fori_loop(0, own, fill, 0)

    def wide_row(ref, first):
        return jnp.concatenate([ref[pl.ds(first + r, 1), :] for r in range(nz)], axis=1)

    def diagonal(s, carry):
        span = pl.ds(s * nz, nz)
        k, v = k_ref[span].reshape(length, hd), v_ref[span].reshape(length, hd)
        q, g = q_all[span].reshape(length, hd), g_all[span].reshape(length, hd)
        lse, delta = wide_row(lse_all, s * nz), wide_row(delta_all, s * nz)
        probs = jnp.exp(scale * dot(k, q, NT) - lse)
        dv_all[span] = dot(probs.astype(BF16), g, NN).reshape(nz, rows, hd)
        grad_scores = (probs * (dot(v, g, NT) - delta)).astype(BF16)
        dk_all[span] = dot(grad_scores, q, NN).reshape(nz, rows, hd)
        dq_all[span] = dot(grad_scores, k, TN).reshape(nz, rows, hd)
        return carry

    lax.fori_loop(0, na, diagonal, 0)

    def terms(j, first):
        k, v = k_ref[j], v_ref[j]
        chosen = picks(by_key, j, n_key[j], first, KEY_GROUP)
        probs, slopes, dqs = [], [], []
        for i, ok in chosen:
            lse = jnp.where(ok, lse_all[pl.ds(i, 1), :], -NEG)
            prob = jnp.exp(scale * dot(k, q_all[i], NT) - lse)
            slope = (prob * (dot(v, g_all[i], NT) - delta_all[pl.ds(i, 1), :])).astype(BF16)
            probs.append(prob.astype(BF16))
            slopes.append(slope)
            dqs.append((i, dot(slope, k, TN)))
        q = jnp.concatenate([q_all[i] for i, _ in chosen], axis=0)
        g = jnp.concatenate([g_all[i] for i, _ in chosen], axis=0)
        dv = dot(jnp.concatenate(probs, axis=1), g, NN)
        dk = dot(jnp.concatenate(slopes, axis=1), q, NN)
        return dv, dk, dqs

    def add(j, found):
        dv, dk, dqs = found
        dv_all[j] += dv
        dk_all[j] += dk
        for i, dq in dqs:
            dq_all[i] += dq

    def pair(step, carry):
        both = [(step * PAIR + p, terms(step * PAIR + p, 0)) for p in range(PAIR)]
        for j, found in both:
            add(j, found)
        return carry

    lax.fori_loop(0, own // PAIR, pair, 0)

    def rest(j, carry):
        def group(step, carry):
            add(j, terms(j, step * KEY_GROUP))
            return carry

        return lax.fori_loop(1, rounds(n_key[j], KEY_GROUP), group, carry)

    lax.fori_loop(0, own, rest, 0)

    for s, out in enumerate(kv_outs):
        for r in range(nz):
            out[0, ids[0] ^ r] = (scale * dk_all[s * nz + r]).astype(BF16)
            out[1, ids[0] ^ r] = dv_all[s * nz + r].astype(BF16)
    for t in range(nb):

        def drain(m, carry, t=t):
            dq_outs[t][m] = scale * dq_all[t * own + m]
            return carry

        lax.fori_loop(0, own, drain, 0)


def grads(plan, by_key, n_key, ids, queries, out_grads, lses, keys, values):
    nb, na, own, rows, total = plan.nb, plan.na, plan.own, plan.rows, plan.total
    hd = HEAD_DIM
    outs = pl.pallas_call(
        functools.partial(grads_kernel, plan),
        out_shape=[sds((2, plan.nz, rows, hd), BF16)] * na + [sds((own, rows, hd), F32)] * nb,
        in_specs=[SMEM] * 3 + [VMEM] * (3 * nb + 2),
        out_specs=[VMEM] * (na + nb),
        scratch_shapes=[
            pltpu.VMEM((total, rows, hd), BF16),
            pltpu.VMEM((total, rows, hd), BF16),
            pltpu.VMEM((total, rows), F32),
            pltpu.VMEM((total, rows), F32),
            pltpu.VMEM((total, rows, hd), F32),
            pltpu.VMEM((own, rows, hd), F32),
            pltpu.VMEM((own, rows, hd), F32),
        ],
        cost_estimate=lasts(15),
        name="grads",
    )(by_key, n_key, ids, *queries, *out_grads, *lses, keys, values)
    return outs[:na], outs[na:]


def pack_kernel(plan, ids, *refs):
    nb, nz = plan.nb, plan.nz
    for s, out in enumerate(refs[nb:]):
        for r in range(nz):
            total = sum(ref[s * nz + r] for ref in refs[:nb])
            out[ids[0] ^ r] = total.astype(BF16)


def pack(plan, ids, partials):
    return pl.pallas_call(
        functools.partial(pack_kernel, plan),
        out_shape=[sds((plan.nz, plan.rows, HEAD_DIM), BF16)] * plan.na,
        in_specs=[SMEM] + [VMEM] * plan.nb,
        out_specs=[VMEM] * plan.na,
        cost_estimate=lasts(2),
        name="pack",
    )(ids, *partials)


def assemble_kernel(plan, n, ids, *refs):
    na, nz, rows, hd = plan.na, plan.nz, plan.rows, HEAD_DIM
    for s in range(na):
        cols = pl.ds(pl.multiple_of((ids[1] ^ s) * hd, hd), hd)
        for w in range(n):
            for r in range(nz):
                refs[na + w][r * rows : (r + 1) * rows, cols] = refs[s][w, r]


def assemble(plan, ids, pieces):
    n = pieces[0].shape[0]
    return pl.pallas_call(
        functools.partial(assemble_kernel, plan, n),
        out_shape=[sds((plan.nz * plan.rows, plan.na * HEAD_DIM), BF16)] * n,
        in_specs=[SMEM] + [VMEM] * plan.na,
        out_specs=[VMEM] * n,
        cost_estimate=lasts(2),
        name="assemble",
    )(ids, *pieces)


def local(queries, key_states, value_states, attn_out, grad_out, frame_order, block_live):
    plan = Plan(queries.shape[0])
    nz, na, nb = plan.nz, plan.na, plan.nb
    slot = lax.axis_index("frame")
    ids = jnp.stack([lax.axis_index("head"), slot // nb, slot % nb]).astype(jnp.int32)

    def head_stage(pieces):
        moved = {r: over_head(pieces[r], r) for r in [*range(2, nz), 1]}
        return [pieces[0]] + [moved[r] for r in range(1, nz)]

    def frame_stage(pieces):
        moved = {s: over_frame(pieces[s], s * nb) for s in range(na - 1, 0, -1)}
        return [pieces[0]] + [moved[s] for s in range(1, na)]

    def regroup(pieces):
        return [jnp.concatenate([p[i : i + 1] for p in pieces]) for i in range(pieces[0].shape[0])]

    def flat_frames_first(by_frame):
        return jnp.concatenate(by_frame)

    def flat_heads_first(by_head):
        return jnp.concatenate([p[s : s + 1] for s in range(na) for p in by_head])

    q_sent = head_stage(prep(plan, ids, queries, True))
    k_near = frame_stage(prep(plan, ids, key_states, False))
    g_near = frame_stage(prep_grad(plan, ids, grad_out, attn_out))
    v_near = frame_stage(prep(plan, ids, value_states, False))
    by_key, n_key, by_query, n_query = lists(plan, ids, frame_order, block_live)
    keys = flat_heads_first(head_stage(regroup(k_near)))
    q_own = flat_frames_first(frame_stage(regroup(q_sent)))
    q_all = [q_own] + [over_frame(q_own, t) for t in range(1, nb)]
    g_own = flat_heads_first(head_stage(regroup(g_near)))
    g_all = [g_own] + [over_frame(g_own, t) for t in range(1, nb)]
    values = flat_heads_first(head_stage(regroup(v_near)))

    lse_own = totals(plan, by_query, n_query, keys, q_all)
    lses = [lse_own] + [over_frame(lse_own, t) for t in range(1, nb)]
    kv_sent, dq_parts = grads(plan, by_key, n_key, ids, q_all, g_all, lses, keys, values)
    dq_parts = [dq_parts[0]] + [over_frame(dq_parts[t], t) for t in range(1, nb)]
    kv_home = frame_stage(kv_sent)
    dq_home = frame_stage(pack(plan, ids, dq_parts))
    grad_key, grad_value = assemble(plan, ids, kv_home)
    (grad_query,) = assemble(plan, ids, [p[None] for p in dq_home])
    return grad_query, grad_key, grad_value


def solution(mesh):
    rows = P(("frame", "head"), None)
    in_specs = (rows,) * 5 + (P(), P())
    out_specs = (P("frame", "head"),) * 3
    return jax.shard_map(local, mesh=mesh, in_specs=in_specs, out_specs=out_specs, check_vma=False)
```

```python
import functools
import math

import jax
import jax.numpy as jnp
from jax import lax
from jax.experimental import pallas as pl
from jax.experimental.pallas import tpu as pltpu
from jax.sharding import PartitionSpec as P


HEADS = 16
HEAD_DIM = 128
NEG = -1e30
KEY_GROUP = 6
QUERY_GROUP = 4
PAIR = 2
EXTRA = 8


VMEM = pl.BlockSpec(memory_space=pltpu.VMEM)
SMEM = pl.BlockSpec(memory_space=pltpu.SMEM)
F32 = jnp.float32
BF16 = jnp.bfloat16
NT = (((1,), (1,)), ((), ()))
TN = (((0,), (0,)), ((), ()))
NN = (((1,), (0,)), ((), ()))


def dot(a, b, dims):
    return lax.dot_general(a, b, dims, preferred_element_type=F32)


def sds(shape, dtype):
    return jax.ShapeDtypeStruct(shape, dtype)


def lasts(microseconds):
    return pl.CostEstimate(flops=0, bytes_accessed=int(microseconds * 3.5e6), transcendentals=0)


def within(*shapes):
    held = sum(math.prod(s.shape) * s.dtype.itemsize for s in shapes)
    return pltpu.CompilerParams(vmem_limit_bytes=int(held * 5 // 4) + (6 << 20))


class Plan:
    def __init__(self, rows):
        self.nz = lax.axis_size("head")
        self.nf = lax.axis_size("frame")
        self.hh = HEADS // self.nz
        self.na = min(self.hh, self.nf)
        self.nb = self.nf // self.na
        self.rows = rows
        self.own = self.na * self.nz
        self.total = self.own * self.nb
        assert self.hh == self.na and rows == HEAD_DIM


def over_head(value, step):
    count = lax.axis_size("head")
    return lax.ppermute(value, "head", [(i, i ^ step) for i in range(count)])


def over_frame(value, step):
    count = lax.axis_size("frame")
    return lax.ppermute(value, "frame", [(i, i ^ step) for i in range(count)])


def prep_kernel(plan, head_first, ids, x_ref, *outs):
    hd = HEAD_DIM
    z, a = ids[0], ids[1]
    for p, out in enumerate(outs):
        for c in range(out.shape[0]):
            r, s = (p, c) if head_first else (c, p)
            head = (z ^ r) * plan.hh + (a ^ s)
            out[c] = x_ref[:, pl.ds(pl.multiple_of(head * hd, hd), hd)]


def prep(plan, ids, x, head_first):
    pieces, chunk = (plan.nz, plan.na) if head_first else (plan.na, plan.nz)
    return pl.pallas_call(
        functools.partial(prep_kernel, plan, head_first),
        out_shape=[sds((chunk, plan.rows, HEAD_DIM), BF16)] * pieces,
        in_specs=[SMEM, VMEM],
        out_specs=[VMEM] * pieces,
        cost_estimate=lasts(2),
        compiler_params=within(x, x),
    )(ids, x)


def prep_grad_kernel(plan, ids, g_ref, o_ref, *outs):
    hd, rows = HEAD_DIM, plan.rows
    z, a = ids[0], ids[1]
    ones = jnp.ones((EXTRA, hd), BF16)
    row = lax.broadcasted_iota(jnp.int32, (EXTRA, rows), 0)
    for s, out in enumerate(outs):
        for r in range(plan.nz):
            head = (z ^ r) * plan.hh + (a ^ s)
            cols = pl.ds(pl.multiple_of(head * hd, hd), hd)
            grad = g_ref[:, cols]
            out[r, :rows] = grad
            product = grad.astype(F32) * o_ref[:, cols].astype(F32)
            high = product.astype(BF16)
            low = (product - high.astype(F32)).astype(BF16)
            delta = dot(ones, high, NT) + dot(ones, low, NT)
            first = delta.astype(BF16)
            rest = delta - first.astype(F32)
            second = rest.astype(BF16)
            third = (rest - second.astype(F32)).astype(BF16)
            parts = jnp.where(
                row == 0,
                first.astype(F32),
                jnp.where(row == 1, second.astype(F32), jnp.where(row == 2, third.astype(F32), 0.0)),
            )
            out[r, rows:] = parts.astype(BF16)


def prep_grad(plan, ids, g, o):
    return pl.pallas_call(
        functools.partial(prep_grad_kernel, plan),
        out_shape=[sds((plan.nz, plan.rows + EXTRA, HEAD_DIM), BF16)] * plan.na,
        in_specs=[SMEM, VMEM, VMEM],
        out_specs=[VMEM] * plan.na,
        cost_estimate=lasts(2.5),
        compiler_params=within(g, o, g),
        name="prep_grad",
    )(ids, g, o)


def lists_kernel(plan, ids, order, live_ref, by_key, n_key, by_query, n_query):
    nz, na, nb = plan.nz, plan.na, plan.nb
    z, a, b = ids[0], ids[1], ids[2]
    true = [z ^ r for r in range(nz)]

    def key_frame(s_key, carry):
        place_key = order[(a ^ s_key) * nb + b]

        def query_frame(ts, counts):
            t = ts // na
            place = order[(a ^ (ts - t * na)) * nb + (b ^ t)]
            distance = jnp.abs(place - place_key)
            away = (ts != s_key).astype(jnp.int32)
            counts = list(counts)
            for r in range(nz):
                i = ts * nz + r
                seen = jnp.where(s_key == 0, 0, n_query[i])
                for rk in range(nz):
                    live = jnp.where(live_ref[distance, true[r], true[rk]] > 0, away, 0)
                    by_key[s_key * nz + rk, counts[rk]] = i
                    by_query[i, seen] = s_key * nz + rk
                    counts[rk] = counts[rk] + live
                    seen = seen + live
                n_query[i] = seen
            return tuple(counts)

        counts = lax.fori_loop(0, na * nb, query_frame, (jnp.int32(0),) * nz)
        for rk in range(nz):
            n_key[s_key * nz + rk] = counts[rk]
        return carry

    lax.fori_loop(0, na, key_frame, 0)


def lists(plan, ids, order, live):
    own, total = plan.own, plan.total
    return pl.pallas_call(
        functools.partial(lists_kernel, plan),
        out_shape=[
            sds((own, total + KEY_GROUP), jnp.int32),
            sds((own,), jnp.int32),
            sds((total, own + QUERY_GROUP), jnp.int32),
            sds((total,), jnp.int32),
        ],
        in_specs=[SMEM] * 3,
        out_specs=[SMEM] * 4,
        cost_estimate=lasts(5),
        compiler_params=within(),
        name="lists",
    )(ids, order, live)


def picks(table, row, count, first, size):
    out = []
    for u in range(size):
        valid = first + u < count
        out.append((jnp.where(valid, table[row, first + u], 0), valid))
    return out


def rounds(count, size):
    return lax.div(count + (size - 1), size)


def totals_kernel(plan, by_query, n_query, k_ref, *refs):
    nz, na, nb, own, rows = plan.nz, plan.na, plan.nb, plan.own, plan.rows
    q_refs, out, peaks, sums = refs[:nb], refs[nb], refs[nb + 1], refs[nb + 2]
    scale = HEAD_DIM**-0.5
    length = nz * rows

    def scores_of(i, q, first):
        parts = []
        for j, valid in picks(by_query, i, n_query[i], first, QUERY_GROUP):
            parts.append(jnp.where(valid, scale * dot(k_ref[j], q, NT), NEG))
        return parts

    for t, q_ref in enumerate(q_refs):

        def frame(s, carry, q_ref=q_ref, t=t):
            if t == 0:
                keys = k_ref[pl.ds(s * nz, nz)].reshape(length, HEAD_DIM)
                wide = scale * dot(keys, q_ref[pl.ds(s * nz, nz)].reshape(length, HEAD_DIM), NT)
            for r in range(nz):
                i = (t * na + s) * nz + r
                parts = scores_of(i, q_ref[s * nz + r], 0)
                if t == 0:
                    column = wide[:, r * rows : (r + 1) * rows]
                    parts += [column[c * rows : (c + 1) * rows] for c in range(nz)]
                peak = jnp.max(functools.reduce(jnp.maximum, parts), axis=0, keepdims=True)
                mass = functools.reduce(jnp.add, [jnp.exp(part - peak) for part in parts])
                peaks[pl.ds(i, 1), :] = peak
                sums[pl.ds(i, 1), :] = jnp.sum(mass, axis=0, keepdims=True)
            return carry

        lax.fori_loop(0, na, frame, 0)

        def block(m, carry, q_ref=q_ref, t=t):
            i = t * own + m

            def group(step, carry):
                parts = scores_of(i, q_ref[m], step * QUERY_GROUP)
                old = peaks[pl.ds(i, 1), :]
                best = functools.reduce(jnp.maximum, parts)
                peak = jnp.maximum(old, jnp.max(best, axis=0, keepdims=True))
                mass = functools.reduce(jnp.add, [jnp.exp(part - peak) for part in parts])
                fresh = jnp.sum(mass, axis=0, keepdims=True)
                peaks[pl.ds(i, 1), :] = peak
                sums[pl.ds(i, 1), :] = sums[pl.ds(i, 1), :] * jnp.exp(old - peak) + fresh
                return carry

            return lax.fori_loop(1, rounds(n_query[i], QUERY_GROUP), group, carry)

        lax.fori_loop(0, own, block, 0)
    peak = peaks[...]
    out[...] = jnp.where(peak > 0.5 * NEG, peak + jnp.log(sums[...]), NEG)


def totals(plan, by_query, n_query, keys, queries):
    return pl.pallas_call(
        functools.partial(totals_kernel, plan),
        out_shape=sds((plan.total, plan.rows), F32),
        in_specs=[SMEM, SMEM] + [VMEM] * (1 + plan.nb),
        out_specs=VMEM,
        scratch_shapes=[pltpu.VMEM((plan.total, plan.rows), F32)] * 2,
        cost_estimate=lasts(10),
        compiler_params=within(keys, *queries),
        name="totals",
    )(by_query, n_query, keys, *queries)


def grads_kernel(plan, by_key, n_key, ids, *refs):
    nz, na, nb, own, rows = plan.nz, plan.na, plan.nb, plan.own, plan.rows
    hd = HEAD_DIM
    scale = hd**-0.5
    length = nz * rows
    refs = list(refs)
    take = lambda n: [refs.pop(0) for _ in range(n)]
    q_refs, g_refs, lse_refs = take(nb), take(nb), take(nb)
    k_ref, v_ref = take(2)
    kv_outs, dq_outs = take(na), take(nb)
    q_all, g_all, lse_all, delta_all, dq_all, dk_all, dv_all = refs

    for t in range(nb):
        span = pl.ds(t * own, own)
        rivals = [lse_refs[u][pl.ds((t ^ u) * own, own), :] for u in range(nb)]
        peak = functools.reduce(jnp.maximum, rivals)
        lse_all[span, :] = peak + jnp.log(sum(jnp.exp(x - peak) for x in rivals))

        def fill(m, carry, t=t):
            i = t * own + m
            q_all[i] = q_refs[t][m]
            g_all[i] = g_refs[t][m, :rows]
            extra = g_refs[t][m, rows:].astype(F32)
            delta_all[pl.ds(i, 1), :] = jnp.sum(extra, axis=0, keepdims=True)
            if t > 0:
                dq_all[i] = jnp.zeros((rows, hd), F32)
            return carry

        lax.fori_loop(0, own, fill, 0)

    def wide_row(ref, first):
        return jnp.concatenate([ref[pl.ds(first + r, 1), :] for r in range(nz)], axis=1)

    def diagonal(s, carry):
        span = pl.ds(s * nz, nz)
        k, v = k_ref[span].reshape(length, hd), v_ref[span].reshape(length, hd)
        q, g = q_all[span].reshape(length, hd), g_all[span].reshape(length, hd)
        lse, delta = wide_row(lse_all, s * nz), wide_row(delta_all, s * nz)
        probs = jnp.exp(scale * dot(k, q, NT) - lse)
        dv_all[span] = dot(probs.astype(BF16), g, NN).reshape(nz, rows, hd)
        grad_scores = (probs * (dot(v, g, NT) - delta)).astype(BF16)
        dk_all[span] = dot(grad_scores, q, NN).reshape(nz, rows, hd)
        dq_all[span] = dot(grad_scores, k, TN).reshape(nz, rows, hd)
        return carry

    lax.fori_loop(0, na, diagonal, 0)

    def terms(j, first):
        k, v = k_ref[j], v_ref[j]
        chosen = picks(by_key, j, n_key[j], first, KEY_GROUP)
        probs, slopes, dqs = [], [], []
        for i, ok in chosen:
            lse = jnp.where(ok, lse_all[pl.ds(i, 1), :], -NEG)
            prob = jnp.exp(scale * dot(k, q_all[i], NT) - lse)
            slope = (prob * (dot(v, g_all[i], NT) - delta_all[pl.ds(i, 1), :])).astype(BF16)
            probs.append(prob.astype(BF16))
            slopes.append(slope)
            dqs.append((i, dot(slope, k, TN)))
        q = jnp.concatenate([q_all[i] for i, _ in chosen], axis=0)
        g = jnp.concatenate([g_all[i] for i, _ in chosen], axis=0)
        dv = dot(jnp.concatenate(probs, axis=1), g, NN)
        dk = dot(jnp.concatenate(slopes, axis=1), q, NN)
        return dv, dk, dqs

    def add(j, found):
        dv, dk, dqs = found
        dv_all[j] += dv
        dk_all[j] += dk
        for i, dq in dqs:
            dq_all[i] += dq

    def pair(step, carry):
        both = [(step * PAIR + p, terms(step * PAIR + p, 0)) for p in range(PAIR)]
        for j, found in both:
            add(j, found)
        return carry

    lax.fori_loop(0, own // PAIR, pair, 0)

    def rest(j, carry):
        def group(step, carry):
            add(j, terms(j, step * KEY_GROUP))
            return carry

        return lax.fori_loop(1, rounds(n_key[j], KEY_GROUP), group, carry)

    lax.fori_loop(0, own, rest, 0)

    for s, out in enumerate(kv_outs):
        for r in range(nz):
            out[0, ids[0] ^ r] = (scale * dk_all[s * nz + r]).astype(BF16)
            out[1, ids[0] ^ r] = dv_all[s * nz + r].astype(BF16)
    for t in range(nb):

        def drain(m, carry, t=t):
            dq_outs[t][m] = scale * dq_all[t * own + m]
            return carry

        lax.fori_loop(0, own, drain, 0)


def grads(plan, by_key, n_key, ids, queries, out_grads, lses, keys, values):
    nb, na, own, rows, total = plan.nb, plan.na, plan.own, plan.rows, plan.total
    hd = HEAD_DIM
    outs = pl.pallas_call(
        functools.partial(grads_kernel, plan),
        out_shape=[sds((2, plan.nz, rows, hd), BF16)] * na + [sds((own, rows, hd), F32)] * nb,
        in_specs=[SMEM] * 3 + [VMEM] * (3 * nb + 2),
        out_specs=[VMEM] * (na + nb),
        scratch_shapes=[
            pltpu.VMEM((total, rows, hd), BF16),
            pltpu.VMEM((total, rows, hd), BF16),
            pltpu.VMEM((total, rows), F32),
            pltpu.VMEM((total, rows), F32),
            pltpu.VMEM((total, rows, hd), F32),
            pltpu.VMEM((own, rows, hd), F32),
            pltpu.VMEM((own, rows, hd), F32),
        ],
        cost_estimate=lasts(15),
        compiler_params=within(*[keys] * (2 + 4 * nb + 2 * nb + 4 * nb + 2 + 4)),
        name="grads",
    )(by_key, n_key, ids, *queries, *out_grads, *lses, keys, values)
    return outs[:na], outs[na:]


def pack_kernel(plan, ids, *refs):
    nb, nz = plan.nb, plan.nz
    for s, out in enumerate(refs[nb:]):
        for r in range(nz):
            total = sum(ref[s * nz + r] for ref in refs[:nb])
            out[ids[0] ^ r] = total.astype(BF16)


def pack(plan, ids, partials):
    return pl.pallas_call(
        functools.partial(pack_kernel, plan),
        out_shape=[sds((plan.nz, plan.rows, HEAD_DIM), BF16)] * plan.na,
        in_specs=[SMEM] + [VMEM] * plan.nb,
        out_specs=[VMEM] * plan.na,
        cost_estimate=lasts(2),
        compiler_params=within(*partials, *partials),
        name="pack",
    )(ids, *partials)


def assemble_kernel(plan, n, ids, *refs):
    na, nz, rows, hd = plan.na, plan.nz, plan.rows, HEAD_DIM
    for s in range(na):
        cols = pl.ds(pl.multiple_of((ids[1] ^ s) * hd, hd), hd)
        for w in range(n):
            for r in range(nz):
                refs[na + w][r * rows : (r + 1) * rows, cols] = refs[s][w, r]


def assemble(plan, ids, pieces):
    n = pieces[0].shape[0]
    return pl.pallas_call(
        functools.partial(assemble_kernel, plan, n),
        out_shape=[sds((plan.nz * plan.rows, plan.na * HEAD_DIM), BF16)] * n,
        in_specs=[SMEM] + [VMEM] * plan.na,
        out_specs=[VMEM] * n,
        cost_estimate=lasts(2),
        compiler_params=within(*pieces, *pieces),
        name="assemble",
    )(ids, *pieces)


def local(queries, key_states, value_states, attn_out, grad_out, frame_order, block_live):
    plan = Plan(queries.shape[0])
    nz, na, nb = plan.nz, plan.na, plan.nb
    slot = lax.axis_index("frame")
    ids = jnp.stack([lax.axis_index("head"), slot // nb, slot % nb]).astype(jnp.int32)

    def staged(order, pieces, send):
        moved = {}
        for step in order:
            moved[step] = send(pieces[step], step)
        return [pieces[0]] + [moved[step] for step in range(1, len(pieces))]

    def head_stage(pieces):
        return staged([*range(2, nz), 1], pieces, over_head)

    def frame_stage(pieces):
        return staged(range(na - 1, 0, -1), pieces, lambda x, s: over_frame(x, s * nb))

    def swapped(parts):
        return staged(range(1, nb), parts, over_frame)

    def regroup(pieces):
        return [jnp.concatenate([p[i : i + 1] for p in pieces]) for i in range(pieces[0].shape[0])]

    def flat_frames_first(by_frame):
        return jnp.concatenate(by_frame)

    def flat_heads_first(by_head):
        return jnp.concatenate([p[s : s + 1] for s in range(na) for p in by_head])

    q_sent = head_stage(prep(plan, ids, queries, True))
    k_near = frame_stage(prep(plan, ids, key_states, False))
    g_near = frame_stage(prep_grad(plan, ids, grad_out, attn_out))
    v_near = frame_stage(prep(plan, ids, value_states, False))
    by_key, n_key, by_query, n_query = lists(plan, ids, frame_order, block_live)
    keys = flat_heads_first(head_stage(regroup(k_near)))
    q_own = flat_frames_first(frame_stage(regroup(q_sent)))
    q_all = swapped([q_own] * nb)
    g_own = flat_heads_first(head_stage(regroup(g_near)))
    g_all = swapped([g_own] * nb)
    values = flat_heads_first(head_stage(regroup(v_near)))

    lse_own = totals(plan, by_query, n_query, keys, q_all)
    lses = swapped([lse_own] * nb)
    kv_sent, dq_parts = grads(plan, by_key, n_key, ids, q_all, g_all, lses, keys, values)
    dq_parts = swapped(dq_parts)
    kv_home = frame_stage(kv_sent)
    dq_home = frame_stage(pack(plan, ids, dq_parts))
    grad_key, grad_value = assemble(plan, ids, kv_home)
    (grad_query,) = assemble(plan, ids, [p[None] for p in dq_home])
    return grad_query, grad_key, grad_value


def solution(mesh):
    rows = P(("frame", "head"), None)
    in_specs = (rows,) * 5 + (P(), P())
    out_specs = (P("frame", "head"),) * 3
    return jax.shard_map(local, mesh=mesh, in_specs=in_specs, out_specs=out_specs, check_vma=False)
```

```python
import functools
import math

import jax
import jax.numpy as jnp
from jax import lax
from jax.experimental import pallas as pl
from jax.experimental.pallas import tpu as pltpu
from jax.sharding import PartitionSpec as P


HEADS = 16
HEAD_DIM = 128
NEG = -1e30
KEY_GROUP = 6
QUERY_GROUP = 4
TOGETHER = 2
EXTRA = 8


VMEM = pl.BlockSpec(memory_space=pltpu.VMEM)
SMEM = pl.BlockSpec(memory_space=pltpu.SMEM)
F32 = jnp.float32
BF16 = jnp.bfloat16
NT = (((1,), (1,)), ((), ()))
TN = (((0,), (0,)), ((), ()))
NN = (((1,), (0,)), ((), ()))


def dot(a, b, dims):
    return lax.dot_general(a, b, dims, preferred_element_type=F32)


def sds(shape, dtype):
    return jax.ShapeDtypeStruct(shape, dtype)


def lasts(microseconds):
    return pl.CostEstimate(flops=0, bytes_accessed=int(microseconds * 3.5e6), transcendentals=0)


def within(*shapes):
    held = sum(math.prod(s.shape) * s.dtype.itemsize for s in shapes)
    return pltpu.CompilerParams(vmem_limit_bytes=int(held * 5 // 4) + (6 << 20))


class Plan:
    def __init__(self, rows):
        self.nz = lax.axis_size("head")
        self.nf = lax.axis_size("frame")
        self.hh = HEADS // self.nz
        self.na = min(self.hh, self.nf)
        self.nb = self.nf // self.na
        self.rows = rows
        self.own = self.na * self.nz
        self.total = self.own * self.nb
        assert self.hh == self.na and rows == HEAD_DIM


def over_head(value, step):
    count = lax.axis_size("head")
    return lax.ppermute(value, "head", [(i, i ^ step) for i in range(count)])


def over_frame(value, step):
    count = lax.axis_size("frame")
    return lax.ppermute(value, "frame", [(i, i ^ step) for i in range(count)])


def prep_kernel(plan, head_first, ids, x_ref, *outs):
    hd = HEAD_DIM
    z, a = ids[0], ids[1]
    for p, out in enumerate(outs):
        for c in range(out.shape[0]):
            r, s = (p, c) if head_first else (c, p)
            head = (z ^ r) * plan.hh + (a ^ s)
            out[c] = x_ref[:, pl.ds(pl.multiple_of(head * hd, hd), hd)]


def prep(plan, ids, x, head_first):
    pieces, chunk = (plan.nz, plan.na) if head_first else (plan.na, plan.nz)
    return pl.pallas_call(
        functools.partial(prep_kernel, plan, head_first),
        out_shape=[sds((chunk, plan.rows, HEAD_DIM), BF16)] * pieces,
        in_specs=[SMEM, VMEM],
        out_specs=[VMEM] * pieces,
        cost_estimate=lasts(2),
        compiler_params=within(x, x),
    )(ids, x)


def prep_grad_kernel(plan, ids, g_ref, o_ref, *outs):
    hd, rows = HEAD_DIM, plan.rows
    z, a = ids[0], ids[1]
    ones = jnp.ones((EXTRA, hd), BF16)
    row = lax.broadcasted_iota(jnp.int32, (EXTRA, rows), 0)
    for s, out in enumerate(outs):
        for r in range(plan.nz):
            head = (z ^ r) * plan.hh + (a ^ s)
            cols = pl.ds(pl.multiple_of(head * hd, hd), hd)
            grad = g_ref[:, cols]
            out[r, :rows] = grad
            product = grad.astype(F32) * o_ref[:, cols].astype(F32)
            high = product.astype(BF16)
            low = (product - high.astype(F32)).astype(BF16)
            delta = dot(ones, high, NT) + dot(ones, low, NT)
            first = delta.astype(BF16)
            rest = delta - first.astype(F32)
            second = rest.astype(BF16)
            third = (rest - second.astype(F32)).astype(BF16)
            parts = jnp.where(
                row == 0,
                first.astype(F32),
                jnp.where(row == 1, second.astype(F32), jnp.where(row == 2, third.astype(F32), 0.0)),
            )
            out[r, rows:] = parts.astype(BF16)


def prep_grad(plan, ids, g, o):
    return pl.pallas_call(
        functools.partial(prep_grad_kernel, plan),
        out_shape=[sds((plan.nz, plan.rows + EXTRA, HEAD_DIM), BF16)] * plan.na,
        in_specs=[SMEM, VMEM, VMEM],
        out_specs=[VMEM] * plan.na,
        cost_estimate=lasts(2.5),
        compiler_params=within(g, o, g),
        name="prep_grad",
    )(ids, g, o)


def lists_kernel(plan, ids, order, live_ref, by_key, n_key, by_query, n_query, key_of, query_of, numbers):
    nz, na, nb, nf = plan.nz, plan.na, plan.nb, plan.nf
    z, a, b = ids[0], ids[1], ids[2]
    true = [z ^ r for r in range(nz)]

    def at_distance(d, carry):
        seen = [jnp.int32(0)] * nz
        for r in range(nz):
            count = jnp.int32(0)
            for rk in range(nz):
                live = (live_ref[d, true[r], true[rk]] > 0).astype(jnp.int32)
                key_of[d * nz + r, count] = jnp.int32(rk)
                query_of[d * nz + rk, seen[rk]] = jnp.int32(r)
                count = count + live
                seen[rk] = seen[rk] + live
            numbers[0, d * nz + r] = count
        for rk in range(nz):
            numbers[1, d * nz + rk] = seen[rk]
        return carry

    lax.fori_loop(0, nf, at_distance, 0)

    def clear(i, carry):
        n_query[i] = 0
        return carry

    lax.fori_loop(0, plan.total, clear, 0)

    def key_frame(s_key, carry):
        place_key = order[(a ^ s_key) * nb + b]

        def query_frame(ts, counts):
            t = ts // na
            place = order[(a ^ (ts - t * na)) * nb + (b ^ t)]
            d = jnp.abs(place - place_key)

            def found(counts):
                counts = list(counts)
                for r in range(nz):
                    i, row = ts * nz + r, d * nz + r
                    seen = n_query[i]
                    for u in range(nz):
                        by_query[i, seen + u] = s_key * nz + key_of[row, u]
                    n_query[i] = seen + numbers[0, row]
                for rk in range(nz):
                    row = d * nz + rk
                    for u in range(nz):
                        by_key[s_key * nz + rk, counts[rk] + u] = ts * nz + query_of[row, u]
                    counts[rk] = counts[rk] + numbers[1, row]
                return tuple(counts)

            return lax.cond(ts != s_key, found, lambda counts: counts, counts)

        counts = lax.fori_loop(0, na * nb, query_frame, (jnp.int32(0),) * nz)
        for rk in range(nz):
            n_key[s_key * nz + rk] = counts[rk]
        return carry

    lax.fori_loop(0, na, key_frame, 0)


def lists(plan, ids, order, live):
    own, total, nz, nf = plan.own, plan.total, plan.nz, plan.nf
    return pl.pallas_call(
        functools.partial(lists_kernel, plan),
        out_shape=[
            sds((own, total + KEY_GROUP + nz), jnp.int32),
            sds((own,), jnp.int32),
            sds((total, own + QUERY_GROUP + nz), jnp.int32),
            sds((total,), jnp.int32),
        ],
        in_specs=[SMEM] * 3,
        out_specs=[SMEM] * 4,
        scratch_shapes=[
            pltpu.SMEM((nf * nz, nz), jnp.int32),
            pltpu.SMEM((nf * nz, nz), jnp.int32),
            pltpu.SMEM((2, nf * nz), jnp.int32),
        ],
        cost_estimate=lasts(3),
        compiler_params=within(),
        name="lists",
    )(ids, order, live)


def picks(table, row, count, first, size):
    out = []
    for u in range(size):
        valid = first + u < count
        out.append((jnp.where(valid, table[row, first + u], 0), valid))
    return out


def totals_kernel(plan, by_query, n_query, k_ref, q_ref, out, peaks, sums):
    nz, na, nb, own, rows = plan.nz, plan.na, plan.nb, plan.own, plan.rows
    scale = HEAD_DIM**-0.5
    length = nz * rows

    def scores_of(i, first):
        chosen = picks(by_query, i, n_query[i], first, QUERY_GROUP)
        keys = jnp.concatenate([k_ref[j] for j, _ in chosen], axis=0)
        scores = scale * dot(keys, q_ref[i], NT)
        return [
            jnp.where(valid, scores[u * rows : (u + 1) * rows], NEG)
            for u, (_, valid) in enumerate(chosen)
        ]

    def near(s, carry):
        span = pl.ds(s * nz, nz)
        keys, q = k_ref[span].reshape(length, HEAD_DIM), q_ref[span].reshape(length, HEAD_DIM)
        scores = scale * dot(keys, q, NT)
        peak = jnp.max(scores, axis=0, keepdims=True)
        mass = jnp.sum(jnp.exp(scores - peak), axis=0, keepdims=True)
        for r in range(nz):
            peaks[pl.ds(s * nz + r, 1), :] = peak[:, r * rows : (r + 1) * rows]
            sums[pl.ds(s * nz + r, 1), :] = mass[:, r * rows : (r + 1) * rows]
        return carry

    lax.fori_loop(0, na, near, 0)
    if nb > 1:
        peaks[own:, :] = jnp.full((plan.total - own, rows), NEG, F32)
        sums[own:, :] = jnp.zeros((plan.total - own, rows), F32)

    def merged(i, parts):
        row = pl.ds(i, 1)
        old = peaks[row, :]
        peak = jnp.maximum(old, jnp.max(functools.reduce(jnp.maximum, parts), axis=0, keepdims=True))
        mass = functools.reduce(jnp.add, [jnp.exp(part - peak) for part in parts])
        fresh = sums[row, :] * jnp.exp(old - peak) + jnp.sum(mass, axis=0, keepdims=True)
        return peak, fresh

    def keep(i, found):
        peaks[pl.ds(i, 1), :], sums[pl.ds(i, 1), :] = found

    def away(m, carry):
        found = [(m * TOGETHER + u, merged(m * TOGETHER + u, scores_of(m * TOGETHER + u, 0))) for u in range(TOGETHER)]
        for i, each in found:
            keep(i, each)
        return carry

    lax.fori_loop(0, plan.total // TOGETHER, away, 0)

    def rest(i, carry):
        def group(step, carry):
            keep(i, merged(i, scores_of(i, step * QUERY_GROUP)))
            return carry

        return lax.fori_loop(1, lax.div(n_query[i] + (QUERY_GROUP - 1), QUERY_GROUP), group, carry)

    lax.fori_loop(0, plan.total, rest, 0)
    peak = peaks[...]
    out[...] = jnp.where(peak > 0.5 * NEG, peak + jnp.log(sums[...]), NEG)


def totals(plan, by_query, n_query, keys, queries):
    return pl.pallas_call(
        functools.partial(totals_kernel, plan),
        out_shape=sds((plan.total, plan.rows), F32),
        in_specs=[SMEM, SMEM, VMEM, VMEM],
        out_specs=VMEM,
        scratch_shapes=[pltpu.VMEM((plan.total, plan.rows), F32)] * 2,
        cost_estimate=lasts(7),
        compiler_params=within(keys, queries),
        name="totals",
    )(by_query, n_query, keys, queries)


def rows_kernel(plan, g_ref, *refs):
    nb, own, rows = plan.nb, plan.own, plan.rows
    parts, lse_all, delta_all = refs[:nb], refs[nb], refs[nb + 1]
    for t in range(nb):
        rivals = [parts[u][pl.ds((t ^ u) * own, own), :] for u in range(nb)]
        peak = functools.reduce(jnp.maximum, rivals)
        lse_all[pl.ds(t * own, own), :] = peak + jnp.log(sum(jnp.exp(x - peak) for x in rivals))

    def fill(i, carry):
        delta_all[pl.ds(i, 1), :] = jnp.sum(g_ref[i, rows:].astype(F32), axis=0, keepdims=True)
        return carry

    lax.fori_loop(0, plan.total, fill, 0)


def query_rows(plan, out_grads, parts):
    return pl.pallas_call(
        functools.partial(rows_kernel, plan),
        out_shape=[sds((plan.total, plan.rows), F32)] * 2,
        in_specs=[VMEM] * (1 + plan.nb),
        out_specs=[VMEM] * 2,
        cost_estimate=lasts(1),
        compiler_params=within(out_grads),
        name="query_rows",
    )(out_grads, *parts)


def grads_kernel(plan, span, first, last, by_key, n_key, q_ref, g_ref, lse_ref, delta_ref, k_ref, *refs):
    nz, na, nb, own, rows = plan.nz, plan.na, plan.nb, plan.own, plan.rows
    hd = HEAD_DIM
    scale = hd**-0.5
    length = nz * rows
    width = len(span)
    refs = list(refs)
    take = lambda n: [refs.pop(0) for _ in range(n)]
    v_refs = take(width)
    if not first:
        (dq_before,) = take(1)
    kv_outs = take(na)
    dq_outs = take(nb if last else 1)
    dk_all, dv_all = take(2)
    dq_all = refs.pop(0) if last else dq_outs[0]

    def begin(i, carry):
        dq_all[i] = jnp.zeros((rows, hd), F32) if first else dq_before[i]
        return carry

    lax.fori_loop(own if first else 0, plan.total, begin, 0)

    def wide_row(ref, start):
        return jnp.concatenate([ref[pl.ds(start + r, 1), :] for r in range(nz)], axis=1)

    def diagonal(s, carry):
        frame = pl.ds(s * nz, nz)
        k = jnp.concatenate([k_ref[s * nz + r] for r in span], axis=0)
        v = jnp.concatenate([v_ref[s] for v_ref in v_refs], axis=0)
        q, g = q_ref[frame].reshape(length, hd), g_ref[frame, :rows].reshape(length, hd)
        lse, delta = wide_row(lse_ref, s * nz), wide_row(delta_ref, s * nz)
        probs = jnp.exp(scale * dot(k, q, NT) - lse)
        dv = dot(probs.astype(BF16), g, NN)
        grad_scores = (probs * (dot(v, g, NT) - delta)).astype(BF16)
        dk = dot(grad_scores, q, NN)
        dq = dot(grad_scores, k, TN).reshape(nz, rows, hd)
        for x in range(width):
            dv_all[s * width + x] = dv[x * rows : (x + 1) * rows]
            dk_all[s * width + x] = dk[x * rows : (x + 1) * rows]
        if first:
            dq_all[frame] = dq
        else:
            dq_all[frame] += dq
        return carry

    lax.fori_loop(0, na, diagonal, 0)

    def add(s, x, j, start, size):
        k, v = k_ref[j], v_refs[x][s]
        chosen = picks(by_key, j, n_key[j], start, size)
        q = jnp.concatenate([q_ref[i] for i, _ in chosen], axis=0)
        g = jnp.concatenate([g_ref[i, :rows] for i, _ in chosen], axis=0)
        lse = jnp.concatenate([jnp.where(ok, lse_ref[pl.ds(i, 1), :], -NEG) for i, ok in chosen], axis=1)
        delta = jnp.concatenate([delta_ref[pl.ds(i, 1), :] for i, _ in chosen], axis=1)
        probs = jnp.exp(scale * dot(k, q, NT) - lse)
        dv_all[s * width + x] += dot(probs.astype(BF16), g, NN)
        grad_scores = (probs * (dot(v, g, NT) - delta)).astype(BF16)
        dk_all[s * width + x] += dot(grad_scores, q, NN)
        dq = dot(grad_scores, k, TN)
        for u, (i, _) in enumerate(chosen):
            dq_all[i] += dq[u * rows : (u + 1) * rows]

    def away(s, carry):
        for x, r in enumerate(span):
            j = s * nz + r
            count = n_key[j]
            full = lax.div(count, KEY_GROUP)

            def group(step, carry, x=x, j=j):
                add(s, x, j, step * KEY_GROUP, KEY_GROUP)
                return carry

            lax.fori_loop(0, full, group, 0)
            left = count - full * KEY_GROUP
            for size in range(2, KEY_GROUP + 1, 2):

                @pl.when((left > size - 2) & (left <= size))
                def _(x=x, j=j, full=full, size=size):
                    add(s, x, j, full * KEY_GROUP, size)

        return carry

    lax.fori_loop(0, na, away, 0)

    for s, out in enumerate(kv_outs):
        for x in range(width):
            out[0, x] = (scale * dk_all[s * width + x]).astype(BF16)
            out[1, x] = dv_all[s * width + x].astype(BF16)
    if last:
        for t in range(nb):

            def drain(m, carry, t=t):
                dq_outs[t][m] = scale * dq_all[t * own + m]
                return carry

            lax.fori_loop(0, own, drain, 0)


def grads(plan, span, tables, queries, out_grads, lse, delta, keys, values, dq_before, last):
    nb, na, own, rows, total = plan.nb, plan.na, plan.own, plan.rows, plan.total
    hd, width, first = HEAD_DIM, len(span), dq_before is None
    kv = [sds((2, width, rows, hd), BF16)] * na
    dq = [sds((own, rows, hd), F32)] * nb if last else [sds((total, rows, hd), F32)]
    before = [] if first else [dq_before]
    partial = sds((own, rows, hd), F32)
    outs = pl.pallas_call(
        functools.partial(grads_kernel, plan, span, first, last),
        out_shape=kv + dq,
        in_specs=[SMEM] * 2 + [VMEM] * (5 + width + len(before)),
        out_specs=[VMEM] * (na + len(dq)),
        scratch_shapes=[pltpu.VMEM((na * width, rows, hd), F32)] * 2
        + ([pltpu.VMEM((total, rows, hd), F32)] if last else []),
        cost_estimate=lasts(7),
        compiler_params=within(queries, out_grads, keys, keys, *[partial] * (4 + 3 * nb)),
    )(*tables, queries, out_grads, lse, delta, keys, *values, *before)
    return outs[:na], outs[na:]


def pack_kernel(plan, *refs):
    nb, nz = plan.nb, plan.nz
    for s, out in enumerate(refs[nb:]):
        for r in range(nz):
            out[0, r] = sum(ref[s * nz + r] for ref in refs[:nb]).astype(BF16)


def pack(plan, partials):
    return pl.pallas_call(
        functools.partial(pack_kernel, plan),
        out_shape=[sds((1, plan.nz, plan.rows, HEAD_DIM), BF16)] * plan.na,
        in_specs=[VMEM] * plan.nb,
        out_specs=[VMEM] * plan.na,
        cost_estimate=lasts(1),
        compiler_params=within(*partials, *partials),
        name="pack",
    )(*partials)


def assemble_kernel(plan, spans, n, ids, *refs):
    na, rows, hd = plan.na, plan.rows, HEAD_DIM
    refs = list(refs)
    outs = refs[na * len(spans) :]
    for span in spans:
        for s in range(na):
            piece = refs.pop(0)
            cols = pl.ds(pl.multiple_of((ids[1] ^ s) * hd, hd), hd)
            for w in range(n):
                for x, r in enumerate(span):
                    place = pl.ds(pl.multiple_of((ids[0] ^ r) * rows, rows), rows)
                    outs[w][place, cols] = piece[w, x]


def assemble(plan, ids, spans, groups):
    n = groups[0][0].shape[0]
    pieces = [piece for group in groups for piece in group]
    return pl.pallas_call(
        functools.partial(assemble_kernel, plan, spans, n),
        out_shape=[sds((plan.nz * plan.rows, plan.na * HEAD_DIM), BF16)] * n,
        in_specs=[SMEM] + [VMEM] * len(pieces),
        out_specs=[VMEM] * n,
        cost_estimate=lasts(1.5),
        compiler_params=within(*pieces, *pieces),
    )(ids, *pieces)


def local(queries, key_states, value_states, attn_out, grad_out, frame_order, block_live):
    plan = Plan(queries.shape[0])
    nz, na, nb = plan.nz, plan.na, plan.nb
    slot = lax.axis_index("frame")
    ids = jnp.stack([lax.axis_index("head"), slot // nb, slot % nb]).astype(jnp.int32)

    def staged(order, pieces, send):
        moved = {}
        for step in order:
            moved[step] = send(pieces[step], step)
        return [pieces[0]] + [moved[step] for step in range(1, len(pieces))]

    def head_stage(pieces):
        return staged([*range(2, nz), 1], pieces, over_head)

    def frame_stage(pieces):
        return staged(range(na - 1, 0, -1), pieces, lambda x, s: over_frame(x, s * nb))

    def swapped(parts):
        return staged(range(1, nb), parts, over_frame)

    def regroup(pieces):
        return [jnp.concatenate([p[i : i + 1] for p in pieces]) for i in range(pieces[0].shape[0])]

    def flat_frames_first(by_frame):
        return jnp.concatenate(by_frame)

    def flat_heads_first(by_head):
        return jnp.concatenate([p[s : s + 1] for s in range(na) for p in by_head])

    q_sent = head_stage(prep(plan, ids, queries, True))
    k_near = frame_stage(prep(plan, ids, key_states, False))
    g_near = frame_stage(prep_grad(plan, ids, grad_out, attn_out))
    v_near = frame_stage(prep(plan, ids, value_states, False))
    by_key, n_key, by_query, n_query = lists(plan, ids, frame_order, block_live)
    keys = flat_heads_first(head_stage(regroup(k_near)))
    q_own = flat_frames_first(frame_stage(regroup(q_sent)))
    q_all = jnp.concatenate(swapped([q_own] * nb))
    g_own = flat_heads_first(head_stage(regroup(g_near)))
    g_all = jnp.concatenate(swapped([g_own] * nb))
    values = head_stage(regroup(v_near))

    lse_part = totals(plan, by_query, n_query, keys, q_all)
    lse, delta = query_rows(plan, g_all, swapped([lse_part] * nb))
    spans = [range(0, 2), range(2, nz)]
    kv_home, dq = [], None
    for place, span in enumerate(spans):
        last = place == len(spans) - 1
        kv, dq_parts = grads(
            plan, span, (by_key, n_key), q_all, g_all, lse, delta, keys,
            [values[r] for r in span], dq, last,
        )
        dq = dq_parts[0]
        kv_home.append(frame_stage(kv))
    dq_home = frame_stage(pack(plan, swapped(dq_parts)))
    grad_key, grad_value = assemble(plan, ids, spans, kv_home)
    (grad_query,) = assemble(plan, ids, [range(nz)], [dq_home])
    return grad_query, grad_key, grad_value


def solution(mesh):
    rows = P(("frame", "head"), None)
    in_specs = (rows,) * 5 + (P(), P())
    out_specs = (P("frame", "head"),) * 3
    return jax.shard_map(local, mesh=mesh, in_specs=in_specs, out_specs=out_specs, check_vma=False)
```

```python
import functools
import math

import jax
import jax.numpy as jnp
from jax import lax
from jax.experimental import pallas as pl
from jax.experimental.pallas import tpu as pltpu
from jax.sharding import PartitionSpec as P


HEADS = 16
HEAD_DIM = 128
NEG = -1e30
KEY_GROUP = 6
REACH = 4
EXTRA = 8


VMEM = pl.BlockSpec(memory_space=pltpu.VMEM)
SMEM = pl.BlockSpec(memory_space=pltpu.SMEM)
F32 = jnp.float32
BF16 = jnp.bfloat16
NT = (((1,), (1,)), ((), ()))
TN = (((0,), (0,)), ((), ()))
NN = (((1,), (0,)), ((), ()))


def dot(a, b, dims):
    return lax.dot_general(a, b, dims, preferred_element_type=F32)


def sds(shape, dtype):
    return jax.ShapeDtypeStruct(shape, dtype)


def lasts(microseconds):
    return pl.CostEstimate(flops=0, bytes_accessed=int(microseconds * 3.5e6), transcendentals=0)


def within(*shapes):
    held = sum(math.prod(s.shape) * s.dtype.itemsize for s in shapes)
    return pltpu.CompilerParams(vmem_limit_bytes=int(held * 5 // 4) + (6 << 20))


class Plan:
    def __init__(self, rows):
        self.nz = lax.axis_size("head")
        self.nf = lax.axis_size("frame")
        self.hh = HEADS // self.nz
        self.na = min(self.hh, self.nf)
        self.nb = self.nf // self.na
        self.rows = rows
        self.own = self.na * self.nz
        self.total = self.own * self.nb
        assert self.hh == self.na and rows == HEAD_DIM


def over_head(value, step):
    count = lax.axis_size("head")
    return lax.ppermute(value, "head", [(i, i ^ step) for i in range(count)])


def over_frame(value, step):
    count = lax.axis_size("frame")
    return lax.ppermute(value, "frame", [(i, i ^ step) for i in range(count)])


def columns(plan, ids, r, s):
    head = (ids[0] ^ r) * plan.hh + (ids[1] ^ s)
    return pl.ds(pl.multiple_of(head * HEAD_DIM, HEAD_DIM), HEAD_DIM)


def prep_query_kernel(plan, ids, x_ref, *refs):
    outs, sems = refs[:-1], refs[-1]
    copies = [
        pltpu.make_async_copy(x_ref.at[:, columns(plan, ids, r, s)], outs[r].at[s], sems.at[r, s])
        for r in range(plan.nz)
        for s in range(plan.na)
    ]
    for copy in copies:
        copy.start()
    for copy in copies:
        copy.wait()


def prep_query(plan, ids, x):
    return pl.pallas_call(
        functools.partial(prep_query_kernel, plan),
        out_shape=[sds((plan.na, plan.rows, HEAD_DIM), BF16)] * plan.nz,
        in_specs=[SMEM, pl.BlockSpec(memory_space=pl.ANY)],
        out_specs=[VMEM] * plan.nz,
        scratch_shapes=[pltpu.SemaphoreType.DMA((plan.nz, plan.na))],
        cost_estimate=lasts(1),
        compiler_params=within(x, x),
        name="prep_q",
    )(ids, x)


def prep_rest_kernel(plan, ids, k_ref, g_ref, o_ref, v_ref, *refs):
    nz, na, rows = plan.nz, plan.na, plan.rows
    k_outs, gv_outs, (o_all, sems, o_sem) = refs[:na], refs[na : 2 * na], refs[2 * na :]
    spots = [(s, r) for s in range(na) for r in range(nz)]
    behind = pl.ds(rows + EXTRA, rows)

    def copy(which, ref, out, s, r):
        return pltpu.make_async_copy(ref.at[:, columns(plan, ids, r, s)], out, sems.at[which, s, r])

    k_copies = [copy(0, k_ref, k_outs[s].at[r], s, r) for s, r in spots]
    g_copies = [copy(1, g_ref, gv_outs[s].at[r, pl.ds(0, rows)], s, r) for s, r in spots]
    v_copies = [copy(2, v_ref, gv_outs[s].at[r, behind], s, r) for s, r in spots]
    o_copy = pltpu.make_async_copy(o_ref, o_all, o_sem)
    for each in k_copies:
        each.start()
    o_copy.start()
    for each in g_copies + v_copies:
        each.start()
    ones = jnp.ones((EXTRA, HEAD_DIM), BF16)
    row = lax.broadcasted_iota(jnp.int32, (EXTRA, rows), 0)
    for each in k_copies:
        each.wait()
    o_copy.wait()
    for (s, r), each in zip(spots, g_copies):
        each.wait()
        grad = gv_outs[s][r, :rows]
        product = grad.astype(F32) * o_all[:, columns(plan, ids, r, s)].astype(F32)
        high = product.astype(BF16)
        low = (product - high.astype(F32)).astype(BF16)
        delta = dot(ones, high, NT) + dot(ones, low, NT)
        first = delta.astype(BF16).astype(F32)
        rest = delta - first
        second = rest.astype(BF16).astype(F32)
        parts = jnp.where(row == 2, rest - second, 0.0)
        parts = jnp.where(row == 0, first, jnp.where(row == 1, second, parts))
        gv_outs[s][r, rows : rows + EXTRA] = parts.astype(BF16)
    for each in v_copies:
        each.wait()


def prep_rest(plan, ids, k, g, o, v):
    outs = pl.pallas_call(
        functools.partial(prep_rest_kernel, plan),
        out_shape=[sds((plan.nz, plan.rows, HEAD_DIM), BF16)] * plan.na
        + [sds((plan.nz, 2 * plan.rows + EXTRA, HEAD_DIM), BF16)] * plan.na,
        in_specs=[SMEM] + [pl.BlockSpec(memory_space=pl.ANY)] * 4,
        out_specs=[VMEM] * (2 * plan.na),
        scratch_shapes=[
            pltpu.VMEM(o.shape, BF16),
            pltpu.SemaphoreType.DMA((3, plan.na, plan.nz)),
            pltpu.SemaphoreType.DMA,
        ],
        cost_estimate=lasts(2.5),
        compiler_params=within(k, g, o, v),
        name="prep_rest",
    )(ids, k, g, o, v)
    return outs[: plan.na], outs[plan.na :]


def lists_kernel(plan, ids, order, live_ref, by_key, n_key, query_of, numbers):
    nz, na, nb = plan.nz, plan.na, plan.nb
    z, a, b = ids[0], ids[1], ids[2]
    true = [z ^ r for r in range(nz)]

    def at_distance(d, carry):
        for rk in range(nz):
            count = jnp.int32(0)
            for r in range(nz):
                query_of[d * nz + rk, count] = jnp.int32(r)
                count = count + (live_ref[d, true[r], true[rk]] > 0).astype(jnp.int32)
            numbers[d * nz + rk] = count
        return carry

    lax.fori_loop(1, REACH, at_distance, 0)

    def key_frame(s_key, carry):
        place_key = order[(a ^ s_key) * nb + b]

        def query_frame(ts, counts):
            t = ts // na
            place = order[(a ^ (ts - t * na)) * nb + (b ^ t)]
            d = jnp.abs(place - place_key)

            def found(counts):
                counts = list(counts)
                for rk in range(nz):
                    row = d * nz + rk
                    for u in range(nz):
                        by_key[s_key * nz + rk, counts[rk] + u] = ts * nz + query_of[row, u]
                    counts[rk] = counts[rk] + numbers[row]
                return tuple(counts)

            return lax.cond((d > 0) & (d < REACH), found, lambda counts: counts, counts)

        counts = lax.fori_loop(0, na * nb, query_frame, (jnp.int32(0),) * nz)
        for rk in range(nz):
            n_key[s_key * nz + rk] = counts[rk]
        return carry

    lax.fori_loop(0, na, key_frame, 0)


def lists(plan, ids, order, live):
    own, total, nz = plan.own, plan.total, plan.nz
    return pl.pallas_call(
        functools.partial(lists_kernel, plan),
        out_shape=[sds((own, total + KEY_GROUP + nz), jnp.int32), sds((own,), jnp.int32)],
        in_specs=[SMEM] * 3,
        out_specs=[SMEM] * 2,
        scratch_shapes=[
            pltpu.SMEM((REACH * nz, nz), jnp.int32),
            pltpu.SMEM((REACH * nz,), jnp.int32),
        ],
        cost_estimate=lasts(3),
        compiler_params=within(),
        name="lists",
    )(ids, order, live)


def picks(table, row, count, first, size):
    out = []
    for u in range(size):
        valid = first + u < count
        out.append((jnp.where(valid, table[row, first + u], 0), valid))
    return out


def in_groups(count, visit):
    full = lax.div(count, KEY_GROUP)

    def group(step, carry):
        visit(step * KEY_GROUP, KEY_GROUP)
        return carry

    lax.fori_loop(0, full, group, 0)
    left = count - full * KEY_GROUP
    for size in range(2, KEY_GROUP + 1, 2):

        @pl.when((left > size - 2) & (left <= size))
        def _(size=size):
            visit(full * KEY_GROUP, size)


def totals_kernel(plan, by_key, n_key, k_ref, q_ref, out, peaks, sums):
    nz, na, own, rows, total = plan.nz, plan.na, plan.own, plan.rows, plan.total
    scale = HEAD_DIM**-0.5
    length = nz * rows
    peaks[own:, :] = jnp.full((peaks.shape[0] - own, rows), NEG, F32)
    sums[own:, :] = jnp.zeros((peaks.shape[0] - own, rows), F32)

    def near(s, carry):
        span = pl.ds(s * nz, nz)
        keys, q = k_ref[span].reshape(length, HEAD_DIM), q_ref[span].reshape(length, HEAD_DIM)
        scores = scale * dot(keys, q, NT)
        peak = jnp.max(scores, axis=0, keepdims=True)
        mass = jnp.sum(jnp.exp(scores - peak), axis=0, keepdims=True)
        for r in range(nz):
            peaks[pl.ds(s * nz + r, 1), :] = peak[:, r * rows : (r + 1) * rows]
            sums[pl.ds(s * nz + r, 1), :] = mass[:, r * rows : (r + 1) * rows]
        return carry

    lax.fori_loop(0, na, near, 0)

    def away(j, carry):
        def visit(start, size):
            chosen = picks(by_key, j, n_key[j], start, size)
            places = [pl.ds(jnp.where(ok, i, total), 1) for i, ok in chosen]
            q = jnp.concatenate([q_ref[i] for i, _ in chosen], axis=0)
            scores = scale * dot(k_ref[j], q, NT)
            peak = jnp.max(scores, axis=0, keepdims=True)
            mass = jnp.sum(jnp.exp(scores - peak), axis=0, keepdims=True)
            old_peak = jnp.concatenate([peaks[place, :] for place in places], axis=1)
            old_mass = jnp.concatenate([sums[place, :] for place in places], axis=1)
            new_peak = jnp.maximum(old_peak, peak)
            new_mass = old_mass * jnp.exp(old_peak - new_peak) + mass * jnp.exp(peak - new_peak)
            for u, place in enumerate(places):
                peaks[place, :] = new_peak[:, u * rows : (u + 1) * rows]
                sums[place, :] = new_mass[:, u * rows : (u + 1) * rows]

        in_groups(n_key[j], visit)
        return carry

    lax.fori_loop(0, own, away, 0)
    peak = peaks[:total, :]
    out[...] = jnp.where(peak > 0.5 * NEG, peak + jnp.log(sums[:total, :]), NEG)


def totals(plan, by_key, n_key, keys, queries):
    return pl.pallas_call(
        functools.partial(totals_kernel, plan),
        out_shape=sds((plan.total, plan.rows), F32),
        in_specs=[SMEM, SMEM, VMEM, VMEM],
        out_specs=VMEM,
        scratch_shapes=[pltpu.VMEM((plan.total + 8, plan.rows), F32)] * 2,
        cost_estimate=lasts(6),
        compiler_params=within(keys, queries),
        name="totals",
    )(by_key, n_key, keys, queries)


def rows_kernel(plan, g_ref, *refs):
    nb, own, rows = plan.nb, plan.own, plan.rows
    parts, lse_all, delta_all = refs[:nb], refs[nb], refs[nb + 1]
    for t in range(nb):
        rivals = [parts[u][pl.ds((t ^ u) * own, own), :] for u in range(nb)]
        peak = functools.reduce(jnp.maximum, rivals)
        lse_all[pl.ds(t * own, own), :] = peak + jnp.log(sum(jnp.exp(x - peak) for x in rivals))

    def fill(i, carry):
        delta_all[pl.ds(i, 1), :] = jnp.sum(g_ref[i, rows:].astype(F32), axis=0, keepdims=True)
        return carry

    lax.fori_loop(0, plan.total, fill, 0)


def query_rows(plan, out_grads, parts):
    return pl.pallas_call(
        functools.partial(rows_kernel, plan),
        out_shape=[sds((plan.total, plan.rows), F32)] * 2,
        in_specs=[VMEM] * (1 + plan.nb),
        out_specs=[VMEM] * 2,
        cost_estimate=lasts(1),
        compiler_params=within(out_grads),
        name="query_rows",
    )(out_grads, *parts)


def grads_kernel(plan, span, first, last, by_key, n_key, q_ref, g_ref, lse_ref, delta_ref, k_ref, *refs):
    nz, na, nb, own, rows = plan.nz, plan.na, plan.nb, plan.own, plan.rows
    hd = HEAD_DIM
    scale = hd**-0.5
    length = nz * rows
    width = len(span)
    refs = list(refs)
    take = lambda n: [refs.pop(0) for _ in range(n)]
    v_refs = take(width)
    if not first:
        (dq_before,) = take(1)
    kv_outs = take(na)
    dq_outs = take(nb if last else 1)
    dk_all, dv_all = take(2)
    dq_all = refs.pop(0) if last else dq_outs[0]

    def begin(i, carry):
        dq_all[i] = jnp.zeros((rows, hd), F32) if first else dq_before[i]
        return carry

    lax.fori_loop(own if first else 0, plan.total, begin, 0)

    def wide_row(ref, start):
        return jnp.concatenate([ref[pl.ds(start + r, 1), :] for r in range(nz)], axis=1)

    def diagonal(s, carry):
        frame = pl.ds(s * nz, nz)
        k = jnp.concatenate([k_ref[s * nz + r] for r in span], axis=0)
        v = jnp.concatenate([v_ref[s] for v_ref in v_refs], axis=0)
        q, g = q_ref[frame].reshape(length, hd), g_ref[frame, :rows].reshape(length, hd)
        lse, delta = wide_row(lse_ref, s * nz), wide_row(delta_ref, s * nz)
        probs = jnp.exp(scale * dot(k, q, NT) - lse)
        dv = dot(probs.astype(BF16), g, NN)
        grad_scores = (probs * (dot(v, g, NT) - delta)).astype(BF16)
        dk = dot(grad_scores, q, NN)
        dq = dot(grad_scores, k, TN).reshape(nz, rows, hd)
        for x in range(width):
            dv_all[s * width + x] = dv[x * rows : (x + 1) * rows]
            dk_all[s * width + x] = dk[x * rows : (x + 1) * rows]
        if first:
            dq_all[frame] = dq
        else:
            dq_all[frame] += dq
        return carry

    lax.fori_loop(0, na, diagonal, 0)

    def add(s, x, j, start, size):
        k, v = k_ref[j], v_refs[x][s]
        chosen = picks(by_key, j, n_key[j], start, size)
        q = jnp.concatenate([q_ref[i] for i, _ in chosen], axis=0)
        g = jnp.concatenate([g_ref[i, :rows] for i, _ in chosen], axis=0)
        lse = jnp.concatenate([jnp.where(ok, lse_ref[pl.ds(i, 1), :], -NEG) for i, ok in chosen], axis=1)
        delta = jnp.concatenate([delta_ref[pl.ds(i, 1), :] for i, _ in chosen], axis=1)
        probs = jnp.exp(scale * dot(k, q, NT) - lse)
        dv_all[s * width + x] += dot(probs.astype(BF16), g, NN)
        grad_scores = (probs * (dot(v, g, NT) - delta)).astype(BF16)
        dk_all[s * width + x] += dot(grad_scores, q, NN)
        dq = dot(grad_scores, k, TN)
        for u, (i, _) in enumerate(chosen):
            dq_all[i] += dq[u * rows : (u + 1) * rows]

    def away(s, carry):
        for x, r in enumerate(span):
            j = s * nz + r
            in_groups(n_key[j], lambda start, size, x=x, j=j: add(s, x, j, start, size))
        return carry

    lax.fori_loop(0, na, away, 0)

    for s, out in enumerate(kv_outs):
        for x in range(width):
            out[0, x] = (scale * dk_all[s * width + x]).astype(BF16)
            out[1, x] = dv_all[s * width + x].astype(BF16)
    if last:
        for t in range(nb):

            def drain(m, carry, t=t):
                dq_outs[t][m] = scale * dq_all[t * own + m]
                return carry

            lax.fori_loop(0, own, drain, 0)


def grads(plan, span, tables, queries, out_grads, lse, delta, keys, values, dq_before, last):
    nb, na, own, rows, total = plan.nb, plan.na, plan.own, plan.rows, plan.total
    hd, width, first = HEAD_DIM, len(span), dq_before is None
    kv = [sds((2, width, rows, hd), BF16)] * na
    dq = [sds((own, rows, hd), F32)] * nb if last else [sds((total, rows, hd), F32)]
    before = [] if first else [dq_before]
    partial = sds((own, rows, hd), F32)
    outs = pl.pallas_call(
        functools.partial(grads_kernel, plan, span, first, last),
        out_shape=kv + dq,
        in_specs=[SMEM] * 2 + [VMEM] * (5 + width + len(before)),
        out_specs=[VMEM] * (na + len(dq)),
        scratch_shapes=[pltpu.VMEM((na * width, rows, hd), F32)] * 2
        + ([pltpu.VMEM((total, rows, hd), F32)] if last else []),
        cost_estimate=lasts(7),
        compiler_params=within(queries, out_grads, keys, keys, *[partial] * (4 + 3 * nb)),
    )(*tables, queries, out_grads, lse, delta, keys, *values, *before)
    return outs[:na], outs[na:]


def pack_kernel(plan, *refs):
    nb, nz = plan.nb, plan.nz
    for s, out in enumerate(refs[nb:]):
        for r in range(nz):
            out[0, r] = sum(ref[s * nz + r] for ref in refs[:nb]).astype(BF16)


def pack(plan, partials):
    return pl.pallas_call(
        functools.partial(pack_kernel, plan),
        out_shape=[sds((1, plan.nz, plan.rows, HEAD_DIM), BF16)] * plan.na,
        in_specs=[VMEM] * plan.nb,
        out_specs=[VMEM] * plan.na,
        cost_estimate=lasts(1),
        compiler_params=within(*partials, *partials),
        name="pack",
    )(*partials)


def assemble_kernel(plan, spans, n, ids, *refs):
    na, rows, hd = plan.na, plan.rows, HEAD_DIM
    refs = list(refs)
    outs = refs[na * len(spans) :]
    for span in spans:
        for s in range(na):
            piece = refs.pop(0)
            cols = pl.ds(pl.multiple_of((ids[1] ^ s) * hd, hd), hd)
            for w in range(n):
                for x, r in enumerate(span):
                    place = pl.ds(pl.multiple_of((ids[0] ^ r) * rows, rows), rows)
                    outs[w][place, cols] = piece[w, x]


def assemble(plan, ids, spans, groups):
    n = groups[0][0].shape[0]
    pieces = [piece for group in groups for piece in group]
    return pl.pallas_call(
        functools.partial(assemble_kernel, plan, spans, n),
        out_shape=[sds((plan.nz * plan.rows, plan.na * HEAD_DIM), BF16)] * n,
        in_specs=[SMEM] + [VMEM] * len(pieces),
        out_specs=[VMEM] * n,
        cost_estimate=lasts(1.5),
        compiler_params=within(*pieces, *pieces),
    )(ids, *pieces)


def local(queries, key_states, value_states, attn_out, grad_out, frame_order, block_live):
    plan = Plan(queries.shape[0])
    nz, na, nb = plan.nz, plan.na, plan.nb
    slot = lax.axis_index("frame")
    ids = jnp.stack([lax.axis_index("head"), slot // nb, slot % nb]).astype(jnp.int32)

    def staged(order, pieces, send):
        moved = {}
        for step in order:
            moved[step] = send(pieces[step], step)
        return [pieces[0]] + [moved[step] for step in range(1, len(pieces))]

    def head_stage(pieces):
        return staged([*range(2, nz), 1], pieces, over_head)

    def frame_stage(pieces):
        return staged(range(na - 1, 0, -1), pieces, lambda x, s: over_frame(x, s * nb))

    def swapped(parts):
        return staged(range(1, nb), parts, over_frame)

    def regroup(pieces):
        return [jnp.concatenate([p[i : i + 1] for p in pieces]) for i in range(pieces[0].shape[0])]

    def flat_frames_first(by_frame):
        return jnp.concatenate(by_frame)

    def flat_heads_first(by_head):
        return jnp.concatenate([p[s : s + 1] for s in range(na) for p in by_head])

    q_sent = head_stage(prep_query(plan, ids, queries))
    k_near, gv_near = prep_rest(plan, ids, key_states, grad_out, attn_out, value_states)
    k_near = frame_stage(k_near)
    gv_near = frame_stage(gv_near)
    by_key, n_key = lists(plan, ids, frame_order, block_live)
    keys = flat_heads_first(head_stage(regroup(k_near)))
    q_own = flat_frames_first(frame_stage(regroup(q_sent)))
    q_all = jnp.concatenate(swapped([q_own] * nb))
    g_own = flat_heads_first(head_stage(regroup([p[:, : plan.rows + EXTRA] for p in gv_near])))
    g_all = jnp.concatenate(swapped([g_own] * nb))
    values = head_stage(regroup([p[:, plan.rows + EXTRA :] for p in gv_near]))

    lse_part = totals(plan, by_key, n_key, keys, q_all)
    lse, delta = query_rows(plan, g_all, swapped([lse_part] * nb))
    spans = [range(0, 2), range(2, nz)]
    kv_home, dq = [], None
    for place, span in enumerate(spans):
        last = place == len(spans) - 1
        kv, dq_parts = grads(
            plan, span, (by_key, n_key), q_all, g_all, lse, delta, keys,
            [values[r] for r in span], dq, last,
        )
        dq = dq_parts[0]
        kv_home.append(frame_stage(kv))
    dq_home = frame_stage(pack(plan, swapped(dq_parts)))
    grad_key, grad_value = assemble(plan, ids, spans, kv_home)
    (grad_query,) = assemble(plan, ids, [range(nz)], [dq_home])
    return grad_query, grad_key, grad_value


def solution(mesh):
    rows = P(("frame", "head"), None)
    in_specs = (rows,) * 5 + (P(), P())
    out_specs = (P("frame", "head"),) * 3
    return jax.shard_map(local, mesh=mesh, in_specs=in_specs, out_specs=out_specs, check_vma=False)
```

```python
import functools
import math

import jax
import jax.numpy as jnp
from jax import lax
from jax.experimental import pallas as pl
from jax.experimental.pallas import tpu as pltpu
from jax.sharding import PartitionSpec as P


HEADS = 16
HEAD_DIM = 128
NEG = -1e30
KEY_GROUP = 4
WIDE_GROUP = 6
TOGETHER = 4
REACH = 4
EXTRA = 8


VMEM = pl.BlockSpec(memory_space=pltpu.VMEM)
SMEM = pl.BlockSpec(memory_space=pltpu.SMEM)
HBM = pl.BlockSpec(memory_space=pltpu.HBM)
F32 = jnp.float32
BF16 = jnp.bfloat16
NT = (((1,), (1,)), ((), ()))
TN = (((0,), (0,)), ((), ()))
NN = (((1,), (0,)), ((), ()))


def dot(a, b, dims):
    return lax.dot_general(a, b, dims, preferred_element_type=F32)


def sds(shape, dtype):
    return jax.ShapeDtypeStruct(shape, dtype)


def lasts(microseconds):
    return pl.CostEstimate(flops=0, bytes_accessed=int(microseconds * 3.5e6), transcendentals=0)


def within(*shapes):
    held = sum(math.prod(s.shape) * s.dtype.itemsize for s in shapes)
    return pltpu.CompilerParams(vmem_limit_bytes=int(held * 5 // 4) + (6 << 20))


class Plan:
    def __init__(self, rows):
        self.nz = lax.axis_size("head")
        self.nf = lax.axis_size("frame")
        self.hh = HEADS // self.nz
        self.na = min(self.hh, self.nf)
        self.nb = self.nf // self.na
        self.rows = rows
        self.own = self.na * self.nz
        self.total = self.own * self.nb
        assert self.hh == self.na and rows == HEAD_DIM


def over_head(value, step):
    count = lax.axis_size("head")
    return lax.ppermute(value, "head", [(i, i ^ step) for i in range(count)])


def over_frame(value, step):
    count = lax.axis_size("frame")
    return lax.ppermute(value, "frame", [(i, i ^ step) for i in range(count)])


def bundles(plan, ids, refs, bufs, sems):
    width = plan.hh * HEAD_DIM
    out = []
    for r in range(plan.nz):
        cols = pl.ds(pl.multiple_of((ids[0] ^ r) * width, width), width)
        for w, (ref, buf) in enumerate(zip(refs, bufs)):
            out.append(pltpu.make_async_copy(ref.at[:, cols], buf.at[r], sems.at[w, r]))
    for copy in out:
        copy.start()
    return out


def within_bundle(ids, s):
    return pl.ds(pl.multiple_of((ids[1] ^ s) * HEAD_DIM, HEAD_DIM), HEAD_DIM)


def prep_kernel(plan, head_first, ids, x_ref, *refs):
    outs, buf, sems = refs[:-2], refs[-2], refs[-1]
    copies = bundles(plan, ids, [x_ref], [buf], sems)
    for r in range(plan.nz):
        copies[r].wait()
        for s in range(plan.na):
            piece = buf[r, :, within_bundle(ids, s)]
            if head_first:
                outs[r][s] = piece
            else:
                outs[s][r] = piece


def prep(plan, ids, x, head_first):
    pieces, chunk = (plan.nz, plan.na) if head_first else (plan.na, plan.nz)
    return pl.pallas_call(
        functools.partial(prep_kernel, plan, head_first),
        out_shape=[sds((chunk, plan.rows, HEAD_DIM), BF16)] * pieces,
        in_specs=[SMEM, HBM],
        out_specs=[VMEM] * pieces,
        scratch_shapes=[
            pltpu.VMEM((plan.nz, plan.rows, plan.hh * HEAD_DIM), BF16),
            pltpu.SemaphoreType.DMA((1, plan.nz)),
        ],
        cost_estimate=lasts(1.2),
        compiler_params=within(x, x),
    )(ids, x)


def prep_rest_kernel(plan, ids, g_ref, o_ref, v_ref, *refs):
    na, rows = plan.na, plan.rows
    outs, bufs, sems = refs[:na], refs[na : na + 3], refs[na + 3]
    copies = bundles(plan, ids, [g_ref, o_ref, v_ref], bufs, sems)
    ones = jnp.ones((EXTRA, HEAD_DIM), BF16)
    row = lax.broadcasted_iota(jnp.int32, (EXTRA, rows), 0)
    for r in range(plan.nz):
        for copy in copies[3 * r : 3 * r + 3]:
            copy.wait()
        for s in range(na):
            cols = within_bundle(ids, s)
            grad = bufs[0][r, :, cols]
            outs[s][r, :rows] = grad
            outs[s][r, rows + EXTRA :] = bufs[2][r, :, cols]
            product = grad.astype(F32) * bufs[1][r, :, cols].astype(F32)
            high = product.astype(BF16)
            low = (product - high.astype(F32)).astype(BF16)
            delta = dot(ones, high, NT) + dot(ones, low, NT)
            first = delta.astype(BF16).astype(F32)
            rest = delta - first
            second = rest.astype(BF16).astype(F32)
            parts = jnp.where(row == 2, rest - second, 0.0)
            parts = jnp.where(row == 0, first, jnp.where(row == 1, second, parts))
            outs[s][r, rows : rows + EXTRA] = parts.astype(BF16)


def prep_rest(plan, ids, g, o, v):
    return pl.pallas_call(
        functools.partial(prep_rest_kernel, plan),
        out_shape=[sds((plan.nz, 2 * plan.rows + EXTRA, HEAD_DIM), BF16)] * plan.na,
        in_specs=[SMEM] + [HBM] * 3,
        out_specs=[VMEM] * plan.na,
        scratch_shapes=[pltpu.VMEM((plan.nz, plan.rows, plan.hh * HEAD_DIM), BF16)] * 3
        + [pltpu.SemaphoreType.DMA((3, plan.nz))],
        cost_estimate=lasts(2),
        compiler_params=within(g, o, v, g, v),
        name="prep_rest",
    )(ids, g, o, v)


def lists_kernel(plan, ids, order, live_ref, by_key, n_key, query_of, numbers):
    nz, na, nb = plan.nz, plan.na, plan.nb
    z, a, b = ids[0], ids[1], ids[2]
    true = [z ^ r for r in range(nz)]

    def at_distance(d, carry):
        for rk in range(nz):
            count = jnp.int32(0)
            for r in range(nz):
                query_of[d * nz + rk, count] = jnp.int32(r)
                count = count + (live_ref[true[r], true[rk], d] > 0).astype(jnp.int32)
            numbers[d * nz + rk] = count
        return carry

    lax.fori_loop(1, REACH, at_distance, 0)

    def key_frame(s_key, carry):
        place_key = order[(a ^ s_key) * nb + b]

        def query_frame(ts, counts):
            t = ts // na
            place = order[(a ^ (ts - t * na)) * nb + (b ^ t)]
            d = jnp.abs(place - place_key)

            def found(counts):
                counts = list(counts)
                for rk in range(nz):
                    row = d * nz + rk
                    for u in range(nz):
                        by_key[s_key * nz + rk, counts[rk] + u] = ts * nz + query_of[row, u]
                    counts[rk] = counts[rk] + numbers[row]
                return tuple(counts)

            return lax.cond((d > 0) & (d < REACH), found, lambda counts: counts, counts)

        counts = lax.fori_loop(0, na * nb, query_frame, (jnp.int32(0),) * nz)
        for rk in range(nz):
            n_key[s_key * nz + rk] = counts[rk]
        return carry

    lax.fori_loop(0, na, key_frame, 0)


def lists(plan, ids, order, live):
    own, total, nz = plan.own, plan.total, plan.nz
    return pl.pallas_call(
        functools.partial(lists_kernel, plan),
        out_shape=[sds((own, total + WIDE_GROUP + nz), jnp.int32), sds((own,), jnp.int32)],
        in_specs=[SMEM] * 3,
        out_specs=[SMEM] * 2,
        scratch_shapes=[
            pltpu.SMEM((REACH * nz, nz), jnp.int32),
            pltpu.SMEM((REACH * nz,), jnp.int32),
        ],
        cost_estimate=lasts(3),
        compiler_params=within(),
        name="lists",
    )(ids, order, live)


def picks(table, row, count, first, size):
    out = []
    for u in range(size):
        valid = first + u < count
        out.append((jnp.where(valid, table[row, first + u], 0), valid))
    return out


def steps(count, size):
    return lax.div(count + (size - 1), size)


def totals_kernel(plan, by_key, n_key, k_ref, q_ref, out, peaks, sums):
    nz, na, own, rows, total = plan.nz, plan.na, plan.own, plan.rows, plan.total
    scale = HEAD_DIM**-0.5
    length = nz * rows
    peaks[own:, :] = jnp.full((peaks.shape[0] - own, rows), NEG, F32)
    sums[own:, :] = jnp.zeros((peaks.shape[0] - own, rows), F32)

    def near(s, carry):
        span = pl.ds(s * nz, nz)
        keys, q = k_ref[span].reshape(length, HEAD_DIM), q_ref[span].reshape(length, HEAD_DIM)
        scores = scale * dot(keys, q, NT)
        peak = jnp.max(scores, axis=0, keepdims=True)
        mass = jnp.sum(jnp.exp(scores - peak), axis=0, keepdims=True)
        for r in range(nz):
            peaks[pl.ds(s * nz + r, 1), :] = peak[:, r * rows : (r + 1) * rows]
            sums[pl.ds(s * nz + r, 1), :] = mass[:, r * rows : (r + 1) * rows]
        return carry

    lax.fori_loop(0, na, near, 0)

    def local(j, start):
        chosen = picks(by_key, j, n_key[j], start, WIDE_GROUP)
        places = [pl.ds(jnp.where(ok, i, total), 1) for i, ok in chosen]
        q = jnp.concatenate([q_ref[i] for i, _ in chosen], axis=0)
        scores = scale * dot(k_ref[j], q, NT)
        peak = jnp.max(scores, axis=0, keepdims=True)
        mass = jnp.sum(jnp.exp(scores - peak), axis=0, keepdims=True)
        return places, peak, mass

    def merge(places, peak, mass):
        old_peak = jnp.concatenate([peaks[place, :] for place in places], axis=1)
        old_mass = jnp.concatenate([sums[place, :] for place in places], axis=1)
        new_peak = jnp.maximum(old_peak, peak)
        new_mass = old_mass * jnp.exp(old_peak - new_peak) + mass * jnp.exp(peak - new_peak)
        for u, place in enumerate(places):
            peaks[place, :] = new_peak[:, u * rows : (u + 1) * rows]
            sums[place, :] = new_mass[:, u * rows : (u + 1) * rows]

    def away(m, carry):
        for found in [local(m * TOGETHER + u, 0) for u in range(TOGETHER)]:
            merge(*found)
        return carry

    lax.fori_loop(0, own // TOGETHER, away, 0)

    def rest(j, carry):
        def group(step, carry):
            merge(*local(j, step * WIDE_GROUP))
            return carry

        return lax.fori_loop(1, steps(n_key[j], WIDE_GROUP), group, carry)

    lax.fori_loop(0, own, rest, 0)
    peak = peaks[:total, :]
    out[...] = jnp.where(peak > 0.5 * NEG, peak + jnp.log(sums[:total, :]), NEG)


def totals(plan, by_key, n_key, keys, queries):
    return pl.pallas_call(
        functools.partial(totals_kernel, plan),
        out_shape=sds((plan.total, plan.rows), F32),
        in_specs=[SMEM, SMEM, VMEM, VMEM],
        out_specs=VMEM,
        scratch_shapes=[pltpu.VMEM((plan.total + 8, plan.rows), F32)] * 2,
        cost_estimate=lasts(6),
        compiler_params=within(keys, queries),
        name="totals",
    )(by_key, n_key, keys, queries)


def rows_kernel(plan, g_ref, *refs):
    nb, own, rows = plan.nb, plan.own, plan.rows
    parts, lse_all, delta_all = refs[:nb], refs[nb], refs[nb + 1]
    for t in range(nb):
        rivals = [parts[u][pl.ds((t ^ u) * own, own), :] for u in range(nb)]
        peak = functools.reduce(jnp.maximum, rivals)
        lse_all[pl.ds(t * own, own), :] = peak + jnp.log(sum(jnp.exp(x - peak) for x in rivals))

    def fill(i, carry):
        delta_all[pl.ds(i, 1), :] = jnp.sum(g_ref[i, rows:].astype(F32), axis=0, keepdims=True)
        return carry

    lax.fori_loop(0, plan.total, fill, 0)


def query_rows(plan, out_grads, parts):
    return pl.pallas_call(
        functools.partial(rows_kernel, plan),
        out_shape=[sds((plan.total, plan.rows), F32)] * 2,
        in_specs=[VMEM] * (1 + plan.nb),
        out_specs=[VMEM] * 2,
        cost_estimate=lasts(1),
        compiler_params=within(out_grads),
        name="query_rows",
    )(out_grads, *parts)


def grads_kernel(plan, span, first, last, by_key, n_key, q_ref, g_ref, lse_ref, delta_ref, k_ref, *refs):
    nz, na, nb, own, rows = plan.nz, plan.na, plan.nb, plan.own, plan.rows
    hd = HEAD_DIM
    scale = hd**-0.5
    length = nz * rows
    width = len(span)
    refs = list(refs)
    take = lambda n: [refs.pop(0) for _ in range(n)]
    v_refs = take(width)
    if not first:
        (dq_before,) = take(1)
    kv_outs = take(na)
    dq_outs = take(nb if last else 1)
    dk_all, dv_all = take(2)
    dq_all = refs.pop(0) if last else dq_outs[0]

    def begin(i, carry):
        dq_all[i] = jnp.zeros((rows, hd), F32) if first else dq_before[i]
        return carry

    lax.fori_loop(own if first else 0, plan.total, begin, 0)

    def wide_row(ref, start):
        return jnp.concatenate([ref[pl.ds(start + r, 1), :] for r in range(nz)], axis=1)

    def diagonal(s, carry):
        frame = pl.ds(s * nz, nz)
        k = jnp.concatenate([k_ref[s * nz + r] for r in span], axis=0)
        v = jnp.concatenate([v_ref[s] for v_ref in v_refs], axis=0)
        q, g = q_ref[frame].reshape(length, hd), g_ref[frame, :rows].reshape(length, hd)
        lse, delta = wide_row(lse_ref, s * nz), wide_row(delta_ref, s * nz)
        probs = jnp.exp(scale * dot(k, q, NT) - lse)
        dv = dot(probs.astype(BF16), g, NN)
        grad_scores = (probs * (dot(v, g, NT) - delta)).astype(BF16)
        dk = dot(grad_scores, q, NN)
        dq = dot(grad_scores, k, TN).reshape(nz, rows, hd)
        for x in range(width):
            dv_all[s * width + x] = dv[x * rows : (x + 1) * rows]
            dk_all[s * width + x] = dk[x * rows : (x + 1) * rows]
        if first:
            dq_all[frame] = dq
        else:
            dq_all[frame] += dq
        return carry

    lax.fori_loop(0, na, diagonal, 0)

    def terms(s, x, j, start):
        k, v = k_ref[j], v_refs[x][s]
        chosen = picks(by_key, j, n_key[j], start, KEY_GROUP)
        q = jnp.concatenate([q_ref[i] for i, _ in chosen], axis=0)
        g = jnp.concatenate([g_ref[i, :rows] for i, _ in chosen], axis=0)
        lse = jnp.concatenate([jnp.where(ok, lse_ref[pl.ds(i, 1), :], -NEG) for i, ok in chosen], axis=1)
        delta = jnp.concatenate([delta_ref[pl.ds(i, 1), :] for i, _ in chosen], axis=1)
        probs = jnp.exp(scale * dot(k, q, NT) - lse)
        dv = dot(probs.astype(BF16), g, NN)
        grad_scores = (probs * (dot(v, g, NT) - delta)).astype(BF16)
        dk = dot(grad_scores, q, NN)
        return chosen, dv, dk, dot(grad_scores, k, TN)

    def add(s, x, found):
        chosen, dv, dk, dq = found
        dv_all[s * width + x] += dv
        dk_all[s * width + x] += dk
        for u, (i, _) in enumerate(chosen):
            dq_all[i] += dq[u * rows : (u + 1) * rows]

    def away(s, carry):
        for x, found in [(x, terms(s, x, s * nz + r, 0)) for x, r in enumerate(span)]:
            add(s, x, found)
        for x, r in enumerate(span):

            def group(step, carry, x=x, r=r):
                add(s, x, terms(s, x, s * nz + r, step * KEY_GROUP))
                return carry

            lax.fori_loop(1, steps(n_key[s * nz + r], KEY_GROUP), group, 0)
        return carry

    lax.fori_loop(0, na, away, 0)

    for s, out in enumerate(kv_outs):
        for x in range(width):
            out[0, x] = (scale * dk_all[s * width + x]).astype(BF16)
            out[1, x] = dv_all[s * width + x].astype(BF16)
    if last:
        for t in range(nb):

            def drain(m, carry, t=t):
                dq_outs[t][m] = scale * dq_all[t * own + m]
                return carry

            lax.fori_loop(0, own, drain, 0)


def grads(plan, span, tables, queries, out_grads, lse, delta, keys, values, dq_before, last):
    nb, na, own, rows, total = plan.nb, plan.na, plan.own, plan.rows, plan.total
    hd, width, first = HEAD_DIM, len(span), dq_before is None
    kv = [sds((2, width, rows, hd), BF16)] * na
    dq = [sds((own, rows, hd), F32)] * nb if last else [sds((total, rows, hd), F32)]
    before = [] if first else [dq_before]
    partial = sds((own, rows, hd), F32)
    outs = pl.pallas_call(
        functools.partial(grads_kernel, plan, span, first, last),
        out_shape=kv + dq,
        in_specs=[SMEM] * 2 + [VMEM] * (5 + width + len(before)),
        out_specs=[VMEM] * (na + len(dq)),
        scratch_shapes=[pltpu.VMEM((na * width, rows, hd), F32)] * 2
        + ([pltpu.VMEM((total, rows, hd), F32)] if last else []),
        cost_estimate=lasts(7),
        compiler_params=within(queries, out_grads, keys, keys, *[partial] * (4 + 3 * nb)),
    )(*tables, queries, out_grads, lse, delta, keys, *values, *before)
    return outs[:na], outs[na:]


def pack_kernel(plan, *refs):
    nb, nz = plan.nb, plan.nz
    for s, out in enumerate(refs[nb:]):
        for r in range(nz):
            out[0, r] = sum(ref[s * nz + r] for ref in refs[:nb]).astype(BF16)


def pack(plan, partials):
    return pl.pallas_call(
        functools.partial(pack_kernel, plan),
        out_shape=[sds((1, plan.nz, plan.rows, HEAD_DIM), BF16)] * plan.na,
        in_specs=[VMEM] * plan.nb,
        out_specs=[VMEM] * plan.na,
        cost_estimate=lasts(1),
        compiler_params=within(*partials, *partials),
        name="pack",
    )(*partials)


def assemble_kernel(plan, spans, n, ids, *refs):
    na, rows, hd = plan.na, plan.rows, HEAD_DIM
    refs = list(refs)
    outs = refs[na * len(spans) :]
    for span in spans:
        for s in range(na):
            piece = refs.pop(0)
            cols = pl.ds(pl.multiple_of((ids[1] ^ s) * hd, hd), hd)
            for w in range(n):
                for x, r in enumerate(span):
                    place = pl.ds(pl.multiple_of((ids[0] ^ r) * rows, rows), rows)
                    outs[w][place, cols] = piece[w, x]


def assemble(plan, ids, spans, groups):
    n = groups[0][0].shape[0]
    pieces = [piece for group in groups for piece in group]
    return pl.pallas_call(
        functools.partial(assemble_kernel, plan, spans, n),
        out_shape=[sds((plan.nz * plan.rows, plan.na * HEAD_DIM), BF16)] * n,
        in_specs=[SMEM] + [VMEM] * len(pieces),
        out_specs=[VMEM] * n,
        cost_estimate=lasts(1.5),
        compiler_params=within(*pieces, *pieces),
    )(ids, *pieces)


def local(queries, key_states, value_states, attn_out, grad_out, frame_order, block_live):
    plan = Plan(queries.shape[0])
    nz, na, nb = plan.nz, plan.na, plan.nb
    slot = lax.axis_index("frame")
    ids = jnp.stack([lax.axis_index("head"), slot // nb, slot % nb]).astype(jnp.int32)

    def staged(order, pieces, send):
        moved = {}
        for step in order:
            moved[step] = send(pieces[step], step)
        return [pieces[0]] + [moved[step] for step in range(1, len(pieces))]

    def head_stage(pieces):
        return staged([*range(2, nz), 1], pieces, over_head)

    def frame_stage(pieces):
        return staged(range(na - 1, 0, -1), pieces, lambda x, s: over_frame(x, s * nb))

    def swapped(parts):
        return staged(range(1, nb), parts, over_frame)

    def regroup(pieces):
        return [jnp.concatenate([p[i : i + 1] for p in pieces]) for i in range(pieces[0].shape[0])]

    def flat_frames_first(by_frame):
        return jnp.concatenate(by_frame)

    def flat_heads_first(by_head):
        return jnp.concatenate([p[s : s + 1] for s in range(na) for p in by_head])

    q_sent = head_stage(prep(plan, ids, queries, True))
    k_near = frame_stage(prep(plan, ids, key_states, False))
    gv_near = frame_stage(prep_rest(plan, ids, grad_out, attn_out, value_states))
    by_key, n_key = lists(plan, ids, frame_order, block_live.transpose(1, 2, 0))
    keys = flat_heads_first(head_stage(regroup(k_near)))
    q_own = flat_frames_first(frame_stage(regroup(q_sent)))
    q_all = jnp.concatenate(swapped([q_own] * nb))
    g_own = flat_heads_first(head_stage(regroup([p[:, : plan.rows + EXTRA] for p in gv_near])))
    g_all = jnp.concatenate(swapped([g_own] * nb))
    values = head_stage(regroup([p[:, plan.rows + EXTRA :] for p in gv_near]))

    lse_part = totals(plan, by_key, n_key, keys, q_all)
    lse, delta = query_rows(plan, g_all, swapped([lse_part] * nb))
    spans = [range(0, 2), range(2, nz)]
    kv_home, dq = [], None
    for place, span in enumerate(spans):
        last = place == len(spans) - 1
        kv, dq_parts = grads(
            plan, span, (by_key, n_key), q_all, g_all, lse, delta, keys,
            [values[r] for r in span], dq, last,
        )
        dq = dq_parts[0]
        kv_home.append(frame_stage(kv))
    dq_home = frame_stage(pack(plan, swapped(dq_parts)))
    grad_key, grad_value = assemble(plan, ids, spans, kv_home)
    (grad_query,) = assemble(plan, ids, [range(nz)], [dq_home])
    return grad_query, grad_key, grad_value


def solution(mesh):
    rows = P(("frame", "head"), None)
    in_specs = (rows,) * 5 + (P(), P())
    out_specs = (P("frame", "head"),) * 3
    return jax.shard_map(local, mesh=mesh, in_specs=in_specs, out_specs=out_specs, check_vma=False)
```

```python
import functools
import math

import jax
import jax.numpy as jnp
from jax import lax
from jax.experimental import pallas as pl
from jax.experimental.pallas import tpu as pltpu
from jax.sharding import PartitionSpec as P


HEADS = 16
HEAD_DIM = 128
NEG = -1e30
KEY_GROUP = 4
WIDE_GROUP = 6
TOGETHER = 4
REACH = 4
EXTRA = 8


VMEM = pl.BlockSpec(memory_space=pltpu.VMEM)
SMEM = pl.BlockSpec(memory_space=pltpu.SMEM)
HBM = pl.BlockSpec(memory_space=pltpu.HBM)
F32 = jnp.float32
BF16 = jnp.bfloat16
NT = (((1,), (1,)), ((), ()))
TN = (((0,), (0,)), ((), ()))
NN = (((1,), (0,)), ((), ()))


def dot(a, b, dims):
    return lax.dot_general(a, b, dims, preferred_element_type=F32)


def sds(shape, dtype):
    return jax.ShapeDtypeStruct(shape, dtype)


def lasts(microseconds):
    return pl.CostEstimate(flops=0, bytes_accessed=int(microseconds * 3.5e6), transcendentals=0)


def within(*shapes):
    held = sum(math.prod(s.shape) * s.dtype.itemsize for s in shapes)
    return pltpu.CompilerParams(vmem_limit_bytes=int(held * 5 // 4) + (6 << 20))


class Plan:
    def __init__(self, rows):
        self.nz = lax.axis_size("head")
        self.nf = lax.axis_size("frame")
        self.hh = HEADS // self.nz
        self.na = min(self.hh, self.nf)
        self.nb = self.nf // self.na
        self.rows = rows
        self.own = self.na * self.nz
        self.total = self.own * self.nb
        assert self.hh == self.na and rows == HEAD_DIM


def over_head(value, step):
    count = lax.axis_size("head")
    return lax.ppermute(value, "head", [(i, i ^ step) for i in range(count)])


def over_frame(value, step):
    count = lax.axis_size("frame")
    return lax.ppermute(value, "frame", [(i, i ^ step) for i in range(count)])


def bundles(plan, ids, refs, bufs, sems):
    width = plan.hh * HEAD_DIM
    out = []
    for r in range(plan.nz):
        cols = pl.ds(pl.multiple_of((ids[0] ^ r) * width, width), width)
        for w, (ref, buf) in enumerate(zip(refs, bufs)):
            out.append(pltpu.make_async_copy(ref.at[:, cols], buf.at[r], sems.at[w, r]))
    for copy in out:
        copy.start()
    return out


def within_bundle(ids, s):
    return pl.ds(pl.multiple_of((ids[1] ^ s) * HEAD_DIM, HEAD_DIM), HEAD_DIM)


def prep_kernel(plan, q_ref, k_ref, out):
    hd, rows = HEAD_DIM, plan.rows
    for a in range(plan.na):
        for z in range(plan.nz):
            head, place = z * plan.hh + a, a * plan.nz + z
            out[place, :rows] = q_ref[:, head * hd : (head + 1) * hd]
            out[place, rows:] = k_ref[:, head * hd : (head + 1) * hd]


def prep(plan, q, k):
    return pl.pallas_call(
        functools.partial(prep_kernel, plan),
        out_shape=sds((plan.own, 2 * plan.rows, HEAD_DIM), BF16),
        in_specs=[VMEM] * 2,
        out_specs=VMEM,
        cost_estimate=lasts(1.5),
        compiler_params=within(q, k, q, k),
        name="prep",
    )(q, k)


def part_kernel(plan, ids, x_ref, q_out, k_out):
    rows = plan.rows
    for s in range(plan.na):
        for r in range(plan.nz):
            place = (ids[1] ^ s) * plan.nz + (ids[0] ^ r)
            q_out[s * plan.nz + r] = x_ref[place, :rows]
            k_out[s * plan.nz + r] = x_ref[place, rows:]


def part(plan, ids, x):
    return pl.pallas_call(
        functools.partial(part_kernel, plan),
        out_shape=[sds((plan.own, plan.rows, HEAD_DIM), BF16)] * 2,
        in_specs=[SMEM, VMEM],
        out_specs=[VMEM] * 2,
        cost_estimate=lasts(1),
        compiler_params=within(x, x),
        name="part",
    )(ids, x)


def prep_rest_kernel(plan, ids, g_ref, o_ref, v_ref, *refs):
    na, rows = plan.na, plan.rows
    outs, bufs, sems = refs[:na], refs[na : na + 3], refs[na + 3]
    copies = bundles(plan, ids, [g_ref, o_ref, v_ref], bufs, sems)
    ones = jnp.ones((EXTRA, HEAD_DIM), BF16)
    row = lax.broadcasted_iota(jnp.int32, (EXTRA, rows), 0)
    for r in range(plan.nz):
        for copy in copies[3 * r : 3 * r + 3]:
            copy.wait()
        for s in range(na):
            cols = within_bundle(ids, s)
            grad = bufs[0][r, :, cols]
            outs[s][r, :rows] = grad
            outs[s][r, rows + EXTRA :] = bufs[2][r, :, cols]
            product = grad.astype(F32) * bufs[1][r, :, cols].astype(F32)
            high = product.astype(BF16)
            low = (product - high.astype(F32)).astype(BF16)
            delta = dot(ones, high, NT) + dot(ones, low, NT)
            first = delta.astype(BF16).astype(F32)
            rest = delta - first
            second = rest.astype(BF16).astype(F32)
            parts = jnp.where(row == 2, rest - second, 0.0)
            parts = jnp.where(row == 0, first, jnp.where(row == 1, second, parts))
            outs[s][r, rows : rows + EXTRA] = parts.astype(BF16)


def prep_rest(plan, ids, g, o, v):
    return pl.pallas_call(
        functools.partial(prep_rest_kernel, plan),
        out_shape=[sds((plan.nz, 2 * plan.rows + EXTRA, HEAD_DIM), BF16)] * plan.na,
        in_specs=[SMEM] + [HBM] * 3,
        out_specs=[VMEM] * plan.na,
        scratch_shapes=[pltpu.VMEM((plan.nz, plan.rows, plan.hh * HEAD_DIM), BF16)] * 3
        + [pltpu.SemaphoreType.DMA((3, plan.nz))],
        cost_estimate=lasts(2),
        compiler_params=within(g, o, v, g, v),
        name="prep_rest",
    )(ids, g, o, v)


def lists_kernel(plan, ids, order, live_ref, by_key, n_key, query_of, numbers):
    nz, na, nb = plan.nz, plan.na, plan.nb
    z, a, b = ids[0], ids[1], ids[2]
    true = [z ^ r for r in range(nz)]

    def at_distance(d, carry):
        for rk in range(nz):
            count = jnp.int32(0)
            for r in range(nz):
                query_of[d * nz + rk, count] = jnp.int32(r)
                count = count + (live_ref[true[r], true[rk], d] > 0).astype(jnp.int32)
            numbers[d * nz + rk] = count
        return carry

    lax.fori_loop(1, REACH, at_distance, 0)

    def key_frame(s_key, carry):
        place_key = order[(a ^ s_key) * nb + b]

        def query_frame(ts, counts):
            t = ts // na
            place = order[(a ^ (ts - t * na)) * nb + (b ^ t)]
            d = jnp.abs(place - place_key)

            def found(counts):
                counts = list(counts)
                for rk in range(nz):
                    row = d * nz + rk
                    for u in range(nz):
                        by_key[s_key * nz + rk, counts[rk] + u] = ts * nz + query_of[row, u]
                    counts[rk] = counts[rk] + numbers[row]
                return tuple(counts)

            return lax.cond((d > 0) & (d < REACH), found, lambda counts: counts, counts)

        counts = lax.fori_loop(0, na * nb, query_frame, (jnp.int32(0),) * nz)
        for rk in range(nz):
            n_key[s_key * nz + rk] = counts[rk]
        return carry

    lax.fori_loop(0, na, key_frame, 0)


def lists(plan, ids, order, live):
    own, total, nz = plan.own, plan.total, plan.nz
    return pl.pallas_call(
        functools.partial(lists_kernel, plan),
        out_shape=[sds((own, total + WIDE_GROUP + nz), jnp.int32), sds((own,), jnp.int32)],
        in_specs=[SMEM] * 3,
        out_specs=[SMEM] * 2,
        scratch_shapes=[
            pltpu.SMEM((REACH * nz, nz), jnp.int32),
            pltpu.SMEM((REACH * nz,), jnp.int32),
        ],
        cost_estimate=lasts(3),
        compiler_params=within(),
        name="lists",
    )(ids, order, live)


def picks(table, row, count, first, size):
    out = []
    for u in range(size):
        valid = first + u < count
        out.append((jnp.where(valid, table[row, first + u], 0), valid))
    return out


def steps(count, size):
    return lax.div(count + (size - 1), size)


def totals_kernel(plan, by_key, n_key, k_ref, q_ref, out, peaks, sums):
    nz, na, own, rows, total = plan.nz, plan.na, plan.own, plan.rows, plan.total
    scale = HEAD_DIM**-0.5
    length = nz * rows
    peaks[own:, :] = jnp.full((peaks.shape[0] - own, rows), NEG, F32)
    sums[own:, :] = jnp.zeros((peaks.shape[0] - own, rows), F32)

    def near(s, carry):
        span = pl.ds(s * nz, nz)
        keys, q = k_ref[span].reshape(length, HEAD_DIM), q_ref[span].reshape(length, HEAD_DIM)
        scores = scale * dot(keys, q, NT)
        peak = jnp.max(scores, axis=0, keepdims=True)
        mass = jnp.sum(jnp.exp(scores - peak), axis=0, keepdims=True)
        for r in range(nz):
            peaks[pl.ds(s * nz + r, 1), :] = peak[:, r * rows : (r + 1) * rows]
            sums[pl.ds(s * nz + r, 1), :] = mass[:, r * rows : (r + 1) * rows]
        return carry

    lax.fori_loop(0, na, near, 0)

    def local(j, start):
        chosen = picks(by_key, j, n_key[j], start, WIDE_GROUP)
        places = [pl.ds(jnp.where(ok, i, total), 1) for i, ok in chosen]
        q = jnp.concatenate([q_ref[i] for i, _ in chosen], axis=0)
        scores = scale * dot(k_ref[j], q, NT)
        peak = jnp.max(scores, axis=0, keepdims=True)
        mass = jnp.sum(jnp.exp(scores - peak), axis=0, keepdims=True)
        return places, peak, mass

    def merge(places, peak, mass):
        old_peak = jnp.concatenate([peaks[place, :] for place in places], axis=1)
        old_mass = jnp.concatenate([sums[place, :] for place in places], axis=1)
        new_peak = jnp.maximum(old_peak, peak)
        new_mass = old_mass * jnp.exp(old_peak - new_peak) + mass * jnp.exp(peak - new_peak)
        for u, place in enumerate(places):
            peaks[place, :] = new_peak[:, u * rows : (u + 1) * rows]
            sums[place, :] = new_mass[:, u * rows : (u + 1) * rows]

    def away(m, carry):
        for found in [local(m * TOGETHER + u, 0) for u in range(TOGETHER)]:
            merge(*found)
        return carry

    lax.fori_loop(0, own // TOGETHER, away, 0)

    def rest(j, carry):
        def group(step, carry):
            merge(*local(j, step * WIDE_GROUP))
            return carry

        return lax.fori_loop(1, steps(n_key[j], WIDE_GROUP), group, carry)

    lax.fori_loop(0, own, rest, 0)
    peak = peaks[:total, :]
    out[...] = jnp.where(peak > 0.5 * NEG, peak + jnp.log(sums[:total, :]), NEG)


def totals(plan, by_key, n_key, keys, queries):
    return pl.pallas_call(
        functools.partial(totals_kernel, plan),
        out_shape=sds((plan.total, plan.rows), F32),
        in_specs=[SMEM, SMEM, VMEM, VMEM],
        out_specs=VMEM,
        scratch_shapes=[pltpu.VMEM((plan.total + 8, plan.rows), F32)] * 2,
        cost_estimate=lasts(6),
        compiler_params=within(keys, queries),
        name="totals",
    )(by_key, n_key, keys, queries)


def rows_kernel(plan, g_ref, *refs):
    nb, own, rows = plan.nb, plan.own, plan.rows
    parts, lse_all, delta_all = refs[:nb], refs[nb], refs[nb + 1]
    for t in range(nb):
        rivals = [parts[u][pl.ds((t ^ u) * own, own), :] for u in range(nb)]
        peak = functools.reduce(jnp.maximum, rivals)
        lse_all[pl.ds(t * own, own), :] = peak + jnp.log(sum(jnp.exp(x - peak) for x in rivals))

    def fill(i, carry):
        delta_all[pl.ds(i, 1), :] = jnp.sum(g_ref[i, rows:].astype(F32), axis=0, keepdims=True)
        return carry

    lax.fori_loop(0, plan.total, fill, 0)


def query_rows(plan, out_grads, parts):
    return pl.pallas_call(
        functools.partial(rows_kernel, plan),
        out_shape=[sds((plan.total, plan.rows), F32)] * 2,
        in_specs=[VMEM] * (1 + plan.nb),
        out_specs=[VMEM] * 2,
        cost_estimate=lasts(1),
        compiler_params=within(out_grads),
        name="query_rows",
    )(out_grads, *parts)


def grads_kernel(plan, span, first, last, by_key, n_key, q_ref, g_ref, lse_ref, delta_ref, k_ref, *refs):
    nz, na, nb, own, rows = plan.nz, plan.na, plan.nb, plan.own, plan.rows
    hd = HEAD_DIM
    scale = hd**-0.5
    length = nz * rows
    width = len(span)
    refs = list(refs)
    take = lambda n: [refs.pop(0) for _ in range(n)]
    v_refs = take(width)
    if not first:
        (dq_before,) = take(1)
    kv_outs = take(na)
    dq_outs = take(nb if last else 1)
    dk_all, dv_all = take(2)
    dq_all = refs.pop(0) if last else dq_outs[0]

    def begin(i, carry):
        dq_all[i] = jnp.zeros((rows, hd), F32) if first else dq_before[i]
        return carry

    lax.fori_loop(own if first else 0, plan.total, begin, 0)

    def wide_row(ref, start):
        return jnp.concatenate([ref[pl.ds(start + r, 1), :] for r in range(nz)], axis=1)

    def diagonal(s, carry):
        frame = pl.ds(s * nz, nz)
        k = jnp.concatenate([k_ref[s * nz + r] for r in span], axis=0)
        v = jnp.concatenate([v_ref[s] for v_ref in v_refs], axis=0)
        q, g = q_ref[frame].reshape(length, hd), g_ref[frame, :rows].reshape(length, hd)
        lse, delta = wide_row(lse_ref, s * nz), wide_row(delta_ref, s * nz)
        probs = jnp.exp(scale * dot(k, q, NT) - lse)
        dv = dot(probs.astype(BF16), g, NN)
        grad_scores = (probs * (dot(v, g, NT) - delta)).astype(BF16)
        dk = dot(grad_scores, q, NN)
        dq = dot(grad_scores, k, TN).reshape(nz, rows, hd)
        for x in range(width):
            dv_all[s * width + x] = dv[x * rows : (x + 1) * rows]
            dk_all[s * width + x] = dk[x * rows : (x + 1) * rows]
        if first:
            dq_all[frame] = dq
        else:
            dq_all[frame] += dq
        return carry

    lax.fori_loop(0, na, diagonal, 0)

    def terms(s, x, j, start):
        k, v = k_ref[j], v_refs[x][s]
        chosen = picks(by_key, j, n_key[j], start, KEY_GROUP)
        q = jnp.concatenate([q_ref[i] for i, _ in chosen], axis=0)
        g = jnp.concatenate([g_ref[i, :rows] for i, _ in chosen], axis=0)
        lse = jnp.concatenate([jnp.where(ok, lse_ref[pl.ds(i, 1), :], -NEG) for i, ok in chosen], axis=1)
        delta = jnp.concatenate([delta_ref[pl.ds(i, 1), :] for i, _ in chosen], axis=1)
        probs = jnp.exp(scale * dot(k, q, NT) - lse)
        dv = dot(probs.astype(BF16), g, NN)
        grad_scores = (probs * (dot(v, g, NT) - delta)).astype(BF16)
        dk = dot(grad_scores, q, NN)
        return chosen, dv, dk, dot(grad_scores, k, TN)

    def add(s, x, found):
        chosen, dv, dk, dq = found
        dv_all[s * width + x] += dv
        dk_all[s * width + x] += dk
        for u, (i, _) in enumerate(chosen):
            dq_all[i] += dq[u * rows : (u + 1) * rows]

    def away(s, carry):
        for x, found in [(x, terms(s, x, s * nz + r, 0)) for x, r in enumerate(span)]:
            add(s, x, found)
        for x, r in enumerate(span):

            def group(step, carry, x=x, r=r):
                add(s, x, terms(s, x, s * nz + r, step * KEY_GROUP))
                return carry

            lax.fori_loop(1, steps(n_key[s * nz + r], KEY_GROUP), group, 0)
        return carry

    lax.fori_loop(0, na, away, 0)

    for s, out in enumerate(kv_outs):
        for x in range(width):
            out[0, x] = (scale * dk_all[s * width + x]).astype(BF16)
            out[1, x] = dv_all[s * width + x].astype(BF16)
    if last:
        for t in range(nb):

            def drain(m, carry, t=t):
                dq_outs[t][m] = scale * dq_all[t * own + m]
                return carry

            lax.fori_loop(0, own, drain, 0)


def grads(plan, span, tables, queries, out_grads, lse, delta, keys, values, dq_before, last):
    nb, na, own, rows, total = plan.nb, plan.na, plan.own, plan.rows, plan.total
    hd, width, first = HEAD_DIM, len(span), dq_before is None
    kv = [sds((2, width, rows, hd), BF16)] * na
    dq = [sds((own, rows, hd), F32)] * nb if last else [sds((total, rows, hd), F32)]
    before = [] if first else [dq_before]
    partial = sds((own, rows, hd), F32)
    outs = pl.pallas_call(
        functools.partial(grads_kernel, plan, span, first, last),
        out_shape=kv + dq,
        in_specs=[SMEM] * 2 + [VMEM] * (5 + width + len(before)),
        out_specs=[VMEM] * (na + len(dq)),
        scratch_shapes=[pltpu.VMEM((na * width, rows, hd), F32)] * 2
        + ([pltpu.VMEM((total, rows, hd), F32)] if last else []),
        cost_estimate=lasts(7),
        compiler_params=within(queries, out_grads, keys, keys, *[partial] * (4 + 3 * nb)),
    )(*tables, queries, out_grads, lse, delta, keys, *values, *before)
    return outs[:na], outs[na:]


def pack_kernel(plan, *refs):
    nb, nz = plan.nb, plan.nz
    for s, out in enumerate(refs[nb:]):
        for r in range(nz):
            out[0, r] = sum(ref[s * nz + r] for ref in refs[:nb]).astype(BF16)


def pack(plan, partials):
    return pl.pallas_call(
        functools.partial(pack_kernel, plan),
        out_shape=[sds((1, plan.nz, plan.rows, HEAD_DIM), BF16)] * plan.na,
        in_specs=[VMEM] * plan.nb,
        out_specs=[VMEM] * plan.na,
        cost_estimate=lasts(1),
        compiler_params=within(*partials, *partials),
        name="pack",
    )(*partials)


def assemble_kernel(plan, spans, n, ids, *refs):
    na, rows, hd = plan.na, plan.rows, HEAD_DIM
    refs = list(refs)
    outs = refs[na * len(spans) :]
    for span in spans:
        for s in range(na):
            piece = refs.pop(0)
            cols = pl.ds(pl.multiple_of((ids[1] ^ s) * hd, hd), hd)
            for w in range(n):
                for x, r in enumerate(span):
                    place = pl.ds(pl.multiple_of((ids[0] ^ r) * rows, rows), rows)
                    outs[w][place, cols] = piece[w, x]


def assemble(plan, ids, spans, groups):
    n = groups[0][0].shape[0]
    pieces = [piece for group in groups for piece in group]
    return pl.pallas_call(
        functools.partial(assemble_kernel, plan, spans, n),
        out_shape=[sds((plan.nz * plan.rows, plan.na * HEAD_DIM), BF16)] * n,
        in_specs=[SMEM] + [VMEM] * len(pieces),
        out_specs=[VMEM] * n,
        cost_estimate=lasts(1.5),
        compiler_params=within(*pieces, *pieces),
    )(ids, *pieces)


def local(queries, key_states, value_states, attn_out, grad_out, frame_order, block_live):
    plan = Plan(queries.shape[0])
    nz, na, nb = plan.nz, plan.na, plan.nb
    slot = lax.axis_index("frame")
    ids = jnp.stack([lax.axis_index("head"), slot // nb, slot % nb]).astype(jnp.int32)

    def staged(order, pieces, send):
        moved = {}
        for step in order:
            moved[step] = send(pieces[step], step)
        return [pieces[0]] + [moved[step] for step in range(1, len(pieces))]

    def head_stage(pieces):
        return staged([*range(2, nz), 1], pieces, over_head)

    def frame_stage(pieces):
        return staged(range(na - 1, 0, -1), pieces, lambda x, s: over_frame(x, s * nb))

    def swapped(parts):
        return staged(range(1, nb), parts, over_frame)

    def regroup(pieces):
        return [jnp.concatenate([p[i : i + 1] for p in pieces]) for i in range(pieces[0].shape[0])]

    def flat_heads_first(by_head):
        return jnp.concatenate([p[s : s + 1] for s in range(na) for p in by_head])

    groups = [
        [(a * nb + b) * nz + z for a in range(na) for z in range(nz)] for b in range(nb)
    ]
    mine = lax.all_to_all(
        prep(plan, queries, key_states), ("frame", "head"), 0, 0,
        tiled=True, axis_index_groups=groups,
    )
    gv_near = frame_stage(prep_rest(plan, ids, grad_out, attn_out, value_states))
    by_key, n_key = lists(plan, ids, frame_order, block_live.transpose(1, 2, 0))
    q_own, keys = part(plan, ids, mine)
    q_all = jnp.concatenate(swapped([q_own] * nb))
    g_own = flat_heads_first(head_stage(regroup([p[:, : plan.rows + EXTRA] for p in gv_near])))
    g_all = jnp.concatenate(swapped([g_own] * nb))
    values = head_stage(regroup([p[:, plan.rows + EXTRA :] for p in gv_near]))

    lse_part = totals(plan, by_key, n_key, keys, q_all)
    lse, delta = query_rows(plan, g_all, swapped([lse_part] * nb))
    spans = [range(0, 2), range(2, nz)]
    kv_home, dq = [], None
    for place, span in enumerate(spans):
        last = place == len(spans) - 1
        kv, dq_parts = grads(
            plan, span, (by_key, n_key), q_all, g_all, lse, delta, keys,
            [values[r] for r in span], dq, last,
        )
        dq = dq_parts[0]
        kv_home.append(frame_stage(kv))
    dq_home = frame_stage(pack(plan, swapped(dq_parts)))
    grad_key, grad_value = assemble(plan, ids, spans, kv_home)
    (grad_query,) = assemble(plan, ids, [range(nz)], [dq_home])
    return grad_query, grad_key, grad_value


def solution(mesh):
    rows = P(("frame", "head"), None)
    in_specs = (rows,) * 5 + (P(), P())
    out_specs = (P("frame", "head"),) * 3
    return jax.shard_map(local, mesh=mesh, in_specs=in_specs, out_specs=out_specs, check_vma=False)
```

```python
import functools
import math

import jax
import jax.numpy as jnp
from jax import lax
from jax.experimental import pallas as pl
from jax.experimental.pallas import tpu as pltpu
from jax.sharding import PartitionSpec as P


HEADS = 16
HEAD_DIM = 128
NEG = -1e30
KEY_GROUP = 4
WIDE_GROUP = 6
TOGETHER = 4
REACH = 4
EXTRA = 8


VMEM = pl.BlockSpec(memory_space=pltpu.VMEM)
SMEM = pl.BlockSpec(memory_space=pltpu.SMEM)
HBM = pl.BlockSpec(memory_space=pltpu.HBM)
F32 = jnp.float32
BF16 = jnp.bfloat16
NT = (((1,), (1,)), ((), ()))
TN = (((0,), (0,)), ((), ()))
NN = (((1,), (0,)), ((), ()))


def dot(a, b, dims):
    return lax.dot_general(a, b, dims, preferred_element_type=F32)


def sds(shape, dtype):
    return jax.ShapeDtypeStruct(shape, dtype)


def lasts(microseconds):
    return pl.CostEstimate(flops=0, bytes_accessed=int(microseconds * 3.5e6), transcendentals=0)


def within(*shapes):
    held = sum(math.prod(s.shape) * s.dtype.itemsize for s in shapes)
    return pltpu.CompilerParams(vmem_limit_bytes=int(held * 5 // 4) + (6 << 20))


class Plan:
    def __init__(self, rows):
        self.nz = lax.axis_size("head")
        self.nf = lax.axis_size("frame")
        self.hh = HEADS // self.nz
        self.na = min(self.hh, self.nf)
        self.nb = self.nf // self.na
        self.rows = rows
        self.own = self.na * self.nz
        self.total = self.own * self.nb
        assert self.hh == self.na and rows == HEAD_DIM


def over_head(value, step):
    count = lax.axis_size("head")
    return lax.ppermute(value, "head", [(i, i ^ step) for i in range(count)])


def over_frame(value, step):
    count = lax.axis_size("frame")
    return lax.ppermute(value, "frame", [(i, i ^ step) for i in range(count)])


def bundles(plan, ids, refs, bufs, sems):
    width = plan.hh * HEAD_DIM
    out = []
    for r in range(plan.nz):
        cols = pl.ds(pl.multiple_of((ids[0] ^ r) * width, width), width)
        for w, (ref, buf) in enumerate(zip(refs, bufs)):
            out.append(pltpu.make_async_copy(ref.at[:, cols], buf.at[r], sems.at[w, r]))
    for copy in out:
        copy.start()
    return out


def within_bundle(ids, s):
    return pl.ds(pl.multiple_of((ids[1] ^ s) * HEAD_DIM, HEAD_DIM), HEAD_DIM)


def prep_kernel(plan, q_ref, k_ref, out):
    hd, rows = HEAD_DIM, plan.rows
    for a in range(plan.na):
        for z in range(plan.nz):
            head, place = z * plan.hh + a, a * plan.nz + z
            out[place, :rows] = q_ref[:, head * hd : (head + 1) * hd]
            out[place, rows:] = k_ref[:, head * hd : (head + 1) * hd]


def prep(plan, q, k):
    return pl.pallas_call(
        functools.partial(prep_kernel, plan),
        out_shape=sds((plan.own, 2 * plan.rows, HEAD_DIM), BF16),
        in_specs=[VMEM] * 2,
        out_specs=VMEM,
        cost_estimate=lasts(1.5),
        compiler_params=pltpu.CompilerParams(vmem_limit_bytes=60 << 20),
        name="prep",
    )(q, k)


def part_kernel(plan, ids, x_ref, q_out, k_out):
    rows = plan.rows
    for s in range(plan.na):
        for r in range(plan.nz):
            place = (ids[1] ^ s) * plan.nz + (ids[0] ^ r)
            q_out[s * plan.nz + r] = x_ref[place, :rows]
            k_out[s * plan.nz + r] = x_ref[place, rows:]


def part(plan, ids, x):
    return pl.pallas_call(
        functools.partial(part_kernel, plan),
        out_shape=[sds((plan.own, plan.rows, HEAD_DIM), BF16)] * 2,
        in_specs=[SMEM, VMEM],
        out_specs=[VMEM] * 2,
        cost_estimate=lasts(1),
        compiler_params=within(x, x),
        name="part",
    )(ids, x)


def prep_rest_kernel(plan, ids, g_ref, o_ref, v_ref, *refs):
    na, rows = plan.na, plan.rows
    g_outs, v_outs, bufs, sems = refs[:na], refs[na : 2 * na], refs[2 * na : 2 * na + 3], refs[-1]
    copies = bundles(plan, ids, [g_ref, o_ref, v_ref], bufs, sems)
    ones = jnp.ones((EXTRA, HEAD_DIM), BF16)
    row = lax.broadcasted_iota(jnp.int32, (EXTRA, rows), 0)
    for r in range(plan.nz):
        for copy in copies[3 * r : 3 * r + 3]:
            copy.wait()
        for s in range(na):
            cols = within_bundle(ids, s)
            grad = bufs[0][r, :, cols]
            g_outs[s][r, :rows] = grad
            v_outs[s][r] = bufs[2][r, :, cols]
            product = grad.astype(F32) * bufs[1][r, :, cols].astype(F32)
            high = product.astype(BF16)
            low = (product - high.astype(F32)).astype(BF16)
            delta = dot(ones, high, NT) + dot(ones, low, NT)
            first = delta.astype(BF16).astype(F32)
            rest = delta - first
            second = rest.astype(BF16).astype(F32)
            parts = jnp.where(row == 2, rest - second, 0.0)
            parts = jnp.where(row == 0, first, jnp.where(row == 1, second, parts))
            g_outs[s][r, rows:] = parts.astype(BF16)


def prep_rest(plan, ids, g, o, v):
    na, nz, rows, hd = plan.na, plan.nz, plan.rows, HEAD_DIM
    outs = pl.pallas_call(
        functools.partial(prep_rest_kernel, plan),
        out_shape=[sds((nz, rows + EXTRA, hd), BF16)] * na + [sds((nz, rows, hd), BF16)] * na,
        in_specs=[SMEM] + [HBM] * 3,
        out_specs=[VMEM] * (2 * na),
        scratch_shapes=[pltpu.VMEM((nz, rows, plan.hh * hd), BF16)] * 3
        + [pltpu.SemaphoreType.DMA((3, nz))],
        cost_estimate=lasts(2),
        compiler_params=within(g, o, v, g, v),
        name="prep_rest",
    )(ids, g, o, v)
    return outs[:na], outs[na:]


def turn_kernel(count, *refs):
    pieces, outs = refs[:count], refs[count:]
    joined = len(outs) == 1
    for c in range(pieces[0].shape[0]):
        for p, piece in enumerate(pieces):
            if joined:
                outs[0][c * count + p] = piece[c]
            else:
                outs[c][p] = piece[c]


def turn(pieces, joined=False):
    count, parts, shape = len(pieces), pieces[0].shape[0], pieces[0].shape[1:]
    out = [sds((parts * count, *shape), BF16)] if joined else [sds((count, *shape), BF16)] * parts
    outs = pl.pallas_call(
        functools.partial(turn_kernel, count),
        out_shape=out,
        in_specs=[VMEM] * count,
        out_specs=[VMEM] * len(out),
        cost_estimate=lasts(0.5),
        compiler_params=within(*pieces, *pieces),
    )(*pieces)
    return outs[0] if joined else outs


def lists_kernel(plan, ids, order, live_ref, by_key, n_key, query_of, numbers):
    nz, na, nb = plan.nz, plan.na, plan.nb
    z, a, b = ids[0], ids[1], ids[2]
    true = [z ^ r for r in range(nz)]

    def at_distance(d, carry):
        for rk in range(nz):
            count = jnp.int32(0)
            for r in range(nz):
                query_of[d * nz + rk, count] = jnp.int32(r)
                count = count + (live_ref[true[r], true[rk], d] > 0).astype(jnp.int32)
            numbers[d * nz + rk] = count
        return carry

    lax.fori_loop(1, REACH, at_distance, 0)

    def key_frame(s_key, carry):
        place_key = order[(a ^ s_key) * nb + b]

        def query_frame(ts, counts):
            t = ts // na
            place = order[(a ^ (ts - t * na)) * nb + (b ^ t)]
            d = jnp.abs(place - place_key)

            def found(counts):
                counts = list(counts)
                for rk in range(nz):
                    row = d * nz + rk
                    for u in range(nz):
                        by_key[s_key * nz + rk, counts[rk] + u] = ts * nz + query_of[row, u]
                    counts[rk] = counts[rk] + numbers[row]
                return tuple(counts)

            return lax.cond((d > 0) & (d < REACH), found, lambda counts: counts, counts)

        counts = lax.fori_loop(0, na * nb, query_frame, (jnp.int32(0),) * nz)
        for rk in range(nz):
            n_key[s_key * nz + rk] = counts[rk]
        return carry

    lax.fori_loop(0, na, key_frame, 0)


def lists(plan, ids, order, live):
    own, total, nz = plan.own, plan.total, plan.nz
    return pl.pallas_call(
        functools.partial(lists_kernel, plan),
        out_shape=[sds((own, total + WIDE_GROUP + nz), jnp.int32), sds((own,), jnp.int32)],
        in_specs=[SMEM] * 3,
        out_specs=[SMEM] * 2,
        scratch_shapes=[
            pltpu.SMEM((REACH * nz, nz), jnp.int32),
            pltpu.SMEM((REACH * nz,), jnp.int32),
        ],
        cost_estimate=lasts(3),
        compiler_params=within(),
        name="lists",
    )(ids, order, live)


def picks(table, row, count, first, size):
    out = []
    for u in range(size):
        valid = first + u < count
        out.append((jnp.where(valid, table[row, first + u], 0), valid))
    return out


def steps(count, size):
    return lax.div(count + (size - 1), size)


def totals_kernel(plan, by_key, n_key, k_ref, *refs):
    parts, (out, q_ref, peaks, sums) = refs[: plan.nb], refs[plan.nb :]
    nz, na, own, rows, total = plan.nz, plan.na, plan.own, plan.rows, plan.total
    scale = HEAD_DIM**-0.5
    length = nz * rows
    for t, each in enumerate(parts):
        q_ref[t * own : (t + 1) * own] = each[...]
    peaks[own:, :] = jnp.full((peaks.shape[0] - own, rows), NEG, F32)
    sums[own:, :] = jnp.zeros((peaks.shape[0] - own, rows), F32)

    def near(s, carry):
        span = pl.ds(s * nz, nz)
        keys, q = k_ref[span].reshape(length, HEAD_DIM), q_ref[span].reshape(length, HEAD_DIM)
        scores = scale * dot(keys, q, NT)
        peak = jnp.max(scores, axis=0, keepdims=True)
        mass = jnp.sum(jnp.exp(scores - peak), axis=0, keepdims=True)
        for r in range(nz):
            peaks[pl.ds(s * nz + r, 1), :] = peak[:, r * rows : (r + 1) * rows]
            sums[pl.ds(s * nz + r, 1), :] = mass[:, r * rows : (r + 1) * rows]
        return carry

    lax.fori_loop(0, na, near, 0)

    def local(j, start):
        chosen = picks(by_key, j, n_key[j], start, WIDE_GROUP)
        places = [pl.ds(jnp.where(ok, i, total), 1) for i, ok in chosen]
        q = jnp.concatenate([q_ref[i] for i, _ in chosen], axis=0)
        scores = scale * dot(k_ref[j], q, NT)
        peak = jnp.max(scores, axis=0, keepdims=True)
        mass = jnp.sum(jnp.exp(scores - peak), axis=0, keepdims=True)
        return places, peak, mass

    def merge(places, peak, mass):
        old_peak = jnp.concatenate([peaks[place, :] for place in places], axis=1)
        old_mass = jnp.concatenate([sums[place, :] for place in places], axis=1)
        new_peak = jnp.maximum(old_peak, peak)
        new_mass = old_mass * jnp.exp(old_peak - new_peak) + mass * jnp.exp(peak - new_peak)
        for u, place in enumerate(places):
            peaks[place, :] = new_peak[:, u * rows : (u + 1) * rows]
            sums[place, :] = new_mass[:, u * rows : (u + 1) * rows]

    def away(m, carry):
        for found in [local(m * TOGETHER + u, 0) for u in range(TOGETHER)]:
            merge(*found)
        return carry

    lax.fori_loop(0, own // TOGETHER, away, 0)

    def rest(j, carry):
        def group(step, carry):
            merge(*local(j, step * WIDE_GROUP))
            return carry

        return lax.fori_loop(1, steps(n_key[j], WIDE_GROUP), group, carry)

    lax.fori_loop(0, own, rest, 0)
    peak = peaks[:total, :]
    out[...] = jnp.where(peak > 0.5 * NEG, peak + jnp.log(sums[:total, :]), NEG)


def totals(plan, by_key, n_key, keys, queries):
    return pl.pallas_call(
        functools.partial(totals_kernel, plan),
        out_shape=[
            sds((plan.total, plan.rows), F32),
            sds((plan.total, plan.rows, HEAD_DIM), BF16),
        ],
        in_specs=[SMEM, SMEM, VMEM] + [VMEM] * plan.nb,
        out_specs=[VMEM] * 2,
        scratch_shapes=[pltpu.VMEM((plan.total + 8, plan.rows), F32)] * 2,
        cost_estimate=lasts(6),
        compiler_params=within(keys, *queries, *queries),
        name="totals",
    )(by_key, n_key, keys, *queries)


def rows_kernel(plan, *refs):
    nb, own, rows = plan.nb, plan.own, plan.rows
    g_refs, parts, (lse_all, delta_all, g_all) = refs[:nb], refs[nb : 2 * nb], refs[2 * nb :]
    for t in range(nb):
        rivals = [parts[u][pl.ds((t ^ u) * own, own), :] for u in range(nb)]
        peak = functools.reduce(jnp.maximum, rivals)
        lse_all[pl.ds(t * own, own), :] = peak + jnp.log(sum(jnp.exp(x - peak) for x in rivals))
        for m in range(own):
            extra = g_refs[t][m, rows:].astype(F32)
            delta_all[t * own + m : t * own + m + 1, :] = jnp.sum(extra, axis=0, keepdims=True)
            g_all[t * own + m] = g_refs[t][m, :rows]


def query_rows(plan, out_grads, parts):
    return pl.pallas_call(
        functools.partial(rows_kernel, plan),
        out_shape=[sds((plan.total, plan.rows), F32)] * 2
        + [sds((plan.total, plan.rows, HEAD_DIM), BF16)],
        in_specs=[VMEM] * (2 * plan.nb),
        out_specs=[VMEM] * 3,
        cost_estimate=lasts(1),
        compiler_params=within(*out_grads, *out_grads),
        name="query_rows",
    )(*out_grads, *parts)


def grads_kernel(plan, span, first, last, by_key, n_key, q_ref, g_ref, lse_ref, delta_ref, k_ref, *refs):
    nz, na, nb, own, rows = plan.nz, plan.na, plan.nb, plan.own, plan.rows
    hd = HEAD_DIM
    scale = hd**-0.5
    length = nz * rows
    width = len(span)
    refs = list(refs)
    take = lambda n: [refs.pop(0) for _ in range(n)]
    v_refs = take(width)
    if not first:
        (dq_before,) = take(1)
    kv_outs = take(na)
    dq_outs = take(nb if last else 1)
    dk_all, dv_all = take(2)
    dq_all = refs.pop(0) if last else dq_outs[0]

    def begin(i, carry):
        dq_all[i] = jnp.zeros((rows, hd), F32) if first else dq_before[i]
        return carry

    lax.fori_loop(own if first else 0, plan.total, begin, 0)

    def wide_row(ref, start):
        return jnp.concatenate([ref[pl.ds(start + r, 1), :] for r in range(nz)], axis=1)

    def diagonal(s, carry):
        frame = pl.ds(s * nz, nz)
        k = jnp.concatenate([k_ref[s * nz + r] for r in span], axis=0)
        v = jnp.concatenate([v_ref[s] for v_ref in v_refs], axis=0)
        q, g = q_ref[frame].reshape(length, hd), g_ref[frame].reshape(length, hd)
        lse, delta = wide_row(lse_ref, s * nz), wide_row(delta_ref, s * nz)
        probs = jnp.exp(scale * dot(k, q, NT) - lse)
        dv = dot(probs.astype(BF16), g, NN)
        grad_scores = (probs * (dot(v, g, NT) - delta)).astype(BF16)
        dk = dot(grad_scores, q, NN)
        dq = dot(grad_scores, k, TN).reshape(nz, rows, hd)
        for x in range(width):
            dv_all[s * width + x] = dv[x * rows : (x + 1) * rows]
            dk_all[s * width + x] = dk[x * rows : (x + 1) * rows]
        if first:
            dq_all[frame] = dq
        else:
            dq_all[frame] += dq
        return carry

    lax.fori_loop(0, na, diagonal, 0)

    def terms(s, x, j, start):
        k, v = k_ref[j], v_refs[x][s]
        chosen = picks(by_key, j, n_key[j], start, KEY_GROUP)
        q = jnp.concatenate([q_ref[i] for i, _ in chosen], axis=0)
        g = jnp.concatenate([g_ref[i] for i, _ in chosen], axis=0)
        lse = jnp.concatenate([jnp.where(ok, lse_ref[pl.ds(i, 1), :], -NEG) for i, ok in chosen], axis=1)
        delta = jnp.concatenate([delta_ref[pl.ds(i, 1), :] for i, _ in chosen], axis=1)
        probs = jnp.exp(scale * dot(k, q, NT) - lse)
        dv = dot(probs.astype(BF16), g, NN)
        grad_scores = (probs * (dot(v, g, NT) - delta)).astype(BF16)
        dk = dot(grad_scores, q, NN)
        return chosen, dv, dk, dot(grad_scores, k, TN)

    def add(s, x, found):
        chosen, dv, dk, dq = found
        dv_all[s * width + x] += dv
        dk_all[s * width + x] += dk
        for u, (i, _) in enumerate(chosen):
            dq_all[i] += dq[u * rows : (u + 1) * rows]

    def away(s, carry):
        for x, found in [(x, terms(s, x, s * nz + r, 0)) for x, r in enumerate(span)]:
            add(s, x, found)
        for x, r in enumerate(span):

            def group(step, carry, x=x, r=r):
                add(s, x, terms(s, x, s * nz + r, step * KEY_GROUP))
                return carry

            lax.fori_loop(1, steps(n_key[s * nz + r], KEY_GROUP), group, 0)
        return carry

    lax.fori_loop(0, na, away, 0)

    for s, out in enumerate(kv_outs):
        for x in range(width):
            out[0, x] = (scale * dk_all[s * width + x]).astype(BF16)
            out[1, x] = dv_all[s * width + x].astype(BF16)
    if last:
        for t in range(nb):

            def drain(m, carry, t=t):
                dq_outs[t][m] = scale * dq_all[t * own + m]
                return carry

            lax.fori_loop(0, own, drain, 0)


def grads(plan, span, tables, queries, out_grads, lse, delta, keys, values, dq_before, last):
    nb, na, own, rows, total = plan.nb, plan.na, plan.own, plan.rows, plan.total
    hd, width, first = HEAD_DIM, len(span), dq_before is None
    kv = [sds((2, width, rows, hd), BF16)] * na
    dq = [sds((own, rows, hd), F32)] * nb if last else [sds((total, rows, hd), F32)]
    before = [] if first else [dq_before]
    partial = sds((own, rows, hd), F32)
    outs = pl.pallas_call(
        functools.partial(grads_kernel, plan, span, first, last),
        out_shape=kv + dq,
        in_specs=[SMEM] * 2 + [VMEM] * (5 + width + len(before)),
        out_specs=[VMEM] * (na + len(dq)),
        scratch_shapes=[pltpu.VMEM((na * width, rows, hd), F32)] * 2
        + ([pltpu.VMEM((total, rows, hd), F32)] if last else []),
        cost_estimate=lasts(7),
        compiler_params=within(queries, out_grads, keys, keys, *[partial] * (4 + 3 * nb)),
    )(*tables, queries, out_grads, lse, delta, keys, *values, *before)
    return outs[:na], outs[na:]


def pack_kernel(plan, *refs):
    nb, nz = plan.nb, plan.nz
    for s, out in enumerate(refs[nb:]):
        for r in range(nz):
            out[0, r] = sum(ref[s * nz + r] for ref in refs[:nb]).astype(BF16)


def pack(plan, partials):
    return pl.pallas_call(
        functools.partial(pack_kernel, plan),
        out_shape=[sds((1, plan.nz, plan.rows, HEAD_DIM), BF16)] * plan.na,
        in_specs=[VMEM] * plan.nb,
        out_specs=[VMEM] * plan.na,
        cost_estimate=lasts(1),
        compiler_params=within(*partials, *partials),
        name="pack",
    )(*partials)


def assemble_kernel(plan, spans, n, ids, *refs):
    na, rows, hd = plan.na, plan.rows, HEAD_DIM
    refs = list(refs)
    outs = refs[na * len(spans) :]
    for span in spans:
        for s in range(na):
            piece = refs.pop(0)
            cols = pl.ds(pl.multiple_of((ids[1] ^ s) * hd, hd), hd)
            for w in range(n):
                for x, r in enumerate(span):
                    place = pl.ds(pl.multiple_of((ids[0] ^ r) * rows, rows), rows)
                    outs[w][place, cols] = piece[w, x]


def assemble(plan, ids, spans, groups):
    n = groups[0][0].shape[0]
    pieces = [piece for group in groups for piece in group]
    return pl.pallas_call(
        functools.partial(assemble_kernel, plan, spans, n),
        out_shape=[sds((plan.nz * plan.rows, plan.na * HEAD_DIM), BF16)] * n,
        in_specs=[SMEM] + [VMEM] * len(pieces),
        out_specs=[VMEM] * n,
        cost_estimate=lasts(1.5),
        compiler_params=within(*pieces, *pieces),
    )(ids, *pieces)


def local(queries, key_states, value_states, attn_out, grad_out, frame_order, block_live):
    plan = Plan(queries.shape[0])
    nz, na, nb = plan.nz, plan.na, plan.nb
    slot = lax.axis_index("frame")
    ids = jnp.stack([lax.axis_index("head"), slot // nb, slot % nb]).astype(jnp.int32)

    def staged(order, pieces, send):
        moved = {}
        for step in order:
            moved[step] = send(pieces[step], step)
        return [pieces[0]] + [moved[step] for step in range(1, len(pieces))]

    def head_stage(pieces):
        return staged([*range(2, nz), 1], pieces, over_head)

    def frame_stage(pieces):
        return staged(range(na - 1, 0, -1), pieces, lambda x, s: over_frame(x, s * nb))

    def swapped(parts):
        return staged(range(1, nb), parts, over_frame)

    groups = [
        [(a * nb + b) * nz + z for a in range(na) for z in range(nz)] for b in range(nb)
    ]
    mine = lax.all_to_all(
        prep(plan, queries, key_states), ("frame", "head"), 0, 0,
        tiled=True, axis_index_groups=groups,
    )
    g_near, v_near = prep_rest(plan, ids, grad_out, attn_out, value_states)
    g_near = frame_stage(g_near)
    v_near = frame_stage(v_near)
    by_key, n_key = lists(plan, ids, frame_order, block_live.transpose(1, 2, 0))
    g_own = turn(head_stage(turn(g_near)), joined=True)
    values = head_stage(turn(v_near))
    q_own, keys = part(plan, ids, mine)
    lse_part, q_all = totals(plan, by_key, n_key, keys, swapped([q_own] * nb))
    lse, delta, g_all = query_rows(plan, swapped([g_own] * nb), swapped([lse_part] * nb))
    spans = [range(0, 2), range(2, nz)]
    kv_home, dq = [], None
    for place, span in enumerate(spans):
        last = place == len(spans) - 1
        kv, dq_parts = grads(
            plan, span, (by_key, n_key), q_all, g_all, lse, delta, keys,
            [values[r] for r in span], dq, last,
        )
        dq = dq_parts[0]
        kv_home.append(frame_stage(kv))
    dq_home = frame_stage(pack(plan, swapped(dq_parts)))
    grad_key, grad_value = assemble(plan, ids, spans, kv_home)
    (grad_query,) = assemble(plan, ids, [range(nz)], [dq_home])
    return grad_query, grad_key, grad_value


def solution(mesh):
    rows = P(("frame", "head"), None)
    in_specs = (rows,) * 5 + (P(), P())
    out_specs = (P("frame", "head"),) * 3
    return jax.shard_map(local, mesh=mesh, in_specs=in_specs, out_specs=out_specs, check_vma=False)
```

```python
import functools
import math

import jax
import jax.numpy as jnp
from jax import lax
from jax.experimental import pallas as pl
from jax.experimental.pallas import tpu as pltpu
from jax.sharding import PartitionSpec as P


HEADS = 16
HEAD_DIM = 128
NEG = -1e30
KEY_GROUP = 4
WIDE_GROUP = 6
TOGETHER = 4
REACH = 4
EXTRA = 8


VMEM = pl.BlockSpec(memory_space=pltpu.VMEM)
SMEM = pl.BlockSpec(memory_space=pltpu.SMEM)
HBM = pl.BlockSpec(memory_space=pltpu.HBM)
F32 = jnp.float32
BF16 = jnp.bfloat16
NT = (((1,), (1,)), ((), ()))
TN = (((0,), (0,)), ((), ()))
NN = (((1,), (0,)), ((), ()))


def dot(a, b, dims):
    return lax.dot_general(a, b, dims, preferred_element_type=F32)


def sds(shape, dtype):
    return jax.ShapeDtypeStruct(shape, dtype)


def lasts(microseconds):
    return pl.CostEstimate(flops=0, bytes_accessed=int(microseconds * 3.5e6), transcendentals=0)


def within(*shapes):
    held = sum(math.prod(s.shape) * s.dtype.itemsize for s in shapes)
    return pltpu.CompilerParams(vmem_limit_bytes=int(held * 5 // 4) + (6 << 20))


class Plan:
    def __init__(self, rows):
        self.nz = lax.axis_size("head")
        self.nf = lax.axis_size("frame")
        self.hh = HEADS // self.nz
        self.na = min(self.hh, self.nf)
        self.nb = self.nf // self.na
        self.rows = rows
        self.own = self.na * self.nz
        self.total = self.own * self.nb
        assert self.hh == self.na and rows == HEAD_DIM


def over_head(value, step):
    count = lax.axis_size("head")
    return lax.ppermute(value, "head", [(i, i ^ step) for i in range(count)])


def over_frame(value, step):
    count = lax.axis_size("frame")
    return lax.ppermute(value, "frame", [(i, i ^ step) for i in range(count)])


def bundles(plan, ids, refs, bufs, sems):
    width = plan.hh * HEAD_DIM
    out = []
    for r in range(plan.nz):
        cols = pl.ds(pl.multiple_of((ids[0] ^ r) * width, width), width)
        for w, (ref, buf) in enumerate(zip(refs, bufs)):
            out.append(pltpu.make_async_copy(ref.at[:, cols], buf.at[r], sems.at[w, r]))
    for copy in out:
        copy.start()
    return out


def within_bundle(ids, s):
    return pl.ds(pl.multiple_of((ids[1] ^ s) * HEAD_DIM, HEAD_DIM), HEAD_DIM)


def prep_kernel(plan, head_first, ids, x_ref, *refs):
    outs, buf, sems = refs[:-2], refs[-2], refs[-1]
    copies = bundles(plan, ids, [x_ref], [buf], sems)
    for r in range(plan.nz):
        copies[r].wait()
        for s in range(plan.na):
            piece = buf[r, :, within_bundle(ids, s)]
            if head_first:
                outs[r][s] = piece
            else:
                outs[s][r] = piece


def prep(plan, ids, x, head_first):
    pieces, chunk = (plan.nz, plan.na) if head_first else (plan.na, plan.nz)
    return pl.pallas_call(
        functools.partial(prep_kernel, plan, head_first),
        out_shape=[sds((chunk, plan.rows, HEAD_DIM), BF16)] * pieces,
        in_specs=[SMEM, HBM],
        out_specs=[VMEM] * pieces,
        scratch_shapes=[
            pltpu.VMEM((plan.nz, plan.rows, plan.hh * HEAD_DIM), BF16),
            pltpu.SemaphoreType.DMA((1, plan.nz)),
        ],
        cost_estimate=lasts(1.2),
        compiler_params=pltpu.CompilerParams(vmem_limit_bytes=60 << 20),
    )(ids, x)


def prep_rest_kernel(plan, ids, g_ref, o_ref, v_ref, *refs):
    na, rows = plan.na, plan.rows
    g_outs, v_outs, bufs, sems = refs[:na], refs[na : 2 * na], refs[2 * na : 2 * na + 3], refs[-1]
    copies = bundles(plan, ids, [g_ref, o_ref, v_ref], bufs, sems)
    ones = jnp.ones((EXTRA, HEAD_DIM), BF16)
    row = lax.broadcasted_iota(jnp.int32, (EXTRA, rows), 0)
    for r in range(plan.nz):
        for copy in copies[3 * r : 3 * r + 3]:
            copy.wait()
        for s in range(na):
            cols = within_bundle(ids, s)
            grad = bufs[0][r, :, cols]
            g_outs[s][r, :rows] = grad
            v_outs[s][r] = bufs[2][r, :, cols]
            product = grad.astype(F32) * bufs[1][r, :, cols].astype(F32)
            high = product.astype(BF16)
            low = (product - high.astype(F32)).astype(BF16)
            delta = dot(ones, high, NT) + dot(ones, low, NT)
            first = delta.astype(BF16).astype(F32)
            rest = delta - first
            second = rest.astype(BF16).astype(F32)
            parts = jnp.where(row == 2, rest - second, 0.0)
            parts = jnp.where(row == 0, first, jnp.where(row == 1, second, parts))
            g_outs[s][r, rows:] = parts.astype(BF16)


def prep_rest(plan, ids, g, o, v):
    na, nz, rows, hd = plan.na, plan.nz, plan.rows, HEAD_DIM
    outs = pl.pallas_call(
        functools.partial(prep_rest_kernel, plan),
        out_shape=[sds((nz, rows + EXTRA, hd), BF16)] * na + [sds((nz, rows, hd), BF16)] * na,
        in_specs=[SMEM] + [HBM] * 3,
        out_specs=[VMEM] * (2 * na),
        scratch_shapes=[pltpu.VMEM((nz, rows, plan.hh * hd), BF16)] * 3
        + [pltpu.SemaphoreType.DMA((3, nz))],
        cost_estimate=lasts(2),
        compiler_params=pltpu.CompilerParams(vmem_limit_bytes=58 << 20),
        name="prep_rest",
    )(ids, g, o, v)
    return outs[:na], outs[na:]


def turn_kernel(count, turned, *refs):
    pieces, outs = refs[:count], refs[count:]
    joined, parts = len(outs) == 1, pieces[0].shape[0]
    for c in range(parts):
        for p, piece in enumerate(pieces):
            if joined:
                outs[0][c * count + p if turned else p * parts + c] = piece[c]
            else:
                outs[c][p] = piece[c]


def turn(pieces, joined=False, turned=True):
    count, parts, shape = len(pieces), pieces[0].shape[0], pieces[0].shape[1:]
    out = [sds((parts * count, *shape), BF16)] if joined else [sds((count, *shape), BF16)] * parts
    outs = pl.pallas_call(
        functools.partial(turn_kernel, count, turned),
        out_shape=out,
        in_specs=[VMEM] * count,
        out_specs=[VMEM] * len(out),
        cost_estimate=lasts(0.5),
        compiler_params=within(*pieces, *pieces),
    )(*pieces)
    return outs[0] if joined else outs


def lists_kernel(plan, ids, order, live_ref, by_key, n_key, query_of, numbers):
    nz, na, nb = plan.nz, plan.na, plan.nb
    z, a, b = ids[0], ids[1], ids[2]
    true = [z ^ r for r in range(nz)]

    def at_distance(d, carry):
        for rk in range(nz):
            count = jnp.int32(0)
            for r in range(nz):
                query_of[d * nz + rk, count] = jnp.int32(r)
                count = count + (live_ref[true[r], true[rk], d] > 0).astype(jnp.int32)
            numbers[d * nz + rk] = count
        return carry

    lax.fori_loop(1, REACH, at_distance, 0)

    def key_frame(s_key, carry):
        place_key = order[(a ^ s_key) * nb + b]

        def query_frame(ts, counts):
            t = ts // na
            place = order[(a ^ (ts - t * na)) * nb + (b ^ t)]
            d = jnp.abs(place - place_key)

            def found(counts):
                counts = list(counts)
                for rk in range(nz):
                    row = d * nz + rk
                    for u in range(nz):
                        by_key[s_key * nz + rk, counts[rk] + u] = ts * nz + query_of[row, u]
                    counts[rk] = counts[rk] + numbers[row]
                return tuple(counts)

            return lax.cond((d > 0) & (d < REACH), found, lambda counts: counts, counts)

        counts = lax.fori_loop(0, na * nb, query_frame, (jnp.int32(0),) * nz)
        for rk in range(nz):
            n_key[s_key * nz + rk] = counts[rk]
        return carry

    lax.fori_loop(0, na, key_frame, 0)


def lists(plan, ids, order, live):
    own, total, nz = plan.own, plan.total, plan.nz
    return pl.pallas_call(
        functools.partial(lists_kernel, plan),
        out_shape=[sds((own, total + WIDE_GROUP + nz), jnp.int32), sds((own,), jnp.int32)],
        in_specs=[SMEM] * 3,
        out_specs=[SMEM] * 2,
        scratch_shapes=[
            pltpu.SMEM((REACH * nz, nz), jnp.int32),
            pltpu.SMEM((REACH * nz,), jnp.int32),
        ],
        cost_estimate=lasts(3),
        compiler_params=within(),
        name="lists",
    )(ids, order, live)


def picks(table, row, count, first, size):
    out = []
    for u in range(size):
        valid = first + u < count
        out.append((jnp.where(valid, table[row, first + u], 0), valid))
    return out


def steps(count, size):
    return lax.div(count + (size - 1), size)


def totals_kernel(plan, by_key, n_key, k_ref, *refs):
    parts, (out, q_ref, peaks, sums) = refs[: plan.nb], refs[plan.nb :]
    nz, na, own, rows, total = plan.nz, plan.na, plan.own, plan.rows, plan.total
    scale = HEAD_DIM**-0.5
    length = nz * rows
    for t, each in enumerate(parts):
        q_ref[t * own : (t + 1) * own] = each[...]
    peaks[own:, :] = jnp.full((peaks.shape[0] - own, rows), NEG, F32)
    sums[own:, :] = jnp.zeros((peaks.shape[0] - own, rows), F32)

    def near(s, carry):
        span = pl.ds(s * nz, nz)
        keys, q = k_ref[span].reshape(length, HEAD_DIM), q_ref[span].reshape(length, HEAD_DIM)
        scores = scale * dot(keys, q, NT)
        peak = jnp.max(scores, axis=0, keepdims=True)
        mass = jnp.sum(jnp.exp(scores - peak), axis=0, keepdims=True)
        for r in range(nz):
            peaks[pl.ds(s * nz + r, 1), :] = peak[:, r * rows : (r + 1) * rows]
            sums[pl.ds(s * nz + r, 1), :] = mass[:, r * rows : (r + 1) * rows]
        return carry

    lax.fori_loop(0, na, near, 0)

    def local(j, start):
        chosen = picks(by_key, j, n_key[j], start, WIDE_GROUP)
        places = [pl.ds(jnp.where(ok, i, total), 1) for i, ok in chosen]
        q = jnp.concatenate([q_ref[i] for i, _ in chosen], axis=0)
        scores = scale * dot(k_ref[j], q, NT)
        peak = jnp.max(scores, axis=0, keepdims=True)
        mass = jnp.sum(jnp.exp(scores - peak), axis=0, keepdims=True)
        return places, peak, mass

    def merge(places, peak, mass):
        old_peak = jnp.concatenate([peaks[place, :] for place in places], axis=1)
        old_mass = jnp.concatenate([sums[place, :] for place in places], axis=1)
        new_peak = jnp.maximum(old_peak, peak)
        new_mass = old_mass * jnp.exp(old_peak - new_peak) + mass * jnp.exp(peak - new_peak)
        for u, place in enumerate(places):
            peaks[place, :] = new_peak[:, u * rows : (u + 1) * rows]
            sums[place, :] = new_mass[:, u * rows : (u + 1) * rows]

    def away(m, carry):
        for found in [local(m * TOGETHER + u, 0) for u in range(TOGETHER)]:
            merge(*found)
        return carry

    lax.fori_loop(0, own // TOGETHER, away, 0)

    def rest(j, carry):
        def group(step, carry):
            merge(*local(j, step * WIDE_GROUP))
            return carry

        return lax.fori_loop(1, steps(n_key[j], WIDE_GROUP), group, carry)

    lax.fori_loop(0, own, rest, 0)
    peak = peaks[:total, :]
    out[...] = jnp.where(peak > 0.5 * NEG, peak + jnp.log(sums[:total, :]), NEG)


def totals(plan, by_key, n_key, keys, queries):
    return pl.pallas_call(
        functools.partial(totals_kernel, plan),
        out_shape=[
            sds((plan.total, plan.rows), F32),
            sds((plan.total, plan.rows, HEAD_DIM), BF16),
        ],
        in_specs=[SMEM, SMEM, VMEM] + [VMEM] * plan.nb,
        out_specs=[VMEM] * 2,
        scratch_shapes=[pltpu.VMEM((plan.total + 8, plan.rows), F32)] * 2,
        cost_estimate=lasts(6),
        compiler_params=within(keys, *queries, *queries),
        name="totals",
    )(by_key, n_key, keys, *queries)


def rows_kernel(plan, *refs):
    nb, own, rows = plan.nb, plan.own, plan.rows
    g_refs, parts, (lse_all, delta_all, g_all) = refs[:nb], refs[nb : 2 * nb], refs[2 * nb :]
    for t in range(nb):
        rivals = [parts[u][pl.ds((t ^ u) * own, own), :] for u in range(nb)]
        peak = functools.reduce(jnp.maximum, rivals)
        lse_all[pl.ds(t * own, own), :] = peak + jnp.log(sum(jnp.exp(x - peak) for x in rivals))
        for m in range(own):
            extra = g_refs[t][m, rows:].astype(F32)
            delta_all[t * own + m : t * own + m + 1, :] = jnp.sum(extra, axis=0, keepdims=True)
            g_all[t * own + m] = g_refs[t][m, :rows]


def query_rows(plan, out_grads, parts):
    return pl.pallas_call(
        functools.partial(rows_kernel, plan),
        out_shape=[sds((plan.total, plan.rows), F32)] * 2
        + [sds((plan.total, plan.rows, HEAD_DIM), BF16)],
        in_specs=[VMEM] * (2 * plan.nb),
        out_specs=[VMEM] * 3,
        cost_estimate=lasts(1),
        compiler_params=within(*out_grads, *out_grads),
        name="query_rows",
    )(*out_grads, *parts)


def grads_kernel(plan, span, first, last, by_key, n_key, q_ref, g_ref, lse_ref, delta_ref, k_ref, *refs):
    nz, na, nb, own, rows = plan.nz, plan.na, plan.nb, plan.own, plan.rows
    hd = HEAD_DIM
    scale = hd**-0.5
    length = nz * rows
    width = len(span)
    refs = list(refs)
    take = lambda n: [refs.pop(0) for _ in range(n)]
    v_refs = take(width)
    if not first:
        (dq_before,) = take(1)
    kv_outs = take(na)
    dq_outs = take(nb if last else 1)
    dk_all, dv_all = take(2)
    dq_all = refs.pop(0) if last else dq_outs[0]

    def begin(i, carry):
        dq_all[i] = jnp.zeros((rows, hd), F32) if first else dq_before[i]
        return carry

    lax.fori_loop(own if first else 0, plan.total, begin, 0)

    def wide_row(ref, start):
        return jnp.concatenate([ref[pl.ds(start + r, 1), :] for r in range(nz)], axis=1)

    def diagonal(s, carry):
        frame = pl.ds(s * nz, nz)
        k = jnp.concatenate([k_ref[s * nz + r] for r in span], axis=0)
        v = jnp.concatenate([v_ref[s] for v_ref in v_refs], axis=0)
        q, g = q_ref[frame].reshape(length, hd), g_ref[frame].reshape(length, hd)
        lse, delta = wide_row(lse_ref, s * nz), wide_row(delta_ref, s * nz)
        probs = jnp.exp(scale * dot(k, q, NT) - lse)
        dv = dot(probs.astype(BF16), g, NN)
        grad_scores = (probs * (dot(v, g, NT) - delta)).astype(BF16)
        dk = dot(grad_scores, q, NN)
        dq = dot(grad_scores, k, TN).reshape(nz, rows, hd)
        for x in range(width):
            dv_all[s * width + x] = dv[x * rows : (x + 1) * rows]
            dk_all[s * width + x] = dk[x * rows : (x + 1) * rows]
        if first:
            dq_all[frame] = dq
        else:
            dq_all[frame] += dq
        return carry

    lax.fori_loop(0, na, diagonal, 0)

    def terms(s, x, j, start):
        k, v = k_ref[j], v_refs[x][s]
        chosen = picks(by_key, j, n_key[j], start, KEY_GROUP)
        q = jnp.concatenate([q_ref[i] for i, _ in chosen], axis=0)
        g = jnp.concatenate([g_ref[i] for i, _ in chosen], axis=0)
        lse = jnp.concatenate([jnp.where(ok, lse_ref[pl.ds(i, 1), :], -NEG) for i, ok in chosen], axis=1)
        delta = jnp.concatenate([delta_ref[pl.ds(i, 1), :] for i, _ in chosen], axis=1)
        probs = jnp.exp(scale * dot(k, q, NT) - lse)
        dv = dot(probs.astype(BF16), g, NN)
        grad_scores = (probs * (dot(v, g, NT) - delta)).astype(BF16)
        dk = dot(grad_scores, q, NN)
        return chosen, dv, dk, dot(grad_scores, k, TN)

    def add(s, x, found):
        chosen, dv, dk, dq = found
        dv_all[s * width + x] += dv
        dk_all[s * width + x] += dk
        for u, (i, _) in enumerate(chosen):
            dq_all[i] += dq[u * rows : (u + 1) * rows]

    def away(s, carry):
        for x, found in [(x, terms(s, x, s * nz + r, 0)) for x, r in enumerate(span)]:
            add(s, x, found)
        for x, r in enumerate(span):

            def group(step, carry, x=x, r=r):
                add(s, x, terms(s, x, s * nz + r, step * KEY_GROUP))
                return carry

            lax.fori_loop(1, steps(n_key[s * nz + r], KEY_GROUP), group, 0)
        return carry

    lax.fori_loop(0, na, away, 0)

    for s, out in enumerate(kv_outs):
        for x in range(width):
            out[0, x] = (scale * dk_all[s * width + x]).astype(BF16)
            out[1, x] = dv_all[s * width + x].astype(BF16)
    if last:
        for t in range(nb):

            def drain(m, carry, t=t):
                dq_outs[t][m] = scale * dq_all[t * own + m]
                return carry

            lax.fori_loop(0, own, drain, 0)


def grads(plan, span, tables, queries, out_grads, lse, delta, keys, values, dq_before, last):
    nb, na, own, rows, total = plan.nb, plan.na, plan.own, plan.rows, plan.total
    hd, width, first = HEAD_DIM, len(span), dq_before is None
    kv = [sds((2, width, rows, hd), BF16)] * na
    dq = [sds((own, rows, hd), F32)] * nb if last else [sds((total, rows, hd), F32)]
    before = [] if first else [dq_before]
    partial = sds((own, rows, hd), F32)
    outs = pl.pallas_call(
        functools.partial(grads_kernel, plan, span, first, last),
        out_shape=kv + dq,
        in_specs=[SMEM] * 2 + [VMEM] * (5 + width + len(before)),
        out_specs=[VMEM] * (na + len(dq)),
        scratch_shapes=[pltpu.VMEM((na * width, rows, hd), F32)] * 2
        + ([pltpu.VMEM((total, rows, hd), F32)] if last else []),
        cost_estimate=lasts(7),
        compiler_params=within(queries, out_grads, keys, keys, *[partial] * (4 + 3 * nb)),
    )(*tables, queries, out_grads, lse, delta, keys, *values, *before)
    return outs[:na], outs[na:]


def pack_kernel(plan, *refs):
    nb, nz = plan.nb, plan.nz
    for s, out in enumerate(refs[nb:]):
        for r in range(nz):
            out[0, r] = sum(ref[s * nz + r] for ref in refs[:nb]).astype(BF16)


def pack(plan, partials):
    return pl.pallas_call(
        functools.partial(pack_kernel, plan),
        out_shape=[sds((1, plan.nz, plan.rows, HEAD_DIM), BF16)] * plan.na,
        in_specs=[VMEM] * plan.nb,
        out_specs=[VMEM] * plan.na,
        cost_estimate=lasts(1),
        compiler_params=within(*partials, *partials),
        name="pack",
    )(*partials)


def assemble_kernel(plan, spans, n, ids, *refs):
    na, rows, hd = plan.na, plan.rows, HEAD_DIM
    refs = list(refs)
    outs = refs[na * len(spans) :]
    for span in spans:
        for s in range(na):
            piece = refs.pop(0)
            cols = pl.ds(pl.multiple_of((ids[1] ^ s) * hd, hd), hd)
            for w in range(n):
                for x, r in enumerate(span):
                    place = pl.ds(pl.multiple_of((ids[0] ^ r) * rows, rows), rows)
                    outs[w][place, cols] = piece[w, x]


def assemble(plan, ids, spans, groups):
    n = groups[0][0].shape[0]
    pieces = [piece for group in groups for piece in group]
    return pl.pallas_call(
        functools.partial(assemble_kernel, plan, spans, n),
        out_shape=[sds((plan.nz * plan.rows, plan.na * HEAD_DIM), BF16)] * n,
        in_specs=[SMEM] + [VMEM] * len(pieces),
        out_specs=[VMEM] * n,
        cost_estimate=lasts(1.5),
        compiler_params=within(*pieces, *pieces),
    )(ids, *pieces)


def local(queries, key_states, value_states, attn_out, grad_out, frame_order, block_live):
    plan = Plan(queries.shape[0])
    nz, na, nb = plan.nz, plan.na, plan.nb
    slot = lax.axis_index("frame")
    ids = jnp.stack([lax.axis_index("head"), slot // nb, slot % nb]).astype(jnp.int32)

    def staged(order, pieces, send):
        moved = {}
        for step in order:
            moved[step] = send(pieces[step], step)
        return [pieces[0]] + [moved[step] for step in range(1, len(pieces))]

    def head_stage(pieces):
        return staged([*range(2, nz), 1], pieces, over_head)

    def frame_stage(pieces):
        return staged(range(na - 1, 0, -1), pieces, lambda x, s: over_frame(x, s * nb))

    def swapped(parts):
        return staged(range(1, nb), parts, over_frame)

    q_sent = head_stage(prep(plan, ids, queries, True))
    k_near = frame_stage(prep(plan, ids, key_states, False))
    g_near, v_near = prep_rest(plan, ids, grad_out, attn_out, value_states)
    g_near = frame_stage(g_near)
    v_near = frame_stage(v_near)
    by_key, n_key = lists(plan, ids, frame_order, block_live.transpose(1, 2, 0))
    g_own = turn(head_stage(turn(g_near)), joined=True)
    values = head_stage(turn(v_near))
    keys = turn(head_stage(turn(k_near)), joined=True)
    q_near = frame_stage(turn(q_sent))
    q_own = turn(q_near, joined=True, turned=False)
    lse_part, q_all = totals(plan, by_key, n_key, keys, swapped([q_own] * nb))
    lse, delta, g_all = query_rows(plan, swapped([g_own] * nb), swapped([lse_part] * nb))
    spans = [range(0, 2), range(2, nz)]
    kv_home, dq = [], None
    for place, span in enumerate(spans):
        last = place == len(spans) - 1
        kv, dq_parts = grads(
            plan, span, (by_key, n_key), q_all, g_all, lse, delta, keys,
            [values[r] for r in span], dq, last,
        )
        dq = dq_parts[0]
        kv_home.append(frame_stage(kv))
    dq_home = frame_stage(pack(plan, swapped(dq_parts)))
    grad_key, grad_value = assemble(plan, ids, spans, kv_home)
    (grad_query,) = assemble(plan, ids, [range(nz)], [dq_home])
    return grad_query, grad_key, grad_value


def solution(mesh):
    rows = P(("frame", "head"), None)
    in_specs = (rows,) * 5 + (P(), P())
    out_specs = (P("frame", "head"),) * 3
    return jax.shard_map(local, mesh=mesh, in_specs=in_specs, out_specs=out_specs, check_vma=False)
```

```python
import functools
import math

import jax
import jax.numpy as jnp
from jax import lax
from jax.experimental import pallas as pl
from jax.experimental.pallas import tpu as pltpu
from jax.sharding import PartitionSpec as P


HEADS = 16
HEAD_DIM = 128
NEG = -1e30
KEY_GROUP = 4
WIDE_GROUP = 6
TOGETHER = 4
REACH = 4
EXTRA = 8


VMEM = pl.BlockSpec(memory_space=pltpu.VMEM)
SMEM = pl.BlockSpec(memory_space=pltpu.SMEM)
HBM = pl.BlockSpec(memory_space=pltpu.HBM)
F32 = jnp.float32
BF16 = jnp.bfloat16
NT = (((1,), (1,)), ((), ()))
TN = (((0,), (0,)), ((), ()))
NN = (((1,), (0,)), ((), ()))


def dot(a, b, dims):
    return lax.dot_general(a, b, dims, preferred_element_type=F32)


def sds(shape, dtype):
    return jax.ShapeDtypeStruct(shape, dtype)


def lasts(microseconds):
    return pl.CostEstimate(flops=0, bytes_accessed=int(microseconds * 3.5e6), transcendentals=0)


def within(*shapes):
    held = sum(math.prod(s.shape) * s.dtype.itemsize for s in shapes)
    return pltpu.CompilerParams(vmem_limit_bytes=int(held * 5 // 4) + (6 << 20))


class Plan:
    def __init__(self, rows):
        self.nz = lax.axis_size("head")
        self.nf = lax.axis_size("frame")
        self.hh = HEADS // self.nz
        self.na = min(self.hh, self.nf)
        self.nb = self.nf // self.na
        self.rows = rows
        self.own = self.na * self.nz
        self.total = self.own * self.nb
        assert self.hh == self.na and rows == HEAD_DIM


def over_head(value, step):
    count = lax.axis_size("head")
    return lax.ppermute(value, "head", [(i, i ^ step) for i in range(count)])


def over_frame(value, step):
    count = lax.axis_size("frame")
    return lax.ppermute(value, "frame", [(i, i ^ step) for i in range(count)])


def bundles(plan, ids, refs, bufs, sems):
    width = plan.hh * HEAD_DIM
    out = []
    for r in range(plan.nz):
        cols = pl.ds(pl.multiple_of((ids[0] ^ r) * width, width), width)
        for w, (ref, buf) in enumerate(zip(refs, bufs)):
            out.append(pltpu.make_async_copy(ref.at[:, cols], buf.at[r], sems.at[w, r]))
    for copy in out:
        copy.start()
    return out


def within_bundle(ids, s):
    return pl.ds(pl.multiple_of((ids[1] ^ s) * HEAD_DIM, HEAD_DIM), HEAD_DIM)


def prep_kernel(plan, q_ref, k_ref, out):
    hd, rows = HEAD_DIM, plan.rows
    for a in range(plan.na):
        for z in range(plan.nz):
            head, place = z * plan.hh + a, a * plan.nz + z
            out[place, :rows] = q_ref[:, head * hd : (head + 1) * hd]
            out[place, rows:] = k_ref[:, head * hd : (head + 1) * hd]


def prep(plan, q, k):
    return pl.pallas_call(
        functools.partial(prep_kernel, plan),
        out_shape=sds((plan.own, 2 * plan.rows, HEAD_DIM), BF16),
        in_specs=[VMEM] * 2,
        out_specs=VMEM,
        cost_estimate=lasts(1.5),
        compiler_params=pltpu.CompilerParams(vmem_limit_bytes=60 << 20),
        name="prep",
    )(q, k)


def part_kernel(plan, ids, x_ref, q_out, k_out):
    rows = plan.rows
    for s in range(plan.na):
        for r in range(plan.nz):
            place = (ids[1] ^ s) * plan.nz + (ids[0] ^ r)
            q_out[s * plan.nz + r] = x_ref[place, :rows]
            k_out[s * plan.nz + r] = x_ref[place, rows:]


def part(plan, ids, x):
    return pl.pallas_call(
        functools.partial(part_kernel, plan),
        out_shape=[sds((plan.own, plan.rows, HEAD_DIM), BF16)] * 2,
        in_specs=[SMEM, VMEM],
        out_specs=[VMEM] * 2,
        cost_estimate=lasts(1),
        compiler_params=within(x, x),
        name="part",
    )(ids, x)


def prep_rest_kernel(plan, ids, g_ref, o_ref, v_ref, *refs):
    na, rows = plan.na, plan.rows
    g_outs, v_outs, bufs, sems = refs[:na], refs[na : 2 * na], refs[2 * na : 2 * na + 3], refs[-1]
    copies = bundles(plan, ids, [g_ref, o_ref, v_ref], bufs, sems)
    ones = jnp.ones((EXTRA, HEAD_DIM), BF16)
    row = lax.broadcasted_iota(jnp.int32, (EXTRA, rows), 0)
    for r in range(plan.nz):
        for copy in copies[3 * r : 3 * r + 3]:
            copy.wait()
        for s in range(na):
            cols = within_bundle(ids, s)
            grad = bufs[0][r, :, cols]
            g_outs[s][r, :rows] = grad
            v_outs[s][r] = bufs[2][r, :, cols]
            product = grad.astype(F32) * bufs[1][r, :, cols].astype(F32)
            high = product.astype(BF16)
            low = (product - high.astype(F32)).astype(BF16)
            delta = dot(ones, high, NT) + dot(ones, low, NT)
            first = delta.astype(BF16).astype(F32)
            rest = delta - first
            second = rest.astype(BF16).astype(F32)
            parts = jnp.where(row == 2, rest - second, 0.0)
            parts = jnp.where(row == 0, first, jnp.where(row == 1, second, parts))
            g_outs[s][r, rows:] = parts.astype(BF16)


def prep_rest(plan, ids, g, o, v):
    na, nz, rows, hd = plan.na, plan.nz, plan.rows, HEAD_DIM
    outs = pl.pallas_call(
        functools.partial(prep_rest_kernel, plan),
        out_shape=[sds((nz, rows + EXTRA, hd), BF16)] * na + [sds((nz, rows, hd), BF16)] * na,
        in_specs=[SMEM] + [HBM] * 3,
        out_specs=[VMEM] * (2 * na),
        scratch_shapes=[pltpu.VMEM((nz, rows, plan.hh * hd), BF16)] * 3
        + [pltpu.SemaphoreType.DMA((3, nz))],
        cost_estimate=lasts(2),
        compiler_params=within(g, o, v, g, v),
        name="prep_rest",
    )(ids, g, o, v)
    return outs[:na], outs[na:]


def turn_kernel(count, *refs):
    pieces, outs = refs[:count], refs[count:]
    joined = len(outs) == 1
    for c in range(pieces[0].shape[0]):
        for p, piece in enumerate(pieces):
            if joined:
                outs[0][c * count + p] = piece[c]
            else:
                outs[c][p] = piece[c]


def turn(pieces, joined=False):
    count, parts, shape = len(pieces), pieces[0].shape[0], pieces[0].shape[1:]
    out = [sds((parts * count, *shape), BF16)] if joined else [sds((count, *shape), BF16)] * parts
    outs = pl.pallas_call(
        functools.partial(turn_kernel, count),
        out_shape=out,
        in_specs=[VMEM] * count,
        out_specs=[VMEM] * len(out),
        cost_estimate=lasts(0.5),
        compiler_params=within(*pieces, *pieces),
    )(*pieces)
    return outs[0] if joined else outs


def lists_kernel(plan, ids, order, live_ref, by_key, n_key, query_of, numbers):
    nz, na, nb = plan.nz, plan.na, plan.nb
    z, a, b = ids[0], ids[1], ids[2]
    true = [z ^ r for r in range(nz)]

    def at_distance(d, carry):
        for rk in range(nz):
            count = jnp.int32(0)
            for r in range(nz):
                query_of[d * nz + rk, count] = jnp.int32(r)
                count = count + (live_ref[true[r], true[rk], d] > 0).astype(jnp.int32)
            numbers[d * nz + rk] = count
        return carry

    lax.fori_loop(1, REACH, at_distance, 0)

    def key_frame(s_key, carry):
        place_key = order[(a ^ s_key) * nb + b]

        def query_frame(ts, counts):
            t = ts // na
            place = order[(a ^ (ts - t * na)) * nb + (b ^ t)]
            d = jnp.abs(place - place_key)

            def found(counts):
                counts = list(counts)
                for rk in range(nz):
                    row = d * nz + rk
                    for u in range(nz):
                        by_key[s_key * nz + rk, counts[rk] + u] = ts * nz + query_of[row, u]
                    counts[rk] = counts[rk] + numbers[row]
                return tuple(counts)

            return lax.cond((d > 0) & (d < REACH), found, lambda counts: counts, counts)

        counts = lax.fori_loop(0, na * nb, query_frame, (jnp.int32(0),) * nz)
        for rk in range(nz):
            n_key[s_key * nz + rk] = counts[rk]
        return carry

    lax.fori_loop(0, na, key_frame, 0)


def lists(plan, ids, order, live):
    own, total, nz = plan.own, plan.total, plan.nz
    return pl.pallas_call(
        functools.partial(lists_kernel, plan),
        out_shape=[sds((own, total + WIDE_GROUP + nz), jnp.int32), sds((own,), jnp.int32)],
        in_specs=[SMEM] * 3,
        out_specs=[SMEM] * 2,
        scratch_shapes=[
            pltpu.SMEM((REACH * nz, nz), jnp.int32),
            pltpu.SMEM((REACH * nz,), jnp.int32),
        ],
        cost_estimate=lasts(3),
        compiler_params=within(),
        name="lists",
    )(ids, order, live)


def picks(table, row, count, first, size):
    out = []
    for u in range(size):
        valid = first + u < count
        out.append((jnp.where(valid, table[row, first + u], 0), valid))
    return out


def steps(count, size):
    return lax.div(count + (size - 1), size)


def totals_kernel(plan, by_key, n_key, k_ref, *refs):
    parts, (out, q_ref, peaks, sums) = refs[: plan.nb], refs[plan.nb :]
    nz, na, own, rows, total = plan.nz, plan.na, plan.own, plan.rows, plan.total
    scale = HEAD_DIM**-0.5
    length = nz * rows
    for t, each in enumerate(parts):
        q_ref[t * own : (t + 1) * own] = each[...]
    peaks[own:, :] = jnp.full((peaks.shape[0] - own, rows), NEG, F32)
    sums[own:, :] = jnp.zeros((peaks.shape[0] - own, rows), F32)

    def near(s, carry):
        span = pl.ds(s * nz, nz)
        keys, q = k_ref[span].reshape(length, HEAD_DIM), q_ref[span].reshape(length, HEAD_DIM)
        scores = scale * dot(keys, q, NT)
        peak = jnp.max(scores, axis=0, keepdims=True)
        mass = jnp.sum(jnp.exp(scores - peak), axis=0, keepdims=True)
        for r in range(nz):
            peaks[pl.ds(s * nz + r, 1), :] = peak[:, r * rows : (r + 1) * rows]
            sums[pl.ds(s * nz + r, 1), :] = mass[:, r * rows : (r + 1) * rows]
        return carry

    lax.fori_loop(0, na, near, 0)

    def local(j, start):
        chosen = picks(by_key, j, n_key[j], start, WIDE_GROUP)
        places = [pl.ds(jnp.where(ok, i, total), 1) for i, ok in chosen]
        q = jnp.concatenate([q_ref[i] for i, _ in chosen], axis=0)
        scores = scale * dot(k_ref[j], q, NT)
        peak = jnp.max(scores, axis=0, keepdims=True)
        mass = jnp.sum(jnp.exp(scores - peak), axis=0, keepdims=True)
        return places, peak, mass

    def merge(places, peak, mass):
        old_peak = jnp.concatenate([peaks[place, :] for place in places], axis=1)
        old_mass = jnp.concatenate([sums[place, :] for place in places], axis=1)
        new_peak = jnp.maximum(old_peak, peak)
        new_mass = old_mass * jnp.exp(old_peak - new_peak) + mass * jnp.exp(peak - new_peak)
        for u, place in enumerate(places):
            peaks[place, :] = new_peak[:, u * rows : (u + 1) * rows]
            sums[place, :] = new_mass[:, u * rows : (u + 1) * rows]

    def away(m, carry):
        for found in [local(m * TOGETHER + u, 0) for u in range(TOGETHER)]:
            merge(*found)
        return carry

    lax.fori_loop(0, own // TOGETHER, away, 0)

    def rest(j, carry):
        def group(step, carry):
            merge(*local(j, step * WIDE_GROUP))
            return carry

        return lax.fori_loop(1, steps(n_key[j], WIDE_GROUP), group, carry)

    lax.fori_loop(0, own, rest, 0)
    peak = peaks[:total, :]
    out[...] = jnp.where(peak > 0.5 * NEG, peak + jnp.log(sums[:total, :]), NEG)


def totals(plan, by_key, n_key, keys, queries):
    return pl.pallas_call(
        functools.partial(totals_kernel, plan),
        out_shape=[
            sds((plan.total, plan.rows), F32),
            sds((plan.total, plan.rows, HEAD_DIM), BF16),
        ],
        in_specs=[SMEM, SMEM, VMEM] + [VMEM] * plan.nb,
        out_specs=[VMEM] * 2,
        scratch_shapes=[pltpu.VMEM((plan.total + 8, plan.rows), F32)] * 2,
        cost_estimate=lasts(6),
        compiler_params=within(keys, *queries, *queries),
        name="totals",
    )(by_key, n_key, keys, *queries)


def rows_kernel(plan, *refs):
    nb, own, rows = plan.nb, plan.own, plan.rows
    g_refs, parts, (lse_all, delta_all, g_all) = refs[:nb], refs[nb : 2 * nb], refs[2 * nb :]
    for t in range(nb):
        rivals = [parts[u][pl.ds((t ^ u) * own, own), :] for u in range(nb)]
        peak = functools.reduce(jnp.maximum, rivals)
        lse_all[pl.ds(t * own, own), :] = peak + jnp.log(sum(jnp.exp(x - peak) for x in rivals))
        for m in range(own):
            extra = g_refs[t][m, rows:].astype(F32)
            delta_all[t * own + m : t * own + m + 1, :] = jnp.sum(extra, axis=0, keepdims=True)
            g_all[t * own + m] = g_refs[t][m, :rows]


def query_rows(plan, out_grads, parts):
    return pl.pallas_call(
        functools.partial(rows_kernel, plan),
        out_shape=[sds((plan.total, plan.rows), F32)] * 2
        + [sds((plan.total, plan.rows, HEAD_DIM), BF16)],
        in_specs=[VMEM] * (2 * plan.nb),
        out_specs=[VMEM] * 3,
        cost_estimate=lasts(1),
        compiler_params=within(*out_grads, *out_grads),
        name="query_rows",
    )(*out_grads, *parts)


def grads_kernel(plan, span, first, last, by_key, n_key, q_ref, g_ref, lse_ref, delta_ref, k_ref, *refs):
    nz, na, nb, own, rows = plan.nz, plan.na, plan.nb, plan.own, plan.rows
    hd = HEAD_DIM
    scale = hd**-0.5
    length = nz * rows
    width = len(span)
    refs = list(refs)
    take = lambda n: [refs.pop(0) for _ in range(n)]
    v_refs = take(width)
    if not first:
        (dq_before,) = take(1)
    kv_outs = take(na)
    dq_outs = take(nb if last else 1)
    dk_all, dv_all = take(2)
    dq_all = refs.pop(0) if last else dq_outs[0]

    def begin(i, carry):
        dq_all[i] = jnp.zeros((rows, hd), F32) if first else dq_before[i]
        return carry

    lax.fori_loop(own if first else 0, plan.total, begin, 0)

    def wide_row(ref, start):
        return jnp.concatenate([ref[pl.ds(start + r, 1), :] for r in range(nz)], axis=1)

    def diagonal(s, carry):
        frame = pl.ds(s * nz, nz)
        k = jnp.concatenate([k_ref[s * nz + r] for r in span], axis=0)
        v = jnp.concatenate([v_ref[s] for v_ref in v_refs], axis=0)
        q, g = q_ref[frame].reshape(length, hd), g_ref[frame].reshape(length, hd)
        lse, delta = wide_row(lse_ref, s * nz), wide_row(delta_ref, s * nz)
        probs = jnp.exp(scale * dot(k, q, NT) - lse)
        dv = dot(probs.astype(BF16), g, NN)
        grad_scores = (probs * (dot(v, g, NT) - delta)).astype(BF16)
        dk = dot(grad_scores, q, NN)
        dq = dot(grad_scores, k, TN).reshape(nz, rows, hd)
        for x in range(width):
            dv_all[s * width + x] = dv[x * rows : (x + 1) * rows]
            dk_all[s * width + x] = dk[x * rows : (x + 1) * rows]
        if first:
            dq_all[frame] = dq
        else:
            dq_all[frame] += dq
        return carry

    lax.fori_loop(0, na, diagonal, 0)

    def terms(s, x, j, start):
        k, v = k_ref[j], v_refs[x][s]
        chosen = picks(by_key, j, n_key[j], start, KEY_GROUP)
        q = jnp.concatenate([q_ref[i] for i, _ in chosen], axis=0)
        g = jnp.concatenate([g_ref[i] for i, _ in chosen], axis=0)
        lse = jnp.concatenate([jnp.where(ok, lse_ref[pl.ds(i, 1), :], -NEG) for i, ok in chosen], axis=1)
        delta = jnp.concatenate([delta_ref[pl.ds(i, 1), :] for i, _ in chosen], axis=1)
        probs = jnp.exp(scale * dot(k, q, NT) - lse)
        dv = dot(probs.astype(BF16), g, NN)
        grad_scores = (probs * (dot(v, g, NT) - delta)).astype(BF16)
        dk = dot(grad_scores, q, NN)
        return chosen, dv, dk, dot(grad_scores, k, TN)

    def add(s, x, found):
        chosen, dv, dk, dq = found
        dv_all[s * width + x] += dv
        dk_all[s * width + x] += dk
        for u, (i, _) in enumerate(chosen):
            dq_all[i] += dq[u * rows : (u + 1) * rows]

    def away(s, carry):
        for x, found in [(x, terms(s, x, s * nz + r, 0)) for x, r in enumerate(span)]:
            add(s, x, found)
        for x, r in enumerate(span):

            def group(step, carry, x=x, r=r):
                add(s, x, terms(s, x, s * nz + r, step * KEY_GROUP))
                return carry

            lax.fori_loop(1, steps(n_key[s * nz + r], KEY_GROUP), group, 0)
        return carry

    lax.fori_loop(0, na, away, 0)

    for s, out in enumerate(kv_outs):
        for x in range(width):
            out[0, x] = (scale * dk_all[s * width + x]).astype(BF16)
            out[1, x] = dv_all[s * width + x].astype(BF16)
    if last:
        for t in range(nb):

            def drain(m, carry, t=t):
                dq_outs[t][m] = scale * dq_all[t * own + m]
                return carry

            lax.fori_loop(0, own, drain, 0)


def grads(plan, span, tables, queries, out_grads, lse, delta, keys, values, dq_before, last):
    nb, na, own, rows, total = plan.nb, plan.na, plan.own, plan.rows, plan.total
    hd, width, first = HEAD_DIM, len(span), dq_before is None
    kv = [sds((2, width, rows, hd), BF16)] * na
    dq = [sds((own, rows, hd), F32)] * nb if last else [sds((total, rows, hd), F32)]
    before = [] if first else [dq_before]
    partial = sds((own, rows, hd), F32)
    outs = pl.pallas_call(
        functools.partial(grads_kernel, plan, span, first, last),
        out_shape=kv + dq,
        in_specs=[SMEM] * 2 + [VMEM] * (5 + width + len(before)),
        out_specs=[VMEM] * (na + len(dq)),
        scratch_shapes=[pltpu.VMEM((na * width, rows, hd), F32)] * 2
        + ([pltpu.VMEM((total, rows, hd), F32)] if last else []),
        cost_estimate=lasts(7),
        compiler_params=within(queries, out_grads, keys, keys, *[partial] * (4 + 3 * nb)),
    )(*tables, queries, out_grads, lse, delta, keys, *values, *before)
    return outs[:na], outs[na:]


def pack_kernel(plan, *refs):
    nb, nz = plan.nb, plan.nz
    for s, out in enumerate(refs[nb:]):
        for r in range(nz):
            out[0, r] = sum(ref[s * nz + r] for ref in refs[:nb]).astype(BF16)


def pack(plan, partials):
    return pl.pallas_call(
        functools.partial(pack_kernel, plan),
        out_shape=[sds((1, plan.nz, plan.rows, HEAD_DIM), BF16)] * plan.na,
        in_specs=[VMEM] * plan.nb,
        out_specs=[VMEM] * plan.na,
        cost_estimate=lasts(1),
        compiler_params=within(*partials, *partials),
        name="pack",
    )(*partials)


def assemble_kernel(plan, spans, n, ids, *refs):
    na, rows, hd = plan.na, plan.rows, HEAD_DIM
    pieces, outs, sems = refs[: na * len(spans)], refs[na * len(spans) : -1], refs[-1]
    copies = []
    for g, span in enumerate(spans):
        for s in range(na):
            cols = pl.ds(pl.multiple_of((ids[1] ^ s) * hd, hd), hd)
            for w in range(n):
                for x, r in enumerate(span):
                    place = pl.ds(pl.multiple_of((ids[0] ^ r) * rows, rows), rows)
                    source = pieces[g * na + s].at[w, x]
                    copies.append(
                        pltpu.make_async_copy(source, outs[w].at[place, cols], sems.at[w, r, s])
                    )
    for copy in copies:
        copy.start()
    for copy in copies:
        copy.wait()


def assemble(plan, ids, spans, groups):
    n = groups[0][0].shape[0]
    pieces = [piece for group in groups for piece in group]
    return pl.pallas_call(
        functools.partial(assemble_kernel, plan, spans, n),
        out_shape=[sds((plan.nz * plan.rows, plan.na * HEAD_DIM), BF16)] * n,
        in_specs=[SMEM] + [VMEM] * len(pieces),
        out_specs=[HBM] * n,
        scratch_shapes=[pltpu.SemaphoreType.DMA((n, plan.nz, plan.na))],
        cost_estimate=lasts(1.5),
        compiler_params=within(*pieces, *pieces),
    )(ids, *pieces)


def local(queries, key_states, value_states, attn_out, grad_out, frame_order, block_live):
    plan = Plan(queries.shape[0])
    nz, na, nb = plan.nz, plan.na, plan.nb
    slot = lax.axis_index("frame")
    ids = jnp.stack([lax.axis_index("head"), slot // nb, slot % nb]).astype(jnp.int32)

    def staged(order, pieces, send):
        moved = {}
        for step in order:
            moved[step] = send(pieces[step], step)
        return [pieces[0]] + [moved[step] for step in range(1, len(pieces))]

    def head_stage(pieces):
        return staged([*range(2, nz), 1], pieces, over_head)

    def frame_stage(pieces):
        return staged(range(na - 1, 0, -1), pieces, lambda x, s: over_frame(x, s * nb))

    def swapped(parts):
        return staged(range(1, nb), parts, over_frame)

    groups = [
        [(a * nb + b) * nz + z for a in range(na) for z in range(nz)] for b in range(nb)
    ]
    mine = lax.all_to_all(
        prep(plan, queries, key_states), ("frame", "head"), 0, 0,
        tiled=True, axis_index_groups=groups,
    )
    g_near, v_near = prep_rest(plan, ids, grad_out, attn_out, value_states)
    g_near = frame_stage(g_near)
    v_near = frame_stage(v_near)
    by_key, n_key = lists(plan, ids, frame_order, block_live.transpose(1, 2, 0))
    g_own = turn(head_stage(turn(g_near)), joined=True)
    values = head_stage(turn(v_near))
    q_own, keys = part(plan, ids, mine)
    lse_part, q_all = totals(plan, by_key, n_key, keys, swapped([q_own] * nb))
    lse, delta, g_all = query_rows(plan, swapped([g_own] * nb), swapped([lse_part] * nb))
    spans = [range(0, 2), range(2, nz)]
    kv_home, dq = [], None
    for place, span in enumerate(spans):
        last = place == len(spans) - 1
        kv, dq_parts = grads(
            plan, span, (by_key, n_key), q_all, g_all, lse, delta, keys,
            [values[r] for r in span], dq, last,
        )
        dq = dq_parts[0]
        kv_home.append(frame_stage(kv))
    dq_home = frame_stage(pack(plan, swapped(dq_parts)))
    grad_key, grad_value = assemble(plan, ids, spans, kv_home)
    (grad_query,) = assemble(plan, ids, [range(nz)], [dq_home])
    return grad_query, grad_key, grad_value


def solution(mesh):
    rows = P(("frame", "head"), None)
    in_specs = (rows,) * 5 + (P(), P())
    out_specs = (P("frame", "head"),) * 3
    return jax.shard_map(local, mesh=mesh, in_specs=in_specs, out_specs=out_specs, check_vma=False)
```

```python
import functools
import math

import jax
import jax.numpy as jnp
from jax import lax
from jax.experimental import pallas as pl
from jax.experimental.pallas import tpu as pltpu
from jax.sharding import PartitionSpec as P


HEADS = 16
HEAD_DIM = 128
NEG = -1e30
KEY_GROUP = 4
WIDE_GROUP = 6
TOGETHER = 4
REACH = 4
EXTRA = 8


VMEM = pl.BlockSpec(memory_space=pltpu.VMEM)
SMEM = pl.BlockSpec(memory_space=pltpu.SMEM)
HBM = pl.BlockSpec(memory_space=pltpu.HBM)
F32 = jnp.float32
BF16 = jnp.bfloat16
NT = (((1,), (1,)), ((), ()))
TN = (((0,), (0,)), ((), ()))
NN = (((1,), (0,)), ((), ()))


def dot(a, b, dims):
    return lax.dot_general(a, b, dims, preferred_element_type=F32)


def sds(shape, dtype):
    return jax.ShapeDtypeStruct(shape, dtype)


def lasts(microseconds):
    return pl.CostEstimate(flops=0, bytes_accessed=int(microseconds * 3.5e6), transcendentals=0)


def within(*shapes):
    held = sum(math.prod(s.shape) * s.dtype.itemsize for s in shapes)
    return pltpu.CompilerParams(vmem_limit_bytes=int(held * 5 // 4) + (6 << 20))


class Plan:
    def __init__(self, rows):
        self.nz = lax.axis_size("head")
        self.nf = lax.axis_size("frame")
        self.hh = HEADS // self.nz
        self.na = min(self.hh, self.nf)
        self.nb = self.nf // self.na
        self.rows = rows
        self.own = self.na * self.nz
        self.total = self.own * self.nb
        assert self.hh == self.na and rows == HEAD_DIM


def over_head(value, step):
    count = lax.axis_size("head")
    return lax.ppermute(value, "head", [(i, i ^ step) for i in range(count)])


def over_frame(value, step):
    count = lax.axis_size("frame")
    return lax.ppermute(value, "frame", [(i, i ^ step) for i in range(count)])


def bundles(plan, ids, refs, bufs, sems):
    width = plan.hh * HEAD_DIM
    out = []
    for r in range(plan.nz):
        cols = pl.ds(pl.multiple_of((ids[0] ^ r) * width, width), width)
        for w, (ref, buf) in enumerate(zip(refs, bufs)):
            out.append(pltpu.make_async_copy(ref.at[:, cols], buf.at[r], sems.at[w, r]))
    for copy in out:
        copy.start()
    return out


def within_bundle(ids, s):
    return pl.ds(pl.multiple_of((ids[1] ^ s) * HEAD_DIM, HEAD_DIM), HEAD_DIM)


def prep_kernel(plan, q_ref, k_ref, out):
    hd, rows = HEAD_DIM, plan.rows
    for a in range(plan.na):
        for z in range(plan.nz):
            head, place = z * plan.hh + a, a * plan.nz + z
            out[place, :rows] = q_ref[:, head * hd : (head + 1) * hd]
            out[place, rows:] = k_ref[:, head * hd : (head + 1) * hd]


def prep(plan, q, k):
    return pl.pallas_call(
        functools.partial(prep_kernel, plan),
        out_shape=sds((plan.own, 2 * plan.rows, HEAD_DIM), BF16),
        in_specs=[VMEM] * 2,
        out_specs=VMEM,
        cost_estimate=lasts(1.5),
        compiler_params=pltpu.CompilerParams(vmem_limit_bytes=60 << 20),
        name="prep",
    )(q, k)


def part_kernel(plan, ids, x_ref, q_out, k_out):
    rows = plan.rows
    for s in range(plan.na):
        for r in range(plan.nz):
            place = (ids[1] ^ s) * plan.nz + (ids[0] ^ r)
            q_out[s * plan.nz + r] = x_ref[place, :rows]
            k_out[s * plan.nz + r] = x_ref[place, rows:]


def part(plan, ids, x):
    return pl.pallas_call(
        functools.partial(part_kernel, plan),
        out_shape=[sds((plan.own, plan.rows, HEAD_DIM), BF16)] * 2,
        in_specs=[SMEM, VMEM],
        out_specs=[VMEM] * 2,
        cost_estimate=lasts(1),
        compiler_params=within(x, x),
        name="part",
    )(ids, x)


def prep_rest_kernel(plan, ids, g_ref, o_ref, v_ref, *refs):
    na, rows = plan.na, plan.rows
    g_outs, v_outs, bufs, sems = refs[:na], refs[na : 2 * na], refs[2 * na : 2 * na + 3], refs[-1]
    copies = bundles(plan, ids, [g_ref, o_ref, v_ref], bufs, sems)
    ones = jnp.ones((EXTRA, HEAD_DIM), BF16)
    row = lax.broadcasted_iota(jnp.int32, (EXTRA, rows), 0)
    for r in range(plan.nz):
        for copy in copies[3 * r : 3 * r + 3]:
            copy.wait()
        for s in range(na):
            cols = within_bundle(ids, s)
            grad = bufs[0][r, :, cols]
            g_outs[s][r, :rows] = grad
            v_outs[s][r] = bufs[2][r, :, cols]
            product = grad.astype(F32) * bufs[1][r, :, cols].astype(F32)
            high = product.astype(BF16)
            low = (product - high.astype(F32)).astype(BF16)
            delta = dot(ones, high, NT) + dot(ones, low, NT)
            first = delta.astype(BF16).astype(F32)
            rest = delta - first
            second = rest.astype(BF16).astype(F32)
            parts = jnp.where(row == 2, rest - second, 0.0)
            parts = jnp.where(row == 0, first, jnp.where(row == 1, second, parts))
            g_outs[s][r, rows:] = parts.astype(BF16)


def prep_rest(plan, ids, g, o, v):
    na, nz, rows, hd = plan.na, plan.nz, plan.rows, HEAD_DIM
    outs = pl.pallas_call(
        functools.partial(prep_rest_kernel, plan),
        out_shape=[sds((nz, rows + EXTRA, hd), BF16)] * na + [sds((nz, rows, hd), BF16)] * na,
        in_specs=[SMEM] + [HBM] * 3,
        out_specs=[VMEM] * (2 * na),
        scratch_shapes=[pltpu.VMEM((nz, rows, plan.hh * hd), BF16)] * 3
        + [pltpu.SemaphoreType.DMA((3, nz))],
        cost_estimate=lasts(2),
        compiler_params=within(g, o, v, g, v),
        name="prep_rest",
    )(ids, g, o, v)
    return outs[:na], outs[na:]


def turn_kernel(count, *refs):
    pieces, outs = refs[:count], refs[count:]
    joined = len(outs) == 1
    for c in range(pieces[0].shape[0]):
        for p, piece in enumerate(pieces):
            if joined:
                outs[0][c * count + p] = piece[c]
            else:
                outs[c][p] = piece[c]


def turn(pieces, joined=False):
    count, parts, shape = len(pieces), pieces[0].shape[0], pieces[0].shape[1:]
    out = [sds((parts * count, *shape), BF16)] if joined else [sds((count, *shape), BF16)] * parts
    outs = pl.pallas_call(
        functools.partial(turn_kernel, count),
        out_shape=out,
        in_specs=[VMEM] * count,
        out_specs=[VMEM] * len(out),
        cost_estimate=lasts(0.5),
        compiler_params=within(*pieces, *pieces),
    )(*pieces)
    return outs[0] if joined else outs


def lists_kernel(plan, ids, order, live_ref, by_key, n_key, query_of, numbers):
    nz, na, nb = plan.nz, plan.na, plan.nb
    z, a, b = ids[0], ids[1], ids[2]
    true = [z ^ r for r in range(nz)]

    def at_distance(d, carry):
        for rk in range(nz):
            count = jnp.int32(0)
            for r in range(nz):
                query_of[d * nz + rk, count] = jnp.int32(r)
                count = count + (live_ref[true[r], true[rk], d] > 0).astype(jnp.int32)
            numbers[d * nz + rk] = count
        return carry

    lax.fori_loop(1, REACH, at_distance, 0)

    def key_frame(s_key, carry):
        place_key = order[(a ^ s_key) * nb + b]

        def query_frame(ts, counts):
            t = ts // na
            place = order[(a ^ (ts - t * na)) * nb + (b ^ t)]
            d = jnp.abs(place - place_key)

            def found(counts):
                counts = list(counts)
                for rk in range(nz):
                    row = d * nz + rk
                    for u in range(nz):
                        by_key[s_key * nz + rk, counts[rk] + u] = ts * nz + query_of[row, u]
                    counts[rk] = counts[rk] + numbers[row]
                return tuple(counts)

            return lax.cond((d > 0) & (d < REACH), found, lambda counts: counts, counts)

        counts = lax.fori_loop(0, na * nb, query_frame, (jnp.int32(0),) * nz)
        for rk in range(nz):
            n_key[s_key * nz + rk] = counts[rk]
        return carry

    lax.fori_loop(0, na, key_frame, 0)


def lists(plan, ids, order, live):
    own, total, nz = plan.own, plan.total, plan.nz
    return pl.pallas_call(
        functools.partial(lists_kernel, plan),
        out_shape=[sds((own, total + WIDE_GROUP + nz), jnp.int32), sds((own,), jnp.int32)],
        in_specs=[SMEM] * 3,
        out_specs=[SMEM] * 2,
        scratch_shapes=[
            pltpu.SMEM((REACH * nz, nz), jnp.int32),
            pltpu.SMEM((REACH * nz,), jnp.int32),
        ],
        cost_estimate=lasts(3),
        compiler_params=within(),
        name="lists",
    )(ids, order, live)


def picks(table, row, count, first, size):
    out = []
    for u in range(size):
        valid = first + u < count
        out.append((jnp.where(valid, table[row, first + u], 0), valid))
    return out


def steps(count, size):
    return lax.div(count + (size - 1), size)


def totals_kernel(plan, by_key, n_key, k_ref, *refs):
    parts, (out, q_ref, peaks, sums) = refs[: plan.nb], refs[plan.nb :]
    nz, na, own, rows, total = plan.nz, plan.na, plan.own, plan.rows, plan.total
    scale = HEAD_DIM**-0.5
    length = nz * rows
    for t, each in enumerate(parts):
        q_ref[t * own : (t + 1) * own] = each[...]
    peaks[own:, :] = jnp.full((peaks.shape[0] - own, rows), NEG, F32)
    sums[own:, :] = jnp.zeros((peaks.shape[0] - own, rows), F32)

    def near(s, carry):
        span = pl.ds(s * nz, nz)
        keys, q = k_ref[span].reshape(length, HEAD_DIM), q_ref[span].reshape(length, HEAD_DIM)
        scores = scale * dot(keys, q, NT)
        peak = jnp.max(scores, axis=0, keepdims=True)
        mass = jnp.sum(jnp.exp(scores - peak), axis=0, keepdims=True)
        for r in range(nz):
            peaks[pl.ds(s * nz + r, 1), :] = peak[:, r * rows : (r + 1) * rows]
            sums[pl.ds(s * nz + r, 1), :] = mass[:, r * rows : (r + 1) * rows]
        return carry

    lax.fori_loop(0, na, near, 0)

    def local(j, start):
        chosen = picks(by_key, j, n_key[j], start, WIDE_GROUP)
        places = [pl.ds(jnp.where(ok, i, total), 1) for i, ok in chosen]
        q = jnp.concatenate([q_ref[i] for i, _ in chosen], axis=0)
        scores = scale * dot(k_ref[j], q, NT)
        peak = jnp.max(scores, axis=0, keepdims=True)
        mass = jnp.sum(jnp.exp(scores - peak), axis=0, keepdims=True)
        return places, peak, mass

    def merge(places, peak, mass):
        old_peak = jnp.concatenate([peaks[place, :] for place in places], axis=1)
        old_mass = jnp.concatenate([sums[place, :] for place in places], axis=1)
        new_peak = jnp.maximum(old_peak, peak)
        new_mass = old_mass * jnp.exp(old_peak - new_peak) + mass * jnp.exp(peak - new_peak)
        for u, place in enumerate(places):
            peaks[place, :] = new_peak[:, u * rows : (u + 1) * rows]
            sums[place, :] = new_mass[:, u * rows : (u + 1) * rows]

    def away(m, carry):
        for found in [local(m * TOGETHER + u, 0) for u in range(TOGETHER)]:
            merge(*found)
        return carry

    lax.fori_loop(0, own // TOGETHER, away, 0)

    def rest(j, carry):
        def group(step, carry):
            merge(*local(j, step * WIDE_GROUP))
            return carry

        return lax.fori_loop(1, steps(n_key[j], WIDE_GROUP), group, carry)

    lax.fori_loop(0, own, rest, 0)
    peak = peaks[:total, :]
    out[...] = jnp.where(peak > 0.5 * NEG, peak + jnp.log(sums[:total, :]), NEG)


def totals(plan, by_key, n_key, keys, queries):
    return pl.pallas_call(
        functools.partial(totals_kernel, plan),
        out_shape=[
            sds((plan.total, plan.rows), F32),
            sds((plan.total, plan.rows, HEAD_DIM), BF16),
        ],
        in_specs=[SMEM, SMEM, VMEM] + [VMEM] * plan.nb,
        out_specs=[VMEM] * 2,
        scratch_shapes=[pltpu.VMEM((plan.total + 8, plan.rows), F32)] * 2,
        cost_estimate=lasts(6),
        compiler_params=within(keys, *queries, *queries),
        name="totals",
    )(by_key, n_key, keys, *queries)


def rows_kernel(plan, *refs):
    nb, own, rows = plan.nb, plan.own, plan.rows
    g_refs, parts, (lse_all, delta_all, g_all) = refs[:nb], refs[nb : 2 * nb], refs[2 * nb :]
    for t in range(nb):
        rivals = [parts[u][pl.ds((t ^ u) * own, own), :] for u in range(nb)]
        peak = functools.reduce(jnp.maximum, rivals)
        lse_all[pl.ds(t * own, own), :] = peak + jnp.log(sum(jnp.exp(x - peak) for x in rivals))
        for m in range(own):
            extra = g_refs[t][m, rows:].astype(F32)
            delta_all[t * own + m : t * own + m + 1, :] = jnp.sum(extra, axis=0, keepdims=True)
            g_all[t * own + m] = g_refs[t][m, :rows]


def query_rows(plan, out_grads, parts):
    return pl.pallas_call(
        functools.partial(rows_kernel, plan),
        out_shape=[sds((plan.total, plan.rows), F32)] * 2
        + [sds((plan.total, plan.rows, HEAD_DIM), BF16)],
        in_specs=[VMEM] * (2 * plan.nb),
        out_specs=[VMEM] * 3,
        cost_estimate=lasts(1),
        compiler_params=within(*out_grads, *out_grads),
        name="query_rows",
    )(*out_grads, *parts)


def grads_kernel(plan, span, first, last, by_key, n_key, q_ref, g_ref, lse_ref, delta_ref, k_ref, *refs):
    nz, na, nb, own, rows = plan.nz, plan.na, plan.nb, plan.own, plan.rows
    hd = HEAD_DIM
    scale = hd**-0.5
    length = nz * rows
    width = len(span)
    refs = list(refs)
    take = lambda n: [refs.pop(0) for _ in range(n)]
    v_refs = take(width)
    if not first:
        (dq_before,) = take(1)
    kv_before = [] if first else take(na)
    kv_outs = take(na)
    dq_outs = take(nb if last else 1)
    dk_all, dv_all = take(2)
    dq_all = refs.pop(0) if last else dq_outs[0]

    def begin(i, carry):
        dq_all[i] = jnp.zeros((rows, hd), F32) if first else dq_before[i]
        return carry

    lax.fori_loop(own if first else 0, plan.total, begin, 0)

    def wide_row(ref, start):
        return jnp.concatenate([ref[pl.ds(start + r, 1), :] for r in range(nz)], axis=1)

    def diagonal(s, carry):
        frame = pl.ds(s * nz, nz)
        k = jnp.concatenate([k_ref[s * nz + r] for r in span], axis=0)
        v = jnp.concatenate([v_ref[s] for v_ref in v_refs], axis=0)
        q, g = q_ref[frame].reshape(length, hd), g_ref[frame].reshape(length, hd)
        lse, delta = wide_row(lse_ref, s * nz), wide_row(delta_ref, s * nz)
        probs = jnp.exp(scale * dot(k, q, NT) - lse)
        dv = dot(probs.astype(BF16), g, NN)
        grad_scores = (probs * (dot(v, g, NT) - delta)).astype(BF16)
        dk = dot(grad_scores, q, NN)
        dq = dot(grad_scores, k, TN).reshape(nz, rows, hd)
        for x in range(width):
            dv_all[s * width + x] = dv[x * rows : (x + 1) * rows]
            dk_all[s * width + x] = dk[x * rows : (x + 1) * rows]
        if first:
            dq_all[frame] = dq
        else:
            dq_all[frame] += dq
        return carry

    lax.fori_loop(0, na, diagonal, 0)

    def terms(s, x, j, start):
        k, v = k_ref[j], v_refs[x][s]
        chosen = picks(by_key, j, n_key[j], start, KEY_GROUP)
        q = jnp.concatenate([q_ref[i] for i, _ in chosen], axis=0)
        g = jnp.concatenate([g_ref[i] for i, _ in chosen], axis=0)
        lse = jnp.concatenate([jnp.where(ok, lse_ref[pl.ds(i, 1), :], -NEG) for i, ok in chosen], axis=1)
        delta = jnp.concatenate([delta_ref[pl.ds(i, 1), :] for i, _ in chosen], axis=1)
        probs = jnp.exp(scale * dot(k, q, NT) - lse)
        dv = dot(probs.astype(BF16), g, NN)
        grad_scores = (probs * (dot(v, g, NT) - delta)).astype(BF16)
        dk = dot(grad_scores, q, NN)
        return chosen, dv, dk, dot(grad_scores, k, TN)

    def add(s, x, found):
        chosen, dv, dk, dq = found
        dv_all[s * width + x] += dv
        dk_all[s * width + x] += dk
        for u, (i, _) in enumerate(chosen):
            dq_all[i] += dq[u * rows : (u + 1) * rows]

    def away(s, carry):
        for x, found in [(x, terms(s, x, s * nz + r, 0)) for x, r in enumerate(span)]:
            add(s, x, found)
        for x, r in enumerate(span):

            def group(step, carry, x=x, r=r):
                add(s, x, terms(s, x, s * nz + r, step * KEY_GROUP))
                return carry

            lax.fori_loop(1, steps(n_key[s * nz + r], KEY_GROUP), group, 0)
        return carry

    lax.fori_loop(0, na, away, 0)

    done = 0 if first else kv_before[0].shape[1]
    for s, out in enumerate(kv_outs):
        if done:
            out[:, :done] = kv_before[s][...]
        for x in range(width):
            out[0, done + x] = (scale * dk_all[s * width + x]).astype(BF16)
            out[1, done + x] = dv_all[s * width + x].astype(BF16)
    if last:
        for t in range(nb):

            def drain(m, carry, t=t):
                dq_outs[t][m] = scale * dq_all[t * own + m]
                return carry

            lax.fori_loop(0, own, drain, 0)


def grads(plan, span, tables, queries, out_grads, lse, delta, keys, values, dq_before, kv_before, last):
    nb, na, own, rows, total = plan.nb, plan.na, plan.own, plan.rows, plan.total
    hd, width, first = HEAD_DIM, len(span), dq_before is None
    done = 0 if first else kv_before[0].shape[1]
    kv = [sds((2, done + width, rows, hd), BF16)] * na
    dq = [sds((own, rows, hd), F32)] * nb if last else [sds((total, rows, hd), F32)]
    before = [] if first else [dq_before, *kv_before]
    partial = sds((own, rows, hd), F32)
    outs = pl.pallas_call(
        functools.partial(grads_kernel, plan, span, first, last),
        out_shape=kv + dq,
        in_specs=[SMEM] * 2 + [VMEM] * (5 + width + len(before)),
        out_specs=[VMEM] * (na + len(dq)),
        scratch_shapes=[pltpu.VMEM((na * width, rows, hd), F32)] * 2
        + ([pltpu.VMEM((total, rows, hd), F32)] if last else []),
        cost_estimate=lasts(7),
        compiler_params=within(queries, out_grads, keys, keys, *[partial] * (4 + 3 * nb)),
    )(*tables, queries, out_grads, lse, delta, keys, *values, *before)
    return outs[:na], outs[na:]


def pack_kernel(plan, *refs):
    nb, nz = plan.nb, plan.nz
    for s, out in enumerate(refs[nb:]):
        for r in range(nz):
            out[0, r] = sum(ref[s * nz + r] for ref in refs[:nb]).astype(BF16)


def pack(plan, partials):
    return pl.pallas_call(
        functools.partial(pack_kernel, plan),
        out_shape=[sds((1, plan.nz, plan.rows, HEAD_DIM), BF16)] * plan.na,
        in_specs=[VMEM] * plan.nb,
        out_specs=[VMEM] * plan.na,
        cost_estimate=lasts(1),
        compiler_params=within(*partials, *partials),
        name="pack",
    )(*partials)


def assemble_kernel(plan, spans, n, ids, *refs):
    na, rows, hd = plan.na, plan.rows, HEAD_DIM
    refs = list(refs)
    outs = refs[na * len(spans) :]
    for span in spans:
        for s in range(na):
            piece = refs.pop(0)
            cols = pl.ds(pl.multiple_of((ids[1] ^ s) * hd, hd), hd)
            for w in range(n):
                for x, r in enumerate(span):
                    place = pl.ds(pl.multiple_of((ids[0] ^ r) * rows, rows), rows)
                    outs[w][place, cols] = piece[w, x]


def assemble(plan, ids, spans, groups):
    n = groups[0][0].shape[0]
    pieces = [piece for group in groups for piece in group]
    return pl.pallas_call(
        functools.partial(assemble_kernel, plan, spans, n),
        out_shape=[sds((plan.nz * plan.rows, plan.na * HEAD_DIM), BF16)] * n,
        in_specs=[SMEM] + [VMEM] * len(pieces),
        out_specs=[VMEM] * n,
        cost_estimate=lasts(1.5),
        compiler_params=within(*pieces, *pieces),
    )(ids, *pieces)


def local(queries, key_states, value_states, attn_out, grad_out, frame_order, block_live):
    plan = Plan(queries.shape[0])
    nz, na, nb = plan.nz, plan.na, plan.nb
    slot = lax.axis_index("frame")
    ids = jnp.stack([lax.axis_index("head"), slot // nb, slot % nb]).astype(jnp.int32)

    def staged(order, pieces, send):
        moved = {}
        for step in order:
            moved[step] = send(pieces[step], step)
        return [pieces[0]] + [moved[step] for step in range(1, len(pieces))]

    def head_stage(pieces):
        return staged([*range(2, nz), 1], pieces, over_head)

    def frame_stage(pieces):
        return staged(range(na - 1, 0, -1), pieces, lambda x, s: over_frame(x, s * nb))

    def swapped(parts):
        return staged(range(1, nb), parts, over_frame)

    groups = [
        [(a * nb + b) * nz + z for a in range(na) for z in range(nz)] for b in range(nb)
    ]
    mine = lax.all_to_all(
        prep(plan, queries, key_states), ("frame", "head"), 0, 0,
        tiled=True, axis_index_groups=groups,
    )
    g_near, v_near = prep_rest(plan, ids, grad_out, attn_out, value_states)
    g_near = frame_stage(g_near)
    v_near = frame_stage(v_near)
    by_key, n_key = lists(plan, ids, frame_order, block_live.transpose(1, 2, 0))
    g_own = turn(head_stage(turn(g_near)), joined=True)
    values = head_stage(turn(v_near))
    q_own, keys = part(plan, ids, mine)
    lse_part, q_all = totals(plan, by_key, n_key, keys, swapped([q_own] * nb))
    lse, delta, g_all = query_rows(plan, swapped([g_own] * nb), swapped([lse_part] * nb))
    spans = [range(0, 2), range(2, nz)]
    kv, dq = [], None
    for place, span in enumerate(spans):
        last = place == len(spans) - 1
        kv, dq_parts = grads(
            plan, span, (by_key, n_key), q_all, g_all, lse, delta, keys,
            [values[r] for r in span], dq, kv, last,
        )
        dq = dq_parts[0]
    kv_home = frame_stage(kv)
    dq_home = frame_stage(pack(plan, swapped(dq_parts)))
    grad_key, grad_value = assemble(plan, ids, [range(nz)], [kv_home])
    (grad_query,) = assemble(plan, ids, [range(nz)], [dq_home])
    return grad_query, grad_key, grad_value


def solution(mesh):
    rows = P(("frame", "head"), None)
    in_specs = (rows,) * 5 + (P(), P())
    out_specs = (P("frame", "head"),) * 3
    return jax.shard_map(local, mesh=mesh, in_specs=in_specs, out_specs=out_specs, check_vma=False)
```

```python
import functools
import math

import jax
import jax.numpy as jnp
from jax import lax
from jax.experimental import pallas as pl
from jax.experimental.pallas import tpu as pltpu
from jax.sharding import PartitionSpec as P


HEADS = 16
HEAD_DIM = 128
NEG = -1e30
KEY_GROUP = 4
WIDE_GROUP = 6
TOGETHER = 4
REACH = 4
EXTRA = 8


VMEM = pl.BlockSpec(memory_space=pltpu.VMEM)
SMEM = pl.BlockSpec(memory_space=pltpu.SMEM)
HBM = pl.BlockSpec(memory_space=pltpu.HBM)
F32 = jnp.float32
BF16 = jnp.bfloat16
NT = (((1,), (1,)), ((), ()))
TN = (((0,), (0,)), ((), ()))
NN = (((1,), (0,)), ((), ()))


def dot(a, b, dims):
    return lax.dot_general(a, b, dims, preferred_element_type=F32)


def sds(shape, dtype):
    return jax.ShapeDtypeStruct(shape, dtype)


def lasts(microseconds):
    return pl.CostEstimate(flops=0, bytes_accessed=int(microseconds * 3.5e6), transcendentals=0)


def within(*shapes):
    held = sum(math.prod(s.shape) * s.dtype.itemsize for s in shapes)
    return pltpu.CompilerParams(vmem_limit_bytes=int(held * 5 // 4) + (6 << 20))


class Plan:
    def __init__(self, rows):
        self.nz = lax.axis_size("head")
        self.nf = lax.axis_size("frame")
        self.hh = HEADS // self.nz
        self.na = min(self.hh, self.nf)
        self.nb = self.nf // self.na
        self.rows = rows
        self.own = self.na * self.nz
        self.total = self.own * self.nb
        assert self.hh == self.na and rows == HEAD_DIM


def over_head(value, step):
    count = lax.axis_size("head")
    return lax.ppermute(value, "head", [(i, i ^ step) for i in range(count)])


def over_frame(value, step):
    count = lax.axis_size("frame")
    return lax.ppermute(value, "frame", [(i, i ^ step) for i in range(count)])


def bundles(plan, ids, refs, bufs, sems):
    width = plan.hh * HEAD_DIM
    out = []
    for r in range(plan.nz):
        cols = pl.ds(pl.multiple_of((ids[0] ^ r) * width, width), width)
        for w, (ref, buf) in enumerate(zip(refs, bufs)):
            out.append(pltpu.make_async_copy(ref.at[:, cols], buf.at[r], sems.at[w, r]))
    for copy in out:
        copy.start()
    return out


def within_bundle(ids, s):
    return pl.ds(pl.multiple_of((ids[1] ^ s) * HEAD_DIM, HEAD_DIM), HEAD_DIM)


def prep_kernel(plan, q_ref, k_ref, out):
    hd, rows = HEAD_DIM, plan.rows
    for a in range(plan.na):
        for z in range(plan.nz):
            head, place = z * plan.hh + a, a * plan.nz + z
            out[place, :rows] = q_ref[:, head * hd : (head + 1) * hd]
            out[place, rows:] = k_ref[:, head * hd : (head + 1) * hd]


def prep(plan, q, k):
    return pl.pallas_call(
        functools.partial(prep_kernel, plan),
        out_shape=sds((plan.own, 2 * plan.rows, HEAD_DIM), BF16),
        in_specs=[VMEM] * 2,
        out_specs=VMEM,
        cost_estimate=lasts(1.5),
        compiler_params=pltpu.CompilerParams(vmem_limit_bytes=60 << 20),
        name="prep",
    )(q, k)


def part_kernel(plan, ids, x_ref, q_out, k_out):
    rows = plan.rows
    for s in range(plan.na):
        for r in range(plan.nz):
            place = (ids[1] ^ s) * plan.nz + (ids[0] ^ r)
            q_out[s * plan.nz + r] = x_ref[place, :rows]
            k_out[s * plan.nz + r] = x_ref[place, rows:]


def part(plan, ids, x):
    return pl.pallas_call(
        functools.partial(part_kernel, plan),
        out_shape=[sds((plan.own, plan.rows, HEAD_DIM), BF16)] * 2,
        in_specs=[SMEM, VMEM],
        out_specs=[VMEM] * 2,
        cost_estimate=lasts(1),
        compiler_params=within(x, x),
        name="part",
    )(ids, x)


def prep_rest_kernel(plan, ids, g_ref, o_ref, v_ref, *refs):
    na, rows = plan.na, plan.rows
    g_outs, v_outs, bufs, sems = refs[:na], refs[na : 2 * na], refs[2 * na : 2 * na + 3], refs[-1]
    copies = bundles(plan, ids, [g_ref, o_ref, v_ref], bufs, sems)
    ones = jnp.ones((EXTRA, HEAD_DIM), BF16)
    row = lax.broadcasted_iota(jnp.int32, (EXTRA, rows), 0)
    for r in range(plan.nz):
        for copy in copies[3 * r : 3 * r + 3]:
            copy.wait()
        for s in range(na):
            cols = within_bundle(ids, s)
            grad = bufs[0][r, :, cols]
            g_outs[s][r, :rows] = grad
            v_outs[s][r] = bufs[2][r, :, cols]
            product = grad.astype(F32) * bufs[1][r, :, cols].astype(F32)
            high = product.astype(BF16)
            low = (product - high.astype(F32)).astype(BF16)
            delta = dot(ones, high, NT) + dot(ones, low, NT)
            first = delta.astype(BF16).astype(F32)
            rest = delta - first
            second = rest.astype(BF16).astype(F32)
            parts = jnp.where(row == 2, rest - second, 0.0)
            parts = jnp.where(row == 0, first, jnp.where(row == 1, second, parts))
            g_outs[s][r, rows:] = parts.astype(BF16)


def prep_rest(plan, ids, g, o, v):
    na, nz, rows, hd = plan.na, plan.nz, plan.rows, HEAD_DIM
    outs = pl.pallas_call(
        functools.partial(prep_rest_kernel, plan),
        out_shape=[sds((nz, rows + EXTRA, hd), BF16)] * na + [sds((nz, rows, hd), BF16)] * na,
        in_specs=[SMEM] + [HBM] * 3,
        out_specs=[VMEM] * (2 * na),
        scratch_shapes=[pltpu.VMEM((nz, rows, plan.hh * hd), BF16)] * 3
        + [pltpu.SemaphoreType.DMA((3, nz))],
        cost_estimate=lasts(2),
        compiler_params=within(g, o, v, g, v),
        name="prep_rest",
    )(ids, g, o, v)
    return outs[:na], outs[na:]


def turn_kernel(count, *refs):
    pieces, outs = refs[:count], refs[count:]
    joined = len(outs) == 1
    for c in range(pieces[0].shape[0]):
        for p, piece in enumerate(pieces):
            if joined:
                outs[0][c * count + p] = piece[c]
            else:
                outs[c][p] = piece[c]


def turn(pieces, joined=False):
    count, parts, shape = len(pieces), pieces[0].shape[0], pieces[0].shape[1:]
    out = [sds((parts * count, *shape), BF16)] if joined else [sds((count, *shape), BF16)] * parts
    outs = pl.pallas_call(
        functools.partial(turn_kernel, count),
        out_shape=out,
        in_specs=[VMEM] * count,
        out_specs=[VMEM] * len(out),
        cost_estimate=lasts(0.5),
        compiler_params=within(*pieces, *pieces),
    )(*pieces)
    return outs[0] if joined else outs


def lists_kernel(plan, ids, order, live_ref, by_key, n_key, query_of, numbers):
    nz, na, nb = plan.nz, plan.na, plan.nb
    z, a, b = ids[0], ids[1], ids[2]
    true = [z ^ r for r in range(nz)]

    def at_distance(d, carry):
        for rk in range(nz):
            count = jnp.int32(0)
            for r in range(nz):
                query_of[d * nz + rk, count] = jnp.int32(r)
                count = count + (live_ref[true[r], true[rk], d] > 0).astype(jnp.int32)
            numbers[d * nz + rk] = count
        return carry

    lax.fori_loop(1, REACH, at_distance, 0)

    def key_frame(s_key, carry):
        place_key = order[(a ^ s_key) * nb + b]

        def query_frame(ts, counts):
            t = ts // na
            place = order[(a ^ (ts - t * na)) * nb + (b ^ t)]
            d = jnp.abs(place - place_key)

            def found(counts):
                counts = list(counts)
                for rk in range(nz):
                    row = d * nz + rk
                    for u in range(nz):
                        by_key[s_key * nz + rk, counts[rk] + u] = ts * nz + query_of[row, u]
                    counts[rk] = counts[rk] + numbers[row]
                return tuple(counts)

            return lax.cond((d > 0) & (d < REACH), found, lambda counts: counts, counts)

        counts = lax.fori_loop(0, na * nb, query_frame, (jnp.int32(0),) * nz)
        for rk in range(nz):
            n_key[s_key * nz + rk] = counts[rk]
        return carry

    lax.fori_loop(0, na, key_frame, 0)


def lists(plan, ids, order, live):
    own, total, nz = plan.own, plan.total, plan.nz
    return pl.pallas_call(
        functools.partial(lists_kernel, plan),
        out_shape=[sds((own, total + WIDE_GROUP + nz), jnp.int32), sds((own,), jnp.int32)],
        in_specs=[SMEM] * 3,
        out_specs=[SMEM] * 2,
        scratch_shapes=[
            pltpu.SMEM((REACH * nz, nz), jnp.int32),
            pltpu.SMEM((REACH * nz,), jnp.int32),
        ],
        cost_estimate=lasts(3),
        compiler_params=within(),
        name="lists",
    )(ids, order, live)


def picks(table, row, count, first, size):
    out = []
    for u in range(size):
        valid = first + u < count
        out.append((jnp.where(valid, table[row, first + u], 0), valid))
    return out


def steps(count, size):
    return lax.div(count + (size - 1), size)


def totals_kernel(plan, by_key, n_key, k_ref, *refs):
    parts, (out, q_ref, peaks, sums) = refs[: plan.nb], refs[plan.nb :]
    nz, na, own, rows, total = plan.nz, plan.na, plan.own, plan.rows, plan.total
    scale = HEAD_DIM**-0.5
    length = nz * rows
    for t, each in enumerate(parts):
        q_ref[t * own : (t + 1) * own] = each[...]
    peaks[own:, :] = jnp.full((peaks.shape[0] - own, rows), NEG, F32)
    sums[own:, :] = jnp.zeros((peaks.shape[0] - own, rows), F32)

    def near(s, carry):
        span = pl.ds(s * nz, nz)
        keys, q = k_ref[span].reshape(length, HEAD_DIM), q_ref[span].reshape(length, HEAD_DIM)
        scores = scale * dot(keys, q, NT)
        peak = jnp.max(scores, axis=0, keepdims=True)
        mass = jnp.sum(jnp.exp(scores - peak), axis=0, keepdims=True)
        for r in range(nz):
            peaks[pl.ds(s * nz + r, 1), :] = peak[:, r * rows : (r + 1) * rows]
            sums[pl.ds(s * nz + r, 1), :] = mass[:, r * rows : (r + 1) * rows]
        return carry

    lax.fori_loop(0, na, near, 0)

    def local(j, start):
        chosen = picks(by_key, j, n_key[j], start, WIDE_GROUP)
        places = [pl.ds(jnp.where(ok, i, total), 1) for i, ok in chosen]
        q = jnp.concatenate([q_ref[i] for i, _ in chosen], axis=0)
        scores = scale * dot(k_ref[j], q, NT)
        peak = jnp.max(scores, axis=0, keepdims=True)
        mass = jnp.sum(jnp.exp(scores - peak), axis=0, keepdims=True)
        return places, peak, mass

    def merge(places, peak, mass):
        old_peak = jnp.concatenate([peaks[place, :] for place in places], axis=1)
        old_mass = jnp.concatenate([sums[place, :] for place in places], axis=1)
        new_peak = jnp.maximum(old_peak, peak)
        new_mass = old_mass * jnp.exp(old_peak - new_peak) + mass * jnp.exp(peak - new_peak)
        for u, place in enumerate(places):
            peaks[place, :] = new_peak[:, u * rows : (u + 1) * rows]
            sums[place, :] = new_mass[:, u * rows : (u + 1) * rows]

    def away(m, carry):
        for found in [local(m * TOGETHER + u, 0) for u in range(TOGETHER)]:
            merge(*found)
        return carry

    lax.fori_loop(0, own // TOGETHER, away, 0)

    def rest(j, carry):
        def group(step, carry):
            merge(*local(j, step * WIDE_GROUP))
            return carry

        return lax.fori_loop(1, steps(n_key[j], WIDE_GROUP), group, carry)

    lax.fori_loop(0, own, rest, 0)
    peak = peaks[:total, :]
    out[...] = jnp.where(peak > 0.5 * NEG, peak + jnp.log(sums[:total, :]), NEG)


def totals(plan, by_key, n_key, keys, queries):
    return pl.pallas_call(
        functools.partial(totals_kernel, plan),
        out_shape=[
            sds((plan.total, plan.rows), F32),
            sds((plan.total, plan.rows, HEAD_DIM), BF16),
        ],
        in_specs=[SMEM, SMEM, VMEM] + [VMEM] * plan.nb,
        out_specs=[VMEM] * 2,
        scratch_shapes=[pltpu.VMEM((plan.total + 8, plan.rows), F32)] * 2,
        cost_estimate=lasts(6),
        compiler_params=within(keys, *queries, *queries),
        name="totals",
    )(by_key, n_key, keys, *queries)


def rows_kernel(plan, *refs):
    nb, own, rows = plan.nb, plan.own, plan.rows
    g_refs, parts, (lse_all, delta_all, g_all) = refs[:nb], refs[nb : 2 * nb], refs[2 * nb :]
    for t in range(nb):
        rivals = [parts[u][pl.ds((t ^ u) * own, own), :] for u in range(nb)]
        peak = functools.reduce(jnp.maximum, rivals)
        lse_all[pl.ds(t * own, own), :] = peak + jnp.log(sum(jnp.exp(x - peak) for x in rivals))
        for m in range(own):
            extra = g_refs[t][m, rows:].astype(F32)
            delta_all[t * own + m : t * own + m + 1, :] = jnp.sum(extra, axis=0, keepdims=True)
            g_all[t * own + m] = g_refs[t][m, :rows]


def query_rows(plan, out_grads, parts):
    return pl.pallas_call(
        functools.partial(rows_kernel, plan),
        out_shape=[sds((plan.total, plan.rows), F32)] * 2
        + [sds((plan.total, plan.rows, HEAD_DIM), BF16)],
        in_specs=[VMEM] * (2 * plan.nb),
        out_specs=[VMEM] * 3,
        cost_estimate=lasts(1),
        compiler_params=within(*out_grads, *out_grads),
        name="query_rows",
    )(*out_grads, *parts)


def grads_kernel(plan, span, first, last, by_key, n_key, q_ref, g_ref, lse_ref, delta_ref, k_ref, *refs):
    nz, na, nb, own, rows = plan.nz, plan.na, plan.nb, plan.own, plan.rows
    hd = HEAD_DIM
    scale = hd**-0.5
    length = nz * rows
    width = len(span)
    refs = list(refs)
    take = lambda n: [refs.pop(0) for _ in range(n)]
    v_refs = take(width)
    if not first:
        (dq_before,) = take(1)
    kv_outs = take(na)
    dq_outs = take(nb if last else 1)
    dk_all, dv_all = take(2)
    dq_all = refs.pop(0) if last else dq_outs[0]

    def begin(i, carry):
        dq_all[i] = jnp.zeros((rows, hd), F32) if first else dq_before[i]
        return carry

    lax.fori_loop(own if first else 0, plan.total, begin, 0)

    def wide_row(ref, start):
        return jnp.concatenate([ref[pl.ds(start + r, 1), :] for r in range(nz)], axis=1)

    def diagonal(s, carry):
        frame = pl.ds(s * nz, nz)
        k = jnp.concatenate([k_ref[s * nz + r] for r in span], axis=0)
        v = jnp.concatenate([v_ref[s] for v_ref in v_refs], axis=0)
        q, g = q_ref[frame].reshape(length, hd), g_ref[frame].reshape(length, hd)
        lse, delta = wide_row(lse_ref, s * nz), wide_row(delta_ref, s * nz)
        probs = jnp.exp(scale * dot(k, q, NT) - lse)
        dv = dot(probs.astype(BF16), g, NN)
        grad_scores = (probs * (dot(v, g, NT) - delta)).astype(BF16)
        dk = dot(grad_scores, q, NN)
        dq = dot(grad_scores, k, TN).reshape(nz, rows, hd)
        for x in range(width):
            dv_all[s * width + x] = dv[x * rows : (x + 1) * rows]
            dk_all[s * width + x] = dk[x * rows : (x + 1) * rows]
        if first:
            dq_all[frame] = dq
        else:
            dq_all[frame] += dq
        return carry

    lax.fori_loop(0, na, diagonal, 0)

    def terms(s, x, j, start, size):
        k, v = k_ref[j], v_refs[x][s]
        chosen = picks(by_key, j, n_key[j], start, size)
        q = jnp.concatenate([q_ref[i] for i, _ in chosen], axis=0)
        g = jnp.concatenate([g_ref[i] for i, _ in chosen], axis=0)
        lse = jnp.concatenate([jnp.where(ok, lse_ref[pl.ds(i, 1), :], -NEG) for i, ok in chosen], axis=1)
        delta = jnp.concatenate([delta_ref[pl.ds(i, 1), :] for i, _ in chosen], axis=1)
        probs = jnp.exp(scale * dot(k, q, NT) - lse)
        dv = dot(probs.astype(BF16), g, NN)
        grad_scores = (probs * (dot(v, g, NT) - delta)).astype(BF16)
        dk = dot(grad_scores, q, NN)
        return chosen, dv, dk, dot(grad_scores, k, TN)

    def add(s, x, found):
        chosen, dv, dk, dq = found
        dv_all[s * width + x] += dv
        dk_all[s * width + x] += dk
        for u, (i, _) in enumerate(chosen):
            dq_all[i] += dq[u * rows : (u + 1) * rows]

    def away(s, carry):
        most = functools.reduce(jnp.maximum, [n_key[s * nz + r] for r in span])

        def together(size):
            for x, found in [(x, terms(s, x, s * nz + r, 0, size)) for x, r in enumerate(span)]:
                add(s, x, found)

        pl.when((most > 0) & (most <= KEY_GROUP))(lambda: together(KEY_GROUP))
        pl.when(most > KEY_GROUP)(lambda: together(WIDE_GROUP))
        for x, r in enumerate(span):
            left = jnp.maximum(n_key[s * nz + r] - WIDE_GROUP, 0)

            def group(step, carry, x=x, r=r):
                add(s, x, terms(s, x, s * nz + r, WIDE_GROUP + step * KEY_GROUP, KEY_GROUP))
                return carry

            lax.fori_loop(0, steps(left, KEY_GROUP), group, 0)
        return carry

    lax.fori_loop(0, na, away, 0)

    for s, out in enumerate(kv_outs):
        for x in range(width):
            out[0, x] = (scale * dk_all[s * width + x]).astype(BF16)
            out[1, x] = dv_all[s * width + x].astype(BF16)
    if last:
        for t in range(nb):

            def drain(m, carry, t=t):
                dq_outs[t][m] = scale * dq_all[t * own + m]
                return carry

            lax.fori_loop(0, own, drain, 0)


def grads(plan, span, tables, queries, out_grads, lse, delta, keys, values, dq_before, last):
    nb, na, own, rows, total = plan.nb, plan.na, plan.own, plan.rows, plan.total
    hd, width, first = HEAD_DIM, len(span), dq_before is None
    kv = [sds((2, width, rows, hd), BF16)] * na
    dq = [sds((own, rows, hd), F32)] * nb if last else [sds((total, rows, hd), F32)]
    before = [] if first else [dq_before]
    partial = sds((own, rows, hd), F32)
    outs = pl.pallas_call(
        functools.partial(grads_kernel, plan, span, first, last),
        out_shape=kv + dq,
        in_specs=[SMEM] * 2 + [VMEM] * (5 + width + len(before)),
        out_specs=[VMEM] * (na + len(dq)),
        scratch_shapes=[pltpu.VMEM((na * width, rows, hd), F32)] * 2
        + ([pltpu.VMEM((total, rows, hd), F32)] if last else []),
        cost_estimate=lasts(7),
        compiler_params=within(queries, out_grads, keys, keys, *[partial] * (4 + 3 * nb)),
    )(*tables, queries, out_grads, lse, delta, keys, *values, *before)
    return outs[:na], outs[na:]


def pack_kernel(plan, *refs):
    nb, nz = plan.nb, plan.nz
    for s, out in enumerate(refs[nb:]):
        for r in range(nz):
            out[0, r] = sum(ref[s * nz + r] for ref in refs[:nb]).astype(BF16)


def pack(plan, partials):
    return pl.pallas_call(
        functools.partial(pack_kernel, plan),
        out_shape=[sds((1, plan.nz, plan.rows, HEAD_DIM), BF16)] * plan.na,
        in_specs=[VMEM] * plan.nb,
        out_specs=[VMEM] * plan.na,
        cost_estimate=lasts(1),
        compiler_params=within(*partials, *partials),
        name="pack",
    )(*partials)


def assemble_kernel(plan, spans, n, ids, *refs):
    na, rows, hd = plan.na, plan.rows, HEAD_DIM
    refs = list(refs)
    outs = refs[na * len(spans) :]
    for span in spans:
        for s in range(na):
            piece = refs.pop(0)
            cols = pl.ds(pl.multiple_of((ids[1] ^ s) * hd, hd), hd)
            for w in range(n):
                for x, r in enumerate(span):
                    place = pl.ds(pl.multiple_of((ids[0] ^ r) * rows, rows), rows)
                    outs[w][place, cols] = piece[w, x]


def assemble(plan, ids, spans, groups):
    n = groups[0][0].shape[0]
    pieces = [piece for group in groups for piece in group]
    return pl.pallas_call(
        functools.partial(assemble_kernel, plan, spans, n),
        out_shape=[sds((plan.nz * plan.rows, plan.na * HEAD_DIM), BF16)] * n,
        in_specs=[SMEM] + [VMEM] * len(pieces),
        out_specs=[VMEM] * n,
        cost_estimate=lasts(1.5),
        compiler_params=within(*pieces, *pieces),
    )(ids, *pieces)


def local(queries, key_states, value_states, attn_out, grad_out, frame_order, block_live):
    plan = Plan(queries.shape[0])
    nz, na, nb = plan.nz, plan.na, plan.nb
    slot = lax.axis_index("frame")
    ids = jnp.stack([lax.axis_index("head"), slot // nb, slot % nb]).astype(jnp.int32)

    def staged(order, pieces, send):
        moved = {}
        for step in order:
            moved[step] = send(pieces[step], step)
        return [pieces[0]] + [moved[step] for step in range(1, len(pieces))]

    def head_stage(pieces):
        return staged([*range(2, nz), 1], pieces, over_head)

    def frame_stage(pieces):
        return staged(range(na - 1, 0, -1), pieces, lambda x, s: over_frame(x, s * nb))

    def swapped(parts):
        return staged(range(1, nb), parts, over_frame)

    groups = [
        [(a * nb + b) * nz + z for a in range(na) for z in range(nz)] for b in range(nb)
    ]
    mine = lax.all_to_all(
        prep(plan, queries, key_states), ("frame", "head"), 0, 0,
        tiled=True, axis_index_groups=groups,
    )
    g_near, v_near = prep_rest(plan, ids, grad_out, attn_out, value_states)
    g_near = frame_stage(g_near)
    v_near = frame_stage(v_near)
    by_key, n_key = lists(plan, ids, frame_order, block_live.transpose(1, 2, 0))
    g_own = turn(head_stage(turn(g_near)), joined=True)
    values = head_stage(turn(v_near))
    q_own, keys = part(plan, ids, mine)
    lse_part, q_all = totals(plan, by_key, n_key, keys, swapped([q_own] * nb))
    lse, delta, g_all = query_rows(plan, swapped([g_own] * nb), swapped([lse_part] * nb))
    spans = [range(0, 2), range(2, nz)]
    kv_home, dq = [], None
    for place, span in enumerate(spans):
        last = place == len(spans) - 1
        kv, dq_parts = grads(
            plan, span, (by_key, n_key), q_all, g_all, lse, delta, keys,
            [values[r] for r in span], dq, last,
        )
        dq = dq_parts[0]
        kv_home.append(frame_stage(kv))
    dq_home = frame_stage(pack(plan, swapped(dq_parts)))
    grad_key, grad_value = assemble(plan, ids, spans, kv_home)
    (grad_query,) = assemble(plan, ids, [range(nz)], [dq_home])
    return grad_query, grad_key, grad_value


def solution(mesh):
    rows = P(("frame", "head"), None)
    in_specs = (rows,) * 5 + (P(), P())
    out_specs = (P("frame", "head"),) * 3
    return jax.shard_map(local, mesh=mesh, in_specs=in_specs, out_specs=out_specs, check_vma=False)
```

```python
import functools
import math

import jax
import jax.numpy as jnp
from jax import lax
from jax.experimental import pallas as pl
from jax.experimental.pallas import tpu as pltpu
from jax.sharding import PartitionSpec as P


HEADS = 16
HEAD_DIM = 128
NEG = -1e30
KEY_GROUP = 4
WIDE_GROUP = 6
TOGETHER = 4
REACH = 4
EXTRA = 8


VMEM = pl.BlockSpec(memory_space=pltpu.VMEM)
SMEM = pl.BlockSpec(memory_space=pltpu.SMEM)
HBM = pl.BlockSpec(memory_space=pltpu.HBM)
F32 = jnp.float32
BF16 = jnp.bfloat16
NT = (((1,), (1,)), ((), ()))
TN = (((0,), (0,)), ((), ()))
NN = (((1,), (0,)), ((), ()))


def dot(a, b, dims):
    return lax.dot_general(a, b, dims, preferred_element_type=F32)


def sds(shape, dtype):
    return jax.ShapeDtypeStruct(shape, dtype)


def lasts(microseconds):
    return pl.CostEstimate(flops=0, bytes_accessed=int(microseconds * 3.5e6), transcendentals=0)


def within(*shapes):
    held = sum(math.prod(s.shape) * s.dtype.itemsize for s in shapes)
    return pltpu.CompilerParams(vmem_limit_bytes=int(held * 5 // 4) + (6 << 20))


class Plan:
    def __init__(self, rows):
        self.nz = lax.axis_size("head")
        self.nf = lax.axis_size("frame")
        self.hh = HEADS // self.nz
        self.na = min(self.hh, self.nf)
        self.nb = self.nf // self.na
        self.rows = rows
        self.own = self.na * self.nz
        self.total = self.own * self.nb
        assert self.hh == self.na and rows == HEAD_DIM


def over_head(value, step):
    count = lax.axis_size("head")
    return lax.ppermute(value, "head", [(i, i ^ step) for i in range(count)])


def over_frame(value, step):
    count = lax.axis_size("frame")
    return lax.ppermute(value, "frame", [(i, i ^ step) for i in range(count)])


def bundles(plan, ids, refs, bufs, sems):
    width = plan.hh * HEAD_DIM
    out = []
    for r in range(plan.nz):
        cols = pl.ds(pl.multiple_of((ids[0] ^ r) * width, width), width)
        for w, (ref, buf) in enumerate(zip(refs, bufs)):
            out.append(pltpu.make_async_copy(ref.at[:, cols], buf.at[r], sems.at[w, r]))
    for copy in out:
        copy.start()
    return out


def within_bundle(ids, s):
    return pl.ds(pl.multiple_of((ids[1] ^ s) * HEAD_DIM, HEAD_DIM), HEAD_DIM)


def prep_kernel(plan, q_ref, k_ref, out):
    hd, rows = HEAD_DIM, plan.rows
    for a in range(plan.na):
        for z in range(plan.nz):
            head, place = z * plan.hh + a, a * plan.nz + z
            out[place, :rows] = q_ref[:, head * hd : (head + 1) * hd]
            out[place, rows:] = k_ref[:, head * hd : (head + 1) * hd]


def prep(plan, q, k):
    return pl.pallas_call(
        functools.partial(prep_kernel, plan),
        out_shape=sds((plan.own, 2 * plan.rows, HEAD_DIM), BF16),
        in_specs=[VMEM] * 2,
        out_specs=VMEM,
        cost_estimate=lasts(1.5),
        compiler_params=pltpu.CompilerParams(vmem_limit_bytes=60 << 20),
        name="prep",
    )(q, k)


def part_kernel(plan, ids, x_ref, q_out, k_out):
    rows = plan.rows
    for s in range(plan.na):
        for r in range(plan.nz):
            place = (ids[1] ^ s) * plan.nz + (ids[0] ^ r)
            q_out[s * plan.nz + r] = x_ref[place, :rows]
            k_out[s * plan.nz + r] = x_ref[place, rows:]


def part(plan, ids, x):
    return pl.pallas_call(
        functools.partial(part_kernel, plan),
        out_shape=[sds((plan.own, plan.rows, HEAD_DIM), BF16)] * 2,
        in_specs=[SMEM, VMEM],
        out_specs=[VMEM] * 2,
        cost_estimate=lasts(1),
        compiler_params=within(x, x),
        name="part",
    )(ids, x)


def prep_rest_kernel(plan, ids, g_ref, o_ref, v_ref, *refs):
    na, rows = plan.na, plan.rows
    g_outs, v_outs, bufs, sems = refs[:na], refs[na : 2 * na], refs[2 * na : 2 * na + 3], refs[-1]
    copies = bundles(plan, ids, [g_ref, o_ref, v_ref], bufs, sems)
    ones = jnp.ones((EXTRA, HEAD_DIM), BF16)
    row = lax.broadcasted_iota(jnp.int32, (EXTRA, rows), 0)
    for r in range(plan.nz):
        for copy in copies[3 * r : 3 * r + 3]:
            copy.wait()
        for s in range(na):
            cols = within_bundle(ids, s)
            grad = bufs[0][r, :, cols]
            g_outs[s][r, :rows] = grad
            v_outs[s][r] = bufs[2][r, :, cols]
            product = grad.astype(F32) * bufs[1][r, :, cols].astype(F32)
            high = product.astype(BF16)
            low = (product - high.astype(F32)).astype(BF16)
            delta = dot(ones, high, NT) + dot(ones, low, NT)
            first = delta.astype(BF16).astype(F32)
            rest = delta - first
            second = rest.astype(BF16).astype(F32)
            parts = jnp.where(row == 2, rest - second, 0.0)
            parts = jnp.where(row == 0, first, jnp.where(row == 1, second, parts))
            g_outs[s][r, rows:] = parts.astype(BF16)


def prep_rest(plan, ids, g, o, v):
    na, nz, rows, hd = plan.na, plan.nz, plan.rows, HEAD_DIM
    outs = pl.pallas_call(
        functools.partial(prep_rest_kernel, plan),
        out_shape=[sds((nz, rows + EXTRA, hd), BF16)] * na + [sds((nz, rows, hd), BF16)] * na,
        in_specs=[SMEM] + [HBM] * 3,
        out_specs=[VMEM] * (2 * na),
        scratch_shapes=[pltpu.VMEM((nz, rows, plan.hh * hd), BF16)] * 3
        + [pltpu.SemaphoreType.DMA((3, nz))],
        cost_estimate=lasts(2),
        compiler_params=within(g, o, v, g, v),
        name="prep_rest",
    )(ids, g, o, v)
    return outs[:na], outs[na:]


def turn_kernel(count, *refs):
    pieces, outs = refs[:count], refs[count:]
    joined = len(outs) == 1
    for c in range(pieces[0].shape[0]):
        for p, piece in enumerate(pieces):
            if joined:
                outs[0][c * count + p] = piece[c]
            else:
                outs[c][p] = piece[c]


def turn(pieces, joined=False):
    count, parts, shape = len(pieces), pieces[0].shape[0], pieces[0].shape[1:]
    out = [sds((parts * count, *shape), BF16)] if joined else [sds((count, *shape), BF16)] * parts
    outs = pl.pallas_call(
        functools.partial(turn_kernel, count),
        out_shape=out,
        in_specs=[VMEM] * count,
        out_specs=[VMEM] * len(out),
        cost_estimate=lasts(0.5),
        compiler_params=within(*pieces, *pieces),
    )(*pieces)
    return outs[0] if joined else outs


def lists_kernel(plan, ids, order, live_ref, by_key, n_key, query_of, numbers):
    nz, na, nb = plan.nz, plan.na, plan.nb
    z, a, b = ids[0], ids[1], ids[2]
    true = [z ^ r for r in range(nz)]

    def at_distance(d, carry):
        for rk in range(nz):
            count = jnp.int32(0)
            for r in range(nz):
                query_of[d * nz + rk, count] = jnp.int32(r)
                count = count + (live_ref[true[r], true[rk], d] > 0).astype(jnp.int32)
            numbers[d * nz + rk] = count
        return carry

    lax.fori_loop(1, REACH, at_distance, 0)

    def key_frame(s_key, carry):
        place_key = order[(a ^ s_key) * nb + b]

        def query_frame(ts, counts):
            t = ts // na
            place = order[(a ^ (ts - t * na)) * nb + (b ^ t)]
            d = jnp.abs(place - place_key)

            def found(counts):
                counts = list(counts)
                for rk in range(nz):
                    row = d * nz + rk
                    for u in range(nz):
                        by_key[s_key * nz + rk, counts[rk] + u] = ts * nz + query_of[row, u]
                    counts[rk] = counts[rk] + numbers[row]
                return tuple(counts)

            return lax.cond((d > 0) & (d < REACH), found, lambda counts: counts, counts)

        counts = lax.fori_loop(0, na * nb, query_frame, (jnp.int32(0),) * nz)
        for rk in range(nz):
            n_key[s_key * nz + rk] = counts[rk]
        return carry

    lax.fori_loop(0, na, key_frame, 0)


def lists(plan, ids, order, live):
    own, total, nz = plan.own, plan.total, plan.nz
    return pl.pallas_call(
        functools.partial(lists_kernel, plan),
        out_shape=[sds((own, total + WIDE_GROUP + nz), jnp.int32), sds((own,), jnp.int32)],
        in_specs=[SMEM] * 3,
        out_specs=[SMEM] * 2,
        scratch_shapes=[
            pltpu.SMEM((REACH * nz, nz), jnp.int32),
            pltpu.SMEM((REACH * nz,), jnp.int32),
        ],
        cost_estimate=lasts(3),
        compiler_params=within(),
        name="lists",
    )(ids, order, live)


def picks(table, row, count, first, size):
    out = []
    for u in range(size):
        valid = first + u < count
        out.append((jnp.where(valid, table[row, first + u], 0), valid))
    return out


def steps(count, size):
    return lax.div(count + (size - 1), size)


def totals_kernel(plan, by_key, n_key, k_ref, *refs):
    parts, (out, q_ref, peaks, sums) = refs[: plan.nb], refs[plan.nb :]
    nz, na, own, rows, total = plan.nz, plan.na, plan.own, plan.rows, plan.total
    scale = HEAD_DIM**-0.5
    length = nz * rows
    for t, each in enumerate(parts):
        q_ref[t * own : (t + 1) * own] = each[...]
    peaks[own:, :] = jnp.full((peaks.shape[0] - own, rows), NEG, F32)
    sums[own:, :] = jnp.zeros((peaks.shape[0] - own, rows), F32)

    def near(s, carry):
        span = pl.ds(s * nz, nz)
        keys, q = k_ref[span].reshape(length, HEAD_DIM), q_ref[span].reshape(length, HEAD_DIM)
        scores = scale * dot(keys, q, NT)
        peak = jnp.max(scores, axis=0, keepdims=True)
        mass = jnp.sum(jnp.exp(scores - peak), axis=0, keepdims=True)
        for r in range(nz):
            peaks[pl.ds(s * nz + r, 1), :] = peak[:, r * rows : (r + 1) * rows]
            sums[pl.ds(s * nz + r, 1), :] = mass[:, r * rows : (r + 1) * rows]
        return carry

    lax.fori_loop(0, na, near, 0)

    def local(j, start, size):
        chosen = picks(by_key, j, n_key[j], start, size)
        places = [pl.ds(jnp.where(ok, i, total), 1) for i, ok in chosen]
        q = jnp.concatenate([q_ref[i] for i, _ in chosen], axis=0)
        scores = scale * dot(k_ref[j], q, NT)
        peak = jnp.max(scores, axis=0, keepdims=True)
        mass = jnp.sum(jnp.exp(scores - peak), axis=0, keepdims=True)
        return places, peak, mass

    def merge(places, peak, mass):
        old_peak = jnp.concatenate([peaks[place, :] for place in places], axis=1)
        old_mass = jnp.concatenate([sums[place, :] for place in places], axis=1)
        new_peak = jnp.maximum(old_peak, peak)
        new_mass = old_mass * jnp.exp(old_peak - new_peak) + mass * jnp.exp(peak - new_peak)
        for u, place in enumerate(places):
            peaks[place, :] = new_peak[:, u * rows : (u + 1) * rows]
            sums[place, :] = new_mass[:, u * rows : (u + 1) * rows]

    def away(m, carry):
        blocks = [m * TOGETHER + u for u in range(TOGETHER)]
        most = functools.reduce(jnp.maximum, [n_key[j] for j in blocks])

        def together(size):
            for found in [local(j, 0, size) for j in blocks]:
                merge(*found)

        pl.when((most > 0) & (most <= KEY_GROUP))(lambda: together(KEY_GROUP))
        pl.when(most > KEY_GROUP)(lambda: together(WIDE_GROUP))
        return carry

    lax.fori_loop(0, own // TOGETHER, away, 0)

    def rest(j, carry):
        def group(step, carry):
            merge(*local(j, step * WIDE_GROUP, WIDE_GROUP))
            return carry

        return lax.fori_loop(1, steps(n_key[j], WIDE_GROUP), group, carry)

    lax.fori_loop(0, own, rest, 0)
    peak = peaks[:total, :]
    out[...] = jnp.where(peak > 0.5 * NEG, peak + jnp.log(sums[:total, :]), NEG)


def totals(plan, by_key, n_key, keys, queries):
    return pl.pallas_call(
        functools.partial(totals_kernel, plan),
        out_shape=[
            sds((plan.total, plan.rows), F32),
            sds((plan.total, plan.rows, HEAD_DIM), BF16),
        ],
        in_specs=[SMEM, SMEM, VMEM] + [VMEM] * plan.nb,
        out_specs=[VMEM] * 2,
        scratch_shapes=[pltpu.VMEM((plan.total + 8, plan.rows), F32)] * 2,
        cost_estimate=lasts(6),
        compiler_params=within(keys, *queries, *queries),
        name="totals",
    )(by_key, n_key, keys, *queries)


def rows_kernel(plan, *refs):
    nb, own, rows = plan.nb, plan.own, plan.rows
    g_refs, parts, (lse_all, delta_all, g_all) = refs[:nb], refs[nb : 2 * nb], refs[2 * nb :]
    for t in range(nb):
        rivals = [parts[u][pl.ds((t ^ u) * own, own), :] for u in range(nb)]
        peak = functools.reduce(jnp.maximum, rivals)
        lse_all[pl.ds(t * own, own), :] = peak + jnp.log(sum(jnp.exp(x - peak) for x in rivals))
        for m in range(own):
            extra = g_refs[t][m, rows:].astype(F32)
            delta_all[t * own + m : t * own + m + 1, :] = jnp.sum(extra, axis=0, keepdims=True)
            g_all[t * own + m] = g_refs[t][m, :rows]


def query_rows(plan, out_grads, parts):
    return pl.pallas_call(
        functools.partial(rows_kernel, plan),
        out_shape=[sds((plan.total, plan.rows), F32)] * 2
        + [sds((plan.total, plan.rows, HEAD_DIM), BF16)],
        in_specs=[VMEM] * (2 * plan.nb),
        out_specs=[VMEM] * 3,
        cost_estimate=lasts(1),
        compiler_params=within(*out_grads, *out_grads),
        name="query_rows",
    )(*out_grads, *parts)


def grads_kernel(plan, span, first, last, by_key, n_key, q_ref, g_ref, lse_ref, delta_ref, k_ref, *refs):
    nz, na, nb, own, rows = plan.nz, plan.na, plan.nb, plan.own, plan.rows
    hd = HEAD_DIM
    scale = hd**-0.5
    length = nz * rows
    width = len(span)
    refs = list(refs)
    take = lambda n: [refs.pop(0) for _ in range(n)]
    v_refs = take(width)
    if not first:
        (dq_before,) = take(1)
    kv_outs = take(na)
    dq_outs = take(nb if last else 1)
    dk_all, dv_all = take(2)
    dq_all = refs.pop(0) if last else dq_outs[0]

    def begin(i, carry):
        dq_all[i] = jnp.zeros((rows, hd), F32) if first else dq_before[i]
        return carry

    lax.fori_loop(own if first else 0, plan.total, begin, 0)

    def wide_row(ref, start):
        return jnp.concatenate([ref[pl.ds(start + r, 1), :] for r in range(nz)], axis=1)

    def diagonal(s, carry):
        frame = pl.ds(s * nz, nz)
        k = jnp.concatenate([k_ref[s * nz + r] for r in span], axis=0)
        v = jnp.concatenate([v_ref[s] for v_ref in v_refs], axis=0)
        q, g = q_ref[frame].reshape(length, hd), g_ref[frame].reshape(length, hd)
        lse, delta = wide_row(lse_ref, s * nz), wide_row(delta_ref, s * nz)
        probs = jnp.exp(scale * dot(k, q, NT) - lse)
        dv = dot(probs.astype(BF16), g, NN)
        grad_scores = (probs * (dot(v, g, NT) - delta)).astype(BF16)
        dk = dot(grad_scores, q, NN)
        dq = dot(grad_scores, k, TN).reshape(nz, rows, hd)
        for x in range(width):
            dv_all[s * width + x] = dv[x * rows : (x + 1) * rows]
            dk_all[s * width + x] = dk[x * rows : (x + 1) * rows]
        if first:
            dq_all[frame] = dq
        else:
            dq_all[frame] += dq
        return carry

    lax.fori_loop(0, na, diagonal, 0)

    def terms(s, x, j, start, size):
        k, v = k_ref[j], v_refs[x][s]
        chosen = picks(by_key, j, n_key[j], start, size)
        q = jnp.concatenate([q_ref[i] for i, _ in chosen], axis=0)
        g = jnp.concatenate([g_ref[i] for i, _ in chosen], axis=0)
        lse = jnp.concatenate([jnp.where(ok, lse_ref[pl.ds(i, 1), :], -NEG) for i, ok in chosen], axis=1)
        delta = jnp.concatenate([delta_ref[pl.ds(i, 1), :] for i, _ in chosen], axis=1)
        probs = jnp.exp(scale * dot(k, q, NT) - lse)
        dv = dot(probs.astype(BF16), g, NN)
        grad_scores = (probs * (dot(v, g, NT) - delta)).astype(BF16)
        dk = dot(grad_scores, q, NN)
        return chosen, dv, dk, dot(grad_scores, k, TN)

    def add(s, x, found):
        chosen, dv, dk, dq = found
        dv_all[s * width + x] += dv
        dk_all[s * width + x] += dk
        for u, (i, _) in enumerate(chosen):
            dq_all[i] += dq[u * rows : (u + 1) * rows]

    def away(s, carry):
        most = functools.reduce(jnp.maximum, [n_key[s * nz + r] for r in span])

        def together(size):
            for x, found in [(x, terms(s, x, s * nz + r, 0, size)) for x, r in enumerate(span)]:
                add(s, x, found)

        pl.when((most > 0) & (most < KEY_GROUP))(lambda: together(KEY_GROUP - 1))
        pl.when(most == KEY_GROUP)(lambda: together(KEY_GROUP))
        pl.when(most == KEY_GROUP + 1)(lambda: together(KEY_GROUP + 1))
        pl.when(most > KEY_GROUP + 1)(lambda: together(WIDE_GROUP))
        for x, r in enumerate(span):
            left = jnp.maximum(n_key[s * nz + r] - WIDE_GROUP, 0)

            def group(step, carry, x=x, r=r):
                add(s, x, terms(s, x, s * nz + r, WIDE_GROUP + step * KEY_GROUP, KEY_GROUP))
                return carry

            lax.fori_loop(0, steps(left, KEY_GROUP), group, 0)
        return carry

    lax.fori_loop(0, na, away, 0)

    for s, out in enumerate(kv_outs):
        for x in range(width):
            out[0, x] = (scale * dk_all[s * width + x]).astype(BF16)
            out[1, x] = dv_all[s * width + x].astype(BF16)
    if last:
        for t in range(nb):

            def drain(m, carry, t=t):
                dq_outs[t][m] = scale * dq_all[t * own + m]
                return carry

            lax.fori_loop(0, own, drain, 0)


def grads(plan, span, tables, queries, out_grads, lse, delta, keys, values, dq_before, last):
    nb, na, own, rows, total = plan.nb, plan.na, plan.own, plan.rows, plan.total
    hd, width, first = HEAD_DIM, len(span), dq_before is None
    kv = [sds((2, width, rows, hd), BF16)] * na
    dq = [sds((own, rows, hd), F32)] * nb if last else [sds((total, rows, hd), F32)]
    before = [] if first else [dq_before]
    partial = sds((own, rows, hd), F32)
    outs = pl.pallas_call(
        functools.partial(grads_kernel, plan, span, first, last),
        out_shape=kv + dq,
        in_specs=[SMEM] * 2 + [VMEM] * (5 + width + len(before)),
        out_specs=[VMEM] * (na + len(dq)),
        scratch_shapes=[pltpu.VMEM((na * width, rows, hd), F32)] * 2
        + ([pltpu.VMEM((total, rows, hd), F32)] if last else []),
        cost_estimate=lasts(7),
        compiler_params=within(queries, out_grads, keys, keys, *[partial] * (4 + 3 * nb)),
    )(*tables, queries, out_grads, lse, delta, keys, *values, *before)
    return outs[:na], outs[na:]


def pack_kernel(plan, *refs):
    nb, nz = plan.nb, plan.nz
    for s, out in enumerate(refs[nb:]):
        for r in range(nz):
            out[0, r] = sum(ref[s * nz + r] for ref in refs[:nb]).astype(BF16)


def pack(plan, partials):
    return pl.pallas_call(
        functools.partial(pack_kernel, plan),
        out_shape=[sds((1, plan.nz, plan.rows, HEAD_DIM), BF16)] * plan.na,
        in_specs=[VMEM] * plan.nb,
        out_specs=[VMEM] * plan.na,
        cost_estimate=lasts(1),
        compiler_params=within(*partials, *partials),
        name="pack",
    )(*partials)


def assemble_kernel(plan, spans, n, ids, *refs):
    na, rows, hd = plan.na, plan.rows, HEAD_DIM
    refs = list(refs)
    outs = refs[na * len(spans) :]
    for span in spans:
        for s in range(na):
            piece = refs.pop(0)
            cols = pl.ds(pl.multiple_of((ids[1] ^ s) * hd, hd), hd)
            for w in range(n):
                for x, r in enumerate(span):
                    place = pl.ds(pl.multiple_of((ids[0] ^ r) * rows, rows), rows)
                    outs[w][place, cols] = piece[w, x]


def assemble(plan, ids, spans, groups):
    n = groups[0][0].shape[0]
    pieces = [piece for group in groups for piece in group]
    return pl.pallas_call(
        functools.partial(assemble_kernel, plan, spans, n),
        out_shape=[sds((plan.nz * plan.rows, plan.na * HEAD_DIM), BF16)] * n,
        in_specs=[SMEM] + [VMEM] * len(pieces),
        out_specs=[VMEM] * n,
        cost_estimate=lasts(1.5),
        compiler_params=within(*pieces, *pieces),
    )(ids, *pieces)


def local(queries, key_states, value_states, attn_out, grad_out, frame_order, block_live):
    plan = Plan(queries.shape[0])
    nz, na, nb = plan.nz, plan.na, plan.nb
    slot = lax.axis_index("frame")
    ids = jnp.stack([lax.axis_index("head"), slot // nb, slot % nb]).astype(jnp.int32)

    def staged(order, pieces, send):
        moved = {}
        for step in order:
            moved[step] = send(pieces[step], step)
        return [pieces[0]] + [moved[step] for step in range(1, len(pieces))]

    def head_stage(pieces):
        return staged([*range(2, nz), 1], pieces, over_head)

    def frame_stage(pieces):
        return staged(range(na - 1, 0, -1), pieces, lambda x, s: over_frame(x, s * nb))

    def swapped(parts):
        return staged(range(1, nb), parts, over_frame)

    groups = [
        [(a * nb + b) * nz + z for a in range(na) for z in range(nz)] for b in range(nb)
    ]
    mine = lax.all_to_all(
        prep(plan, queries, key_states), ("frame", "head"), 0, 0,
        tiled=True, axis_index_groups=groups,
    )
    g_near, v_near = prep_rest(plan, ids, grad_out, attn_out, value_states)
    g_near = frame_stage(g_near)
    v_near = frame_stage(v_near)
    by_key, n_key = lists(plan, ids, frame_order, block_live.transpose(1, 2, 0))
    g_own = turn(head_stage(turn(g_near)), joined=True)
    values = head_stage(turn(v_near))
    q_own, keys = part(plan, ids, mine)
    lse_part, q_all = totals(plan, by_key, n_key, keys, swapped([q_own] * nb))
    lse, delta, g_all = query_rows(plan, swapped([g_own] * nb), swapped([lse_part] * nb))
    spans = [range(0, 2), range(2, nz)]
    kv_home, dq = [], None
    for place, span in enumerate(spans):
        last = place == len(spans) - 1
        kv, dq_parts = grads(
            plan, span, (by_key, n_key), q_all, g_all, lse, delta, keys,
            [values[r] for r in span], dq, last,
        )
        dq = dq_parts[0]
        kv_home.append(frame_stage(kv))
    dq_home = frame_stage(pack(plan, swapped(dq_parts)))
    grad_key, grad_value = assemble(plan, ids, spans, kv_home)
    (grad_query,) = assemble(plan, ids, [range(nz)], [dq_home])
    return grad_query, grad_key, grad_value


def solution(mesh):
    rows = P(("frame", "head"), None)
    in_specs = (rows,) * 5 + (P(), P())
    out_specs = (P("frame", "head"),) * 3
    return jax.shard_map(local, mesh=mesh, in_specs=in_specs, out_specs=out_specs, check_vma=False)
```
